32 devices in a mesh: dp: 8 (over z, core), tensor: 4 (over y, x).
Axes of the slice: x: 2, y: 2, z: 4, core: 2. Of those that a mesh axis runs over, the one named last changes fastest.
Arguments:
- hidden_in: bfloat16 [2, 4096, 2048], P(None, ('dp', 'tensor')), may hold values from -6 to 6
- cotangent: bfloat16 [2, 4096, 2048], P(None, ('dp', 'tensor')), may hold values from -6 to 6
- segment_ids: int32 [2, 4096], P(None, 'dp'), may hold values from 0 to 8, as said below
- positions: int32 [2, 4096], P(None, 'dp'), may hold values from 0 to 399, as said below
- pad_mask: int32 [2, 4096], P(None, 'dp'), may hold values from 0 to 1, as said below
- attn_gain: bfloat16 [2048], P('dp'), may hold values from 0.5 to 1.5
- w_query: bfloat16 [2048, 2048], P('dp', 'tensor'), may hold values from -0.125 to 0.125
- key_weight: bfloat16 [2048, 1024], P('dp', 'tensor'), may hold values from -0.125 to 0.125
- value_weight: bfloat16 [2048, 1024], P('dp', 'tensor'), may hold values from -0.125 to 0.125
- query_norm_gain: bfloat16 [128], P('dp'), may hold values from 0.5 to 1.5
- key_gain: bfloat16 [128], P('dp'), may hold values from 0.5 to 1.5
- w_out: bfloat16 [2048, 2048], P('tensor', 'dp'), may hold values from -1 to 1
- ffn_gain: bfloat16 [2048], P('dp'), may hold values from 0.5 to 1.5
- w_gate: bfloat16 [2048, 6144], P('dp', 'tensor'), may hold values from -0.125 to 0.125
- w_up: bfloat16 [2048, 6144], P('dp', 'tensor'), may hold values from -0.125 to 0.125
- w_down: bfloat16 [6144, 2048], P('tensor', 'dp'), may hold values from -0.078125 to 0.078125
Outputs:
- layer_out: bfloat16 [2, 4096, 2048], P(None, ('dp', 'tensor'))
- input_grad: bfloat16 [2, 4096, 2048], P(None, ('dp', 'tensor'))
- grad_attn_gain: float32 [2048], P('dp')
- grad_query: float32 [2048, 2048], P('dp', 'tensor')
- grad_key: float32 [2048, 1024], P('dp', 'tensor')
- grad_value: float32 [2048, 1024], P('dp', 'tensor')
- grad_query_gain: float32 [128], P('dp')
- grad_key_gain: float32 [128], P('dp')
- grad_out: float32 [2048, 2048], P('tensor', 'dp')
- grad_ffn_gain: float32 [2048], P('dp')
- grad_gate: float32 [2048, 6144], P('dp', 'tensor')
- grad_up: float32 [2048, 6144], P('dp', 'tensor')
- grad_down: float32 [6144, 2048], P('tensor', 'dp')
The draws below stay inside these ranges and needn't reach their ends.
Inputs may be any that keep to these rules, and one draw needn't show every extreme that they name: `segment_ids`: segment numbers start at 0 and never fall within a sequence; documents hold 60 to 400 tokens and are followed by one padding segment of 1 to 400 tokens. `positions`: positions count from 0 within each document and are 0 on padding. `pad_mask`: 0 exactly on the last segment of each sequence.
All inputs are finite; a program needn't handle non-finite values.
Results may differ from the reference program's by a relative error of at most 0.023.
Values may be sent and summed in bfloat16 or wider, within the bound.
A program may use at most 384 MiB of HBM per device.

```python
import math
import jax
import jax.numpy as jnp
from jax import lax

MODEL_WIDTH = 2048
QUERY_HEADS = 16
KEY_VALUE_HEADS = 8
HEAD_SIZE = 128
FF = 6144
PACKED_TOKENS = 512
MICRO = 2
DOC_LEAST = 60
DOC_MOST = 400
ROWS = 4096


def doc_layout(key):
    seq_count = ROWS // PACKED_TOKENS
    doc_slots = PACKED_TOKENS // DOC_LEAST + 1
    doc_sizes = jax.random.randint(jax.random.fold_in(key, 11), (MICRO, seq_count, doc_slots), DOC_LEAST, DOC_MOST + 1)
    first_micro = jnp.arange(MICRO)[:, None, None] == 0
    seq_index = jnp.arange(seq_count)[None, :, None]
    forced = first_micro & (seq_index == 0) & (jnp.arange(doc_slots)[None, None, :] == 0)
    smallest = first_micro & (seq_index == 1)
    doc_sizes = jnp.where(forced, DOC_MOST, doc_sizes)
    doc_sizes = jnp.where(smallest, DOC_LEAST, doc_sizes).astype(jnp.int32)
    doc_ends = jnp.cumsum(doc_sizes, axis=-1)
    tokens = jnp.arange(PACKED_TOKENS).astype(jnp.int32)
    segment = jnp.sum((doc_ends[..., None, :] <= tokens[:, None]).astype(jnp.int32), axis=-1)
    live_docs = jnp.sum((doc_ends <= PACKED_TOKENS - 1).astype(jnp.int32), axis=-1)
    inside = segment < live_docs[..., None]
    doc_starts = doc_ends - doc_sizes
    doc_start = jnp.take_along_axis(doc_starts, jnp.minimum(segment, doc_slots - 1), axis=-1)
    offsets = jnp.where(inside, tokens - doc_start, 0).astype(jnp.int32)
    return (segment.reshape(MICRO, ROWS), offsets.reshape(MICRO, ROWS), inside.astype(jnp.int32).reshape(MICRO, ROWS))


def draw_segment_ids(key, part):
    return doc_layout(key)[0]


def draw_positions(key, part):
    return doc_layout(key)[1]


def draw_pad_mask(key, part):
    return doc_layout(key)[2]


def shard_levels(stream_key, dims, cuts, low, top_value):
    loudness, own = 1.0, jax.random.fold_in(stream_key, 6)
    for position, parts in cuts:
        steps = jnp.exp(jax.random.uniform(jax.random.fold_in(own, position), (parts,), jnp.float32, low / len(cuts), top_value / len(cuts)))
        loudness = loudness * jnp.repeat(steps, dims[position] // parts).reshape([-1 if axis == position else 1 for axis in range(len(dims))])
    return loudness


def noise(key, dims, width, reach, shards=(), dtype=jnp.bfloat16):
    values = width * jax.random.normal(key, dims, jnp.float32)
    if shards:
        values = values * shard_levels(key, dims, shards, -0.22, 0.18)
    return jnp.clip(values, -reach, reach).astype(dtype)


def setup_inputs(seed: int = 0) -> dict:
    splits = jax.random.split(jax.random.key(seed), 17)
    return {
        "hidden_in": noise(splits[0], (MICRO, ROWS, MODEL_WIDTH), 1.0, 6.0, ((1, 32),)),
        "cotangent": noise(splits[1], (MICRO, ROWS, MODEL_WIDTH), 1.0, 6.0, ((1, 32),)),
        "segment_ids": draw_segment_ids(jax.random.fold_in(splits[16], 71), 0),
        "positions": draw_positions(jax.random.fold_in(splits[16], 71), 0),
        "pad_mask": draw_pad_mask(jax.random.fold_in(splits[16], 71), 0),
        "attn_gain": jnp.clip(1.0 + 0.1 * jax.random.normal(splits[5], (MODEL_WIDTH,), jnp.float32), 0.5, 1.5).astype(jnp.bfloat16),
        "w_query": noise(splits[6], (MODEL_WIDTH, QUERY_HEADS * HEAD_SIZE), MODEL_WIDTH ** -0.5, 0.125, ((0, 8), (1, 4))),
        "key_weight": noise(splits[7], (MODEL_WIDTH, KEY_VALUE_HEADS * HEAD_SIZE), MODEL_WIDTH ** -0.5, 0.125, ((0, 8), (1, 4))),
        "value_weight": noise(splits[8], (MODEL_WIDTH, KEY_VALUE_HEADS * HEAD_SIZE), MODEL_WIDTH ** -0.5, 0.125, ((0, 8), (1, 4))),
        "query_norm_gain": jnp.clip(1.0 + 0.1 * jax.random.normal(splits[9], (HEAD_SIZE,), jnp.float32), 0.5, 1.5).astype(jnp.bfloat16),
        "key_gain": jnp.clip(1.0 + 0.1 * jax.random.normal(splits[10], (HEAD_SIZE,), jnp.float32), 0.5, 1.5).astype(jnp.bfloat16),
        "w_out": noise(splits[11], (QUERY_HEADS * HEAD_SIZE, MODEL_WIDTH), (QUERY_HEADS * HEAD_SIZE // 64) ** -0.5, 1.0, ((0, 4), (1, 8))),
        "ffn_gain": jnp.clip(1.0 + 0.1 * jax.random.normal(splits[12], (MODEL_WIDTH,), jnp.float32), 0.5, 1.5).astype(jnp.bfloat16),
        "w_gate": noise(splits[13], (MODEL_WIDTH, FF), MODEL_WIDTH ** -0.5, 0.125, ((0, 8), (1, 4))),
        "w_up": noise(splits[14], (MODEL_WIDTH, FF), MODEL_WIDTH ** -0.5, 0.125, ((0, 8), (1, 4))),
        "w_down": noise(splits[15], (FF, MODEL_WIDTH), FF ** -0.5, 0.078125, ((0, 4), (1, 8))),
    }


EPS = 1e-06
THETA = 1000000.0

@jax.custom_vjp
def lowered_rows(v):
    return lax.optimization_barrier(v.astype(jnp.bfloat16)).astype(jnp.float32)

@jax.custom_vjp
def lowered_backward(v):
    return v

def low_keep(v):
    return (lowered_rows(v), None)

def low_pass(kept, grad):
    return (grad,)

def back_keep(v):
    return (v, None)

def back_low(kept, grad):
    return (lowered_rows(grad),)
lowered_rows.defvjp(low_keep, low_pass)
lowered_backward.defvjp(back_keep, back_low)

def matrix_product(left, right):
    return jnp.dot(left, right, precision=lax.Precision.HIGHEST, preferred_element_type=jnp.float32)

def root_mean_scale(value_rows, gain):
    return value_rows * lax.rsqrt(lax.optimization_barrier(jnp.mean(value_rows * value_rows, axis=-1, keepdims=True)) + EPS) * gain

def rotary(offsets):
    freqs = jnp.exp(jnp.arange(0, HEAD_SIZE, 2).astype(jnp.float32) * (-math.log(THETA) / HEAD_SIZE))
    angles = offsets.astype(jnp.float32)[:, None] * freqs[None, :]
    return (jnp.cos(angles)[:, None, :], jnp.sin(angles)[:, None, :])

def rotary_apply(value_rows, cosine_table, sine_table):
    half = value_rows.shape[-1] // 2
    lower = value_rows[..., :half]
    higher = value_rows[..., half:]
    return jnp.concatenate([lower * cosine_table - higher * sine_table, higher * cosine_table + lower * sine_table], axis=-1)

def attention(query_rows, key_rows, value_rows, segment, valid):
    block = min(512, PACKED_TOKENS)
    blocks = PACKED_TOKENS // block
    scale = 1.0 / math.sqrt(HEAD_SIZE)
    columns = jnp.arange(PACKED_TOKENS).astype(jnp.int32)

    def one_block(items):
        query_block, seg_block, row_ids = items
        scores = lowered_backward(scale * jnp.einsum('qkgd,tkd->kgqt', query_block, key_rows, precision=lax.Precision.HIGHEST))
        allowed = (seg_block[:, None] == segment[None, :]) & (columns[None, :] <= row_ids[:, None]) & ((valid[None, :] > 0) | (columns[None, :] == row_ids[:, None]))
        masked = jnp.where(allowed, scores, -1e+30)
        totals = jax.nn.logsumexp(masked, axis=-1, keepdims=True)
        probs = lowered_rows(jnp.where(allowed, jnp.exp(masked - totals), 0.0))
        return jnp.einsum('kgqt,tkd->qkgd', probs, value_rows, precision=lax.Precision.HIGHEST)
    outputs = lax.map(jax.checkpoint(one_block), (query_rows.reshape((blocks, block) + query_rows.shape[1:]), segment.reshape(blocks, block), columns.reshape(blocks, block)))
    return outputs.reshape(query_rows.shape)

def forward(inputs, params, segment, offsets, valid):
    attn_gain, w_query, key_weight, value_weight, query_norm_gain, key_gain, w_out, ffn_gain, w_gate, w_up, w_down = params
    head_groups = QUERY_HEADS // KEY_VALUE_HEADS
    cosine_table, sine_table = rotary(offsets)
    normalized_input = lowered_rows(root_mean_scale(inputs, attn_gain))
    query_rows = lowered_backward(matrix_product(normalized_input, w_query)).reshape(PACKED_TOKENS, QUERY_HEADS, HEAD_SIZE)
    key_rows = lowered_backward(matrix_product(normalized_input, key_weight)).reshape(PACKED_TOKENS, KEY_VALUE_HEADS, HEAD_SIZE)
    value_rows = lowered_rows(lowered_backward(matrix_product(normalized_input, value_weight))).reshape(PACKED_TOKENS, KEY_VALUE_HEADS, HEAD_SIZE)
    query_rows = lowered_rows(rotary_apply(root_mean_scale(query_rows, query_norm_gain), cosine_table, sine_table)).reshape(PACKED_TOKENS, KEY_VALUE_HEADS, head_groups, HEAD_SIZE)
    key_rows = lowered_rows(rotary_apply(root_mean_scale(key_rows, key_gain), cosine_table, sine_table))
    mixed = attention(query_rows, key_rows, value_rows, segment, valid).reshape(PACKED_TOKENS, QUERY_HEADS * HEAD_SIZE)
    mixed = lowered_rows(lowered_backward(mixed * valid[:, None].astype(jnp.float32)))
    resid = inputs + lowered_backward(matrix_product(mixed, w_out))
    normed_two = lowered_rows(root_mean_scale(resid, ffn_gain))
    gate = lowered_backward(matrix_product(normed_two, w_gate))
    upper = lowered_backward(matrix_product(normed_two, w_up))
    inner = lowered_rows(jax.nn.silu(gate) * upper)
    return resid + lowered_backward(matrix_product(inner, w_down))

def reference(hidden_in, cotangent, segment_ids, positions, pad_mask, attn_gain, w_query, key_weight, value_weight, query_norm_gain, key_gain, w_out, ffn_gain, w_gate, w_up, w_down):
    seq_count = MICRO * ROWS // PACKED_TOKENS
    inputs = hidden_in.astype(jnp.float32).reshape(seq_count, PACKED_TOKENS, MODEL_WIDTH)
    grads_in = cotangent.astype(jnp.float32).reshape(seq_count, PACKED_TOKENS, MODEL_WIDTH)
    segments = segment_ids.reshape(seq_count, PACKED_TOKENS)
    offsets = positions.reshape(seq_count, PACKED_TOKENS)
    valids = pad_mask.reshape(seq_count, PACKED_TOKENS)
    params = tuple((weight.astype(jnp.float32) for weight in (attn_gain, w_query, key_weight, value_weight, query_norm_gain, key_gain, w_out, ffn_gain, w_gate, w_up, w_down)))
    zeros = tuple((jnp.zeros(weight.shape, jnp.float32) for weight in params))

    def step(totals, items):
        row_block, grad_block, segment, offset_block, valid = items

        def apply(row_values, *weights):
            return forward(row_values, weights, segment, offset_block, valid)
        result, pull = jax.vjp(apply, row_block, *params)
        pulled = pull(grad_block)
        summed = tuple((total + part for total, part in zip(totals, pulled[1:])))
        return (summed, (result.astype(jnp.bfloat16), pulled[0].astype(jnp.bfloat16)))
    totals, (outputs, input_grads) = lax.scan(step, zeros, (inputs, grads_in, segments, offsets, valids))
    return (outputs.reshape(MICRO, ROWS, MODEL_WIDTH), input_grads.reshape(MICRO, ROWS, MODEL_WIDTH), totals[0], totals[1], totals[2], totals[3], totals[4], totals[5], totals[6], totals[7], totals[8], totals[9], totals[10])
```

```python
import math

import jax
import jax.numpy as jnp
from jax import lax
from jax.experimental import pallas as pl
from jax.experimental.pallas import tpu as pltpu
from jax.sharding import PartitionSpec as P

HEAD_SIZE = 128
EPS = 1e-06
THETA = 1000000.0
CHUNKS = 3
F32 = jnp.float32
BF16 = jnp.bfloat16

ORDER = (0, 2, 4, 6, 1, 3, 5, 7)
PAIR = [(d, d ^ 2) for d in range(8)]
CORE = [(d, d ^ 1) for d in range(8)]
INNER = [(2, 4), (3, 5), (4, 2), (5, 3)]
OUTWARD = [(2, 0), (3, 1), (4, 6), (5, 7)]
INWARD = [(0, 2), (1, 3), (6, 4), (7, 5)]
XNEXT = [(t, t ^ 1) for t in range(4)]
YNEXT = [(t, t ^ 2) for t in range(4)]


def add_rounded(left, right):
    return (left.astype(F32) + right.astype(F32)).astype(BF16)


def dot_nn(left, right):
    return jnp.dot(left, right, preferred_element_type=F32)


def dot_nt(left, right):
    return lax.dot_general(left, right, (((1,), (1,)), ((), ())), preferred_element_type=F32)


def dot_tn(left, right):
    return lax.dot_general(left, right, (((0,), (0,)), ((), ())), preferred_element_type=F32)


def block_move(table, rows):
    micro, count, width = rows.shape
    blocks = table.shape[0]
    size = width // blocks

    def body(table_ref, in_ref, out_ref):
        out_ref[...] = in_ref[...]

    return pl.pallas_call(
        body,
        out_shape=jax.ShapeDtypeStruct(rows.shape, rows.dtype),
        grid_spec=pltpu.PrefetchScalarGridSpec(
            num_scalar_prefetch=1,
            grid=(blocks,),
            in_specs=[pl.BlockSpec((micro, count, size), lambda i, ref: (0, 0, ref[i]))],
            out_specs=pl.BlockSpec((micro, count, size), lambda i, ref: (0, 0, i)),
        ),
        cost_estimate=pl.CostEstimate(
            flops=0, bytes_accessed=4 * micro * count * width, transcendentals=0
        ),
    )(table, rows)


class Direct:
    def __init__(self, dp, tensor):
        self.dp, self.tensor = dp, tensor
        self.me = lax.axis_index("dp")
        self.own = lax.axis_index("tensor")

    def to_local(self, rows):
        return rows

    def from_local(self, rows):
        return rows

    def row_order(self, value):
        return value

    def gather_gains(self, packed):
        return lax.all_gather(packed, "dp", axis=0)

    def gains_local(self, blocks):
        return blocks.reshape(-1)

    def gains_plain(self, blocks):
        return blocks.reshape(-1)

    def plain_vector(self, vector):
        return vector

    def gather_weights(self, buf):
        return lax.all_gather(buf, "dp", axis=0, tiled=True)

    def scatter_grads(self, parts):
        full = jnp.concatenate([dot_tn(l, r).astype(BF16) for l, r in parts], axis=1)
        return lax.psum_scatter(full, "dp", scatter_dimension=0, tiled=True).astype(F32)

    def gather_rows(self, rows):
        return lax.all_gather(rows, "tensor", axis=1, tiled=True)

    def scatter_rows(self, partial):
        return lax.psum_scatter(partial, "tensor", scatter_dimension=1, tiled=True).astype(F32)


class Links(Direct):
    def __init__(self, dp, tensor):
        super().__init__(dp, tensor)
        z = self.me // 2
        self.inner = (z == 1) | (z == 2)
        self.blocks = self.me ^ jnp.array(ORDER, jnp.int32)
        place = jnp.array([ORDER.index(b) for b in range(8)], jnp.int32)
        hit = (self.me ^ jnp.arange(8, dtype=jnp.int32))[:, None] == jnp.array(ORDER, jnp.int32)
        self.hit = hit
        self.places = jnp.sum(jnp.where(hit, jnp.arange(8, dtype=jnp.int32)[None, :], 0), axis=1)

    def to_local(self, rows):
        return block_move(self.blocks, rows)

    def from_local(self, rows):
        return block_move(self.places, rows)

    def row_order(self, value):
        parts = list(jnp.split(value, 4, axis=-1))
        for bit in (1, 2):
            swap = (self.own & bit) != 0
            parts = [jnp.where(swap, parts[j ^ bit], parts[j]) for j in range(4)]
        return jnp.concatenate(parts, axis=-1)

    def gather_gains(self, packed):
        got = [packed]
        for b in ORDER[1:]:
            got.append(lax.ppermute(packed, "dp", [(d, d ^ b) for d in range(8)]))
        return jnp.stack(got)

    def gains_plain(self, blocks):
        return jnp.sum(jnp.where(self.hit[:, :, None], blocks[None], 0), axis=1).reshape(-1)

    def plain_vector(self, vector):
        return self.gains_plain(vector.reshape(8, -1))

    def gather_weights(self, buf):
        pair = lax.ppermute(buf, "dp", PAIR)
        over_own = lax.ppermute(buf, "dp", INNER)
        over_pair = lax.ppermute(pair, "dp", INNER)
        out_own = lax.ppermute(over_own, "dp", OUTWARD)
        out_pair = lax.ppermute(over_pair, "dp", OUTWARD)
        far_two = jnp.where(self.inner, over_pair, out_own)
        far_three = jnp.where(self.inner, over_own, out_pair)
        mine = jnp.concatenate([buf, pair, far_two, far_three], axis=0)
        other = lax.ppermute(mine, "dp", CORE)
        return jnp.concatenate([mine, other], axis=0)

    def scatter_grads(self, parts):
        summed = []
        for left, right in parts:
            half = left.shape[1] // 2
            away = dot_tn(left[:, half:], right).astype(BF16)
            here = dot_tn(left[:, :half], right)
            summed.append((here + lax.ppermute(away, "dp", CORE).astype(F32)).astype(BF16))
        own, pair, two, three = jnp.split(jnp.concatenate(summed, axis=1), 4, axis=0)
        two = add_rounded(two, lax.ppermute(three, "dp", INWARD)), two
        three = add_rounded(three, lax.ppermute(two[1], "dp", INWARD))
        pair = add_rounded(pair, lax.ppermute(two[0], "dp", INNER))
        own = own.astype(F32) + lax.ppermute(three, "dp", INNER).astype(F32)
        return own + lax.ppermute(pair, "dp", PAIR).astype(F32)

    def gather_rows(self, rows):
        first, second = rows[0], rows[1]
        x_first = lax.ppermute(first, "tensor", XNEXT)
        y_second = lax.ppermute(second, "tensor", YNEXT)
        x_second = lax.ppermute(second, "tensor", XNEXT)
        y_first = lax.ppermute(first, "tensor", YNEXT)
        d_first = lax.ppermute(x_first, "tensor", YNEXT)
        d_second = lax.ppermute(y_second, "tensor", XNEXT)
        return jnp.stack(
            [
                jnp.concatenate([first, x_first, y_first, d_first], axis=0),
                jnp.concatenate([second, x_second, y_second, d_second], axis=0),
            ]
        )

    def scatter_rows(self, partial):
        out = []
        for part, near, far, a, b in (
            (partial[0], XNEXT, YNEXT, 1, 2),
            (partial[1], YNEXT, XNEXT, 2, 1),
        ):
            block = jnp.split(part, 4, axis=0)
            got_diag = lax.ppermute(block[3], "tensor", near)
            got_own = lax.ppermute(block[a], "tensor", near)
            passed = lax.ppermute(add_rounded(block[b], got_diag), "tensor", far)
            out.append(block[0].astype(F32) + got_own.astype(F32) + passed.astype(F32))
        return jnp.stack(out)


def unit_of(rows):
    recip = lax.rsqrt(jnp.mean(rows * rows, axis=-1, keepdims=True) + EPS)
    return rows * recip, recip


def norm_back(upstream, unit, recip, gain):
    scaled = upstream * gain
    return recip * (scaled - unit * jnp.mean(scaled * unit, axis=-1, keepdims=True))


def rotary(offsets):
    freqs = jnp.exp(
        jnp.arange(0, HEAD_SIZE, 2).astype(F32) * (-math.log(THETA) / HEAD_SIZE)
    )
    angles = offsets.astype(F32)[..., None] * freqs
    return jnp.cos(angles)[..., None, :], jnp.sin(angles)[..., None, :]


def rotate(rows, cosine, sine):
    half = rows.shape[-1] // 2
    low, high = rows[..., :half], rows[..., half:]
    return jnp.concatenate([low * cosine - high * sine, high * cosine + low * sine], axis=-1)


def on_device(
    net,
    hidden_in,
    cotangent,
    segment_ids,
    positions,
    pad_mask,
    attn_gain,
    w_query,
    key_weight,
    value_weight,
    query_norm_gain,
    key_gain,
    w_out,
    ffn_gain,
    w_gate,
    w_up,
    w_down,
):
    net = net()
    scale = 1.0 / math.sqrt(HEAD_SIZE)
    micro, own_rows, width = hidden_in.shape
    seq_len = segment_ids.shape[1]
    rows = micro * seq_len
    share = attn_gain.shape[0]
    head_share = query_norm_gain.shape[0]
    q_cols, kv_cols = w_query.shape[1], key_weight.shape[1]
    heads_q, heads_kv = q_cols // HEAD_SIZE, kv_cols // HEAD_SIZE
    groups = heads_q // heads_kv
    qkv_cols = q_cols + 2 * kv_cols
    units = w_gate.shape[1] // CHUNKS

    attn_buf = jnp.concatenate([w_query, key_weight, value_weight, w_out.T], axis=1)
    w_attn = net.gather_weights(attn_buf)
    w_qkv, w_out_t = w_attn[:, :qkv_cols], w_attn[:, qkv_cols:]
    x_own = net.to_local(hidden_in)
    x_all = net.gather_rows(x_own).reshape(rows, width).astype(F32)
    packed = jnp.concatenate(
        [attn_gain, ffn_gain, query_norm_gain, key_gain], axis=0
    )
    gains = net.gather_gains(packed).astype(F32)
    gain_one = net.gains_local(gains[:, :share])
    gain_two = net.gains_local(gains[:, share : 2 * share])
    gain_q = net.gains_plain(gains[:, 2 * share : 2 * share + head_share])
    gain_k = net.gains_plain(gains[:, 2 * share + head_share :])
    ffn_sets = []
    for chunk in range(CHUNKS):
        cut = slice(chunk * units, (chunk + 1) * units)
        ffn_sets.append(
            net.gather_weights(
                jnp.concatenate([w_gate[:, cut], w_up[:, cut], w_down[cut, :].T], axis=1)
            )
        )
    g_own = net.to_local(cotangent)
    g_all = net.gather_rows(g_own).reshape(rows, width)

    segment = net.row_order(segment_ids)
    offsets = net.row_order(positions)
    valid = net.row_order(pad_mask)
    row_ids = net.row_order(jnp.arange(seq_len, dtype=jnp.int32))
    cosine, sine = rotary(offsets)
    valid_col = valid.reshape(rows, 1).astype(F32)
    unit_all, _ = unit_of(x_all)
    a1 = (unit_all * gain_one).astype(BF16)
    qkv = dot_nn(a1, w_qkv)
    q_raw = qkv[:, :q_cols].reshape(micro, seq_len, heads_q, HEAD_SIZE)
    k_raw = qkv[:, q_cols : q_cols + kv_cols].reshape(micro, seq_len, heads_kv, HEAD_SIZE)
    value = (
        qkv[:, q_cols + kv_cols :].astype(BF16).reshape(micro, seq_len, heads_kv, HEAD_SIZE)
    )
    q_unit, q_recip = unit_of(q_raw)
    k_unit, k_recip = unit_of(k_raw)
    query = (
        rotate(q_unit * gain_q, cosine, sine)
        .astype(BF16)
        .reshape(micro, seq_len, heads_kv, groups, HEAD_SIZE)
    )
    key = rotate(k_unit * gain_k, cosine, sine).astype(BF16)
    allowed = (
        (segment[:, :, None] == segment[:, None, :])
        & (row_ids[None, None, :] <= row_ids[None, :, None])
        & ((valid[:, None, :] > 0) | (row_ids[None, None, :] == row_ids[None, :, None]))
    )[:, None, None]
    scores = scale * jnp.einsum("mqkgd,mtkd->mkgqt", query, key, preferred_element_type=F32)
    masked = jnp.where(allowed, scores, -1e30)
    lse = jax.nn.logsumexp(masked, axis=-1, keepdims=True)
    probs = jnp.where(allowed, jnp.exp(masked - lse), 0.0)
    probs_bf = probs.astype(BF16)
    mixed = jnp.einsum("mkgqt,mtkd->mqkgd", probs_bf, value, preferred_element_type=F32)
    mixed_bf = (mixed.reshape(rows, q_cols) * valid_col).astype(BF16)
    attn_part = dot_nt(mixed_bf, w_out_t).astype(BF16).reshape(micro, seq_len, width)
    resid = x_own.astype(F32) + net.scatter_rows(attn_part)
    unit_two, recip_two = unit_of(resid)
    a2_own = (unit_two * gain_two).astype(BF16)
    a2 = net.gather_rows(a2_own).reshape(rows, width)

    mlp = da2 = None
    grads_ffn = []
    for chunk in range(CHUNKS):
        w_chunk = ffn_sets[chunk]
        w_gu, w_down_t = w_chunk[:, : 2 * units], w_chunk[:, 2 * units :]
        gate_up = dot_nn(a2, w_gu)
        gate, upper = gate_up[:, :units], gate_up[:, units:]
        d_inner = dot_nn(g_all, w_down_t)
        sigma = jax.nn.sigmoid(gate)
        swish = gate * sigma
        inner = (swish * upper).astype(BF16)
        d_gate = (d_inner * upper * sigma * (1.0 + gate * (1.0 - sigma))).astype(BF16)
        d_upper = (d_inner * swish).astype(BF16)
        d_gu = jnp.concatenate([d_gate, d_upper], axis=1)
        part_mlp = dot_nt(inner, w_down_t)
        part_da2 = dot_nt(d_gu, w_gu)
        mlp = part_mlp if mlp is None else mlp + part_mlp
        da2 = part_da2 if da2 is None else da2 + part_da2
        grads_ffn.append(net.scatter_grads([(a2, d_gu), (g_all, inner)]))
    d_normed_two = net.scatter_rows(da2.astype(BF16).reshape(micro, seq_len, width))
    d_resid = g_own.astype(F32) + norm_back(d_normed_two, unit_two, recip_two, gain_two)
    acc_ffn_gain = jnp.sum(d_normed_two * unit_two, axis=(0, 1))
    d_resid_all = net.gather_rows(d_resid.astype(BF16)).reshape(rows, width)
    mlp_own = net.scatter_rows(mlp.astype(BF16).reshape(micro, seq_len, width))
    layer_out = net.from_local((resid + mlp_own).astype(BF16))

    d_mixed = dot_nn(d_resid_all, w_out_t).astype(BF16) * valid_col.astype(BF16)
    d_mixed = d_mixed.reshape(micro, seq_len, heads_kv, groups, HEAD_SIZE)
    d_probs = jnp.einsum("mqkgd,mtkd->mkgqt", d_mixed, value, preferred_element_type=F32)
    delta = jnp.sum(probs * d_probs, axis=-1, keepdims=True)
    d_scores = (probs * (d_probs - delta)).astype(BF16)
    d_query = scale * jnp.einsum("mkgqt,mtkd->mqkgd", d_scores, key, preferred_element_type=F32)
    d_key = scale * jnp.einsum("mkgqt,mqkgd->mtkd", d_scores, query, preferred_element_type=F32)
    d_value = jnp.einsum("mkgqt,mqkgd->mtkd", probs_bf, d_mixed, preferred_element_type=F32)
    d_query = rotate(
        d_query.reshape(micro, seq_len, heads_q, HEAD_SIZE), cosine, -sine
    )
    d_key = rotate(d_key, cosine, -sine)
    acc_q_gain = jnp.sum(d_query * q_unit, axis=(0, 1, 2))
    acc_k_gain = jnp.sum(d_key * k_unit, axis=(0, 1, 2))
    d_qkv = jnp.concatenate(
        [
            norm_back(d_query, q_unit, q_recip, gain_q).astype(BF16).reshape(rows, q_cols),
            norm_back(d_key, k_unit, k_recip, gain_k).astype(BF16).reshape(rows, kv_cols),
            d_value.astype(BF16).reshape(rows, kv_cols),
        ],
        axis=1,
    )
    da1 = dot_nt(d_qkv, w_qkv)
    acc_attn_gain = jnp.sum(da1 * unit_all, axis=0)
    d_normed = net.scatter_rows(da1.astype(BF16).reshape(micro, seq_len, width))
    grads_attn = net.scatter_grads([(a1, d_qkv), (d_resid_all, mixed_bf)])
    unit_one, recip_one = unit_of(x_own.astype(F32))
    input_grad = net.from_local(
        (d_resid + norm_back(d_normed, unit_one, recip_one, gain_one)).astype(BF16)
    )

    sums = lax.psum(
        jnp.concatenate(
            [
                net.plain_vector(acc_attn_gain),
                net.plain_vector(acc_ffn_gain),
                acc_q_gain,
                acc_k_gain,
            ]
        ),
        ("dp", "tensor"),
    )

    def own_part(start, size):
        return lax.dynamic_slice_in_dim(sums, start + net.me * size, size, 0)

    return (
        layer_out,
        input_grad,
        own_part(0, share),
        grads_attn[:, :q_cols],
        grads_attn[:, q_cols : q_cols + kv_cols],
        grads_attn[:, q_cols + kv_cols : qkv_cols],
        own_part(2 * width, head_share),
        own_part(2 * width + HEAD_SIZE, head_share),
        grads_attn[:, qkv_cols:].T,
        own_part(width, share),
        jnp.concatenate([g[:, :units] for g in grads_ffn], axis=1),
        jnp.concatenate([g[:, units : 2 * units] for g in grads_ffn], axis=1),
        jnp.concatenate([g[:, 2 * units :] for g in grads_ffn], axis=1).T,
    )


def solution(mesh):
    dp, tensor = mesh.shape["dp"], mesh.shape["tensor"]
    kind = Links if (dp, tensor) == (8, 4) else Direct
    weight, weight_t = P("dp", "tensor"), P("tensor", "dp")
    acts, ids = P(None, ("dp", "tensor"), None), P(None, "dp")
    gain = P("dp")

    def step(*args):
        return on_device(lambda: kind(dp, tensor), *args)

    return jax.shard_map(
        step,
        mesh=mesh,
        in_specs=(
            acts,
            acts,
            ids,
            ids,
            ids,
            gain,
            weight,
            weight,
            weight,
            gain,
            gain,
            weight_t,
            gain,
            weight,
            weight,
            weight_t,
        ),
        out_specs=(
            acts,
            acts,
            gain,
            weight,
            weight,
            weight,
            gain,
            gain,
            weight_t,
            gain,
            weight,
            weight,
            weight_t,
        ),
        check_vma=False,
    )
```

```python
import math

import jax
import jax.numpy as jnp
from jax import lax
from jax.experimental import pallas as pl
from jax.experimental.pallas import tpu as pltpu
from jax.sharding import PartitionSpec as P

HEAD_SIZE = 128
EPS = 1e-06
THETA = 1000000.0
CHUNKS = 3
F32 = jnp.float32
BF16 = jnp.bfloat16

ORDER = (0, 2, 4, 6, 1, 3, 5, 7)
PAIR = [(d, d ^ 2) for d in range(8)]
ACROSS = [(d, d ^ 4) for d in range(8)]
CORE = [(d, d ^ 1) for d in range(8)]
INNER = [(2, 4), (3, 5), (4, 2), (5, 3)]
OUTWARD = [(2, 0), (3, 1), (4, 6), (5, 7)]
INWARD = [(0, 2), (1, 3), (6, 4), (7, 5)]
XNEXT = [(t, t ^ 1) for t in range(4)]
YNEXT = [(t, t ^ 2) for t in range(4)]


def add_rounded(left, right):
    return (left.astype(F32) + right.astype(F32)).astype(BF16)


def dot_nn(left, right):
    return jnp.dot(left, right, preferred_element_type=F32)


def dot_nt(left, right):
    return lax.dot_general(left, right, (((1,), (1,)), ((), ())), preferred_element_type=F32)


def dot_tn(left, right):
    return lax.dot_general(left, right, (((0,), (0,)), ((), ())), preferred_element_type=F32)


def block_move(table, rows):
    micro, count, width = rows.shape
    blocks = table.shape[0]
    size = width // blocks

    def body(table_ref, in_ref, out_ref):
        out_ref[...] = in_ref[...]

    return pl.pallas_call(
        body,
        out_shape=jax.ShapeDtypeStruct(rows.shape, rows.dtype),
        grid_spec=pltpu.PrefetchScalarGridSpec(
            num_scalar_prefetch=1,
            grid=(blocks,),
            in_specs=[pl.BlockSpec((micro, count, size), lambda i, ref: (0, 0, ref[i]))],
            out_specs=pl.BlockSpec((micro, count, size), lambda i, ref: (0, 0, i)),
        ),
        cost_estimate=pl.CostEstimate(
            flops=0, bytes_accessed=4 * micro * count * width, transcendentals=0
        ),
    )(table, rows)


class Job:
    def __init__(self, gen, open_at):
        self.gen, self.open_at = gen, open_at
        self.rounds, self.flight, self.value, self.done = 0, (), None, False

    def step(self, results, anchor=()):
        try:
            sends = self.gen.send(results)
        except StopIteration as stop:
            self.value, self.done, self.flight = stop.value, True, ()
            return
        arrays = [array for array, _ in sends]
        if anchor:
            arrays = lax.optimization_barrier((*arrays, *anchor))[: len(arrays)]
        self.flight = tuple(
            lax.ppermute(array, "dp", perm) for array, (_, perm) in zip(arrays, sends)
        )
        self.rounds += 1

    @property
    def open(self):
        return self.done or self.rounds >= self.open_at


class Rounds:
    def __init__(self):
        self.live, self.queue = [], []

    def add(self, gen, open_at):
        job = Job(gen, open_at)
        self.queue.append(job)
        return job

    def pump(self, *values):
        flight = [array for job in self.live for array in job.flight]
        if flight:
            out = lax.optimization_barrier((*values, *flight))
            values, flight = out[: len(values)], list(out[len(values) :])
            for job in self.live:
                count = len(job.flight)
                results, flight = flight[:count], flight[count:]
                job.step(results)
            self.live = [job for job in self.live if not job.done]
        while self.queue and all(job.open for job in self.live):
            job = self.queue.pop(0)
            job.step(None, values[:1])
            if not job.done:
                self.live.append(job)
        return values

    def drain(self):
        while self.live or self.queue:
            self.pump()


class Steps:
    def __init__(self, gen):
        self.gen, self.pending, self.value = gen, (), None
        self.feed(None)

    def feed(self, results):
        try:
            self.pending = self.gen.send(results)
        except StopIteration as stop:
            self.value, self.pending = stop.value, ()


class Direct:
    def __init__(self, dp, tensor):
        self.dp, self.tensor = dp, tensor
        self.me = lax.axis_index("dp")
        self.own = lax.axis_index("tensor")
        self.rounds = Rounds()

    def mix(self, steps, *values):
        out = self.rounds.pump(*values, *steps.pending)
        if steps.pending:
            steps.feed(out[len(values) :])
        return out[: len(values)]

    def run(self, gen):
        steps = Steps(gen)
        while steps.pending:
            self.mix(steps)
        return steps.value

    def free(self, gen):
        steps = gen if isinstance(gen, Steps) else Steps(gen)
        while steps.pending:
            steps.feed(steps.pending)
        return steps.value

    def to_local(self, rows):
        return rows

    def from_local(self, rows):
        return rows

    def row_order(self, value):
        return value

    def gather_gains(self, packed):
        return lax.all_gather(packed, "dp", axis=0)

    def gains_local(self, blocks):
        return blocks.reshape(-1)

    def gains_plain(self, blocks):
        return blocks.reshape(-1)

    def plain_vector(self, vector):
        return vector

    def sum_all(self, vector):
        return lax.psum(vector, ("dp", "tensor"))

    def gather_weights(self, buf):
        return lax.all_gather(buf, "dp", axis=0, tiled=True)
        yield

    def scatter_grads(self, parts):
        full = jnp.concatenate([dot_tn(l, r).astype(BF16) for l, r in parts], axis=1)
        return lax.psum_scatter(full, "dp", scatter_dimension=0, tiled=True).astype(F32)
        yield

    def gather_rows(self, rows):
        return lax.all_gather(rows, "tensor", axis=1, tiled=True)
        yield

    def scatter_rows(self, partial):
        return lax.psum_scatter(partial, "tensor", scatter_dimension=1, tiled=True).astype(F32)
        yield


class Links(Direct):
    def __init__(self, dp, tensor):
        super().__init__(dp, tensor)
        z = self.me // 2
        self.inner = (z == 1) | (z == 2)
        self.blocks = self.me ^ jnp.array(ORDER, jnp.int32)
        hit = (self.me ^ jnp.arange(8, dtype=jnp.int32))[:, None] == jnp.array(ORDER, jnp.int32)
        self.hit = hit
        self.places = jnp.sum(jnp.where(hit, jnp.arange(8, dtype=jnp.int32)[None, :], 0), axis=1)

    def to_local(self, rows):
        return block_move(self.blocks, rows)

    def from_local(self, rows):
        return block_move(self.places, rows)

    def row_order(self, value):
        parts = list(jnp.split(value, 4, axis=-1))
        for bit in (1, 2):
            swap = (self.own & bit) != 0
            parts = [jnp.where(swap, parts[j ^ bit], parts[j]) for j in range(4)]
        return jnp.concatenate(parts, axis=-1)

    def gather_gains(self, packed):
        got = packed[None]
        for perm in (PAIR, ACROSS, CORE):
            got = jnp.concatenate([got, lax.ppermute(got, "dp", perm)], axis=0)
        return got

    def gains_plain(self, blocks):
        return jnp.sum(jnp.where(self.hit[:, :, None], blocks[None], 0), axis=1).reshape(-1)

    def plain_vector(self, vector):
        return self.gains_plain(vector.reshape(8, -1))

    def sum_all(self, vector):
        for axis, perm in (
            ("tensor", XNEXT),
            ("tensor", YNEXT),
            ("dp", CORE),
            ("dp", PAIR),
            ("dp", ACROSS),
        ):
            vector = vector + lax.ppermute(vector, axis, perm)
        return vector

    def gather_weights(self, buf):
        pair, over_own, other = yield [(buf, PAIR), (buf, INNER), (buf, CORE)]
        over_pair, out_own, other_pair = yield [(pair, INNER), (over_own, OUTWARD), (pair, CORE)]
        two = jnp.where(self.inner, over_pair, out_own)
        out_pair, other_two = yield [(over_pair, OUTWARD), (two, CORE)]
        three = jnp.where(self.inner, over_own, out_pair)
        other_three = lax.ppermute(three, "dp", CORE)
        return jnp.concatenate(
            [buf, pair, two, three, other, other_pair, other_two, other_three], axis=0
        )

    def scatter_grads(self, parts):
        away, half = [], parts[0][0].shape[1] // 2
        for left, right in parts:
            away.append(dot_tn(left[:, half:], right).astype(BF16))
        summed = [
            (dot_tn(left[:, :half], right) + lax.ppermute(array, "dp", CORE).astype(F32)).astype(BF16)
            for (left, right), array in zip(parts, away)
        ]
        own, pair, two, three = jnp.split(jnp.concatenate(summed, axis=1), 4, axis=0)
        (got,) = yield [(three, INWARD)]
        two_sum = add_rounded(two, got)
        got, got_inner = yield [(two, INWARD), (two_sum, INNER)]
        three, pair = add_rounded(three, got), add_rounded(pair, got_inner)
        got_inner, got_pair = yield [(three, INNER), (pair, PAIR)]
        return own.astype(F32) + got_inner.astype(F32) + got_pair.astype(F32)

    def gather_rows(self, rows):
        first, second = rows[0], rows[1]
        x_first = lax.ppermute(first, "tensor", XNEXT)
        y_second = lax.ppermute(second, "tensor", YNEXT)
        x_second = lax.ppermute(second, "tensor", XNEXT)
        y_first = lax.ppermute(first, "tensor", YNEXT)
        x_first, y_second = yield (x_first, y_second)
        d_first = lax.ppermute(x_first, "tensor", YNEXT)
        d_second = lax.ppermute(y_second, "tensor", XNEXT)
        x_second, y_first, d_first, d_second = yield (x_second, y_first, d_first, d_second)
        return jnp.stack(
            [
                jnp.concatenate([first, x_first, y_first, d_first], axis=0),
                jnp.concatenate([second, x_second, y_second, d_second], axis=0),
            ]
        )

    def scatter_rows(self, partial):
        first, second = (jnp.split(partial[i], 4, axis=0) for i in range(2))
        diag_first = lax.ppermute(first[3], "tensor", XNEXT)
        diag_second = lax.ppermute(second[3], "tensor", YNEXT)
        near_first = lax.ppermute(first[1], "tensor", XNEXT)
        near_second = lax.ppermute(second[2], "tensor", YNEXT)
        diag_first, diag_second = yield (diag_first, diag_second)
        far_first = lax.ppermute(add_rounded(first[2], diag_first), "tensor", YNEXT)
        far_second = lax.ppermute(add_rounded(second[1], diag_second), "tensor", XNEXT)
        near_first, near_second, far_first, far_second = yield (
            near_first,
            near_second,
            far_first,
            far_second,
        )
        return jnp.stack(
            [
                first[0].astype(F32) + near_first.astype(F32) + far_first.astype(F32),
                second[0].astype(F32) + near_second.astype(F32) + far_second.astype(F32),
            ]
        )


def unit_of(rows):
    recip = lax.rsqrt(jnp.mean(rows * rows, axis=-1, keepdims=True) + EPS)
    return rows * recip, recip


def norm_back(upstream, unit, recip, gain):
    scaled = upstream * gain
    return recip * (scaled - unit * jnp.mean(scaled * unit, axis=-1, keepdims=True))


def rotary(offsets):
    freqs = jnp.exp(
        jnp.arange(0, HEAD_SIZE, 2).astype(F32) * (-math.log(THETA) / HEAD_SIZE)
    )
    angles = offsets.astype(F32)[..., None] * freqs
    return jnp.cos(angles)[..., None, :], jnp.sin(angles)[..., None, :]


def rotate(rows, cosine, sine):
    half = rows.shape[-1] // 2
    low, high = rows[..., :half], rows[..., half:]
    return jnp.concatenate([low * cosine - high * sine, high * cosine + low * sine], axis=-1)


def on_device(
    net,
    hidden_in,
    cotangent,
    segment_ids,
    positions,
    pad_mask,
    attn_gain,
    w_query,
    key_weight,
    value_weight,
    query_norm_gain,
    key_gain,
    w_out,
    ffn_gain,
    w_gate,
    w_up,
    w_down,
):
    net = net()
    scale = 1.0 / math.sqrt(HEAD_SIZE)
    micro, own_rows, width = hidden_in.shape
    seq_len = segment_ids.shape[1]
    rows = micro * seq_len
    share = attn_gain.shape[0]
    head_share = query_norm_gain.shape[0]
    q_cols, kv_cols = w_query.shape[1], key_weight.shape[1]
    heads_q, heads_kv = q_cols // HEAD_SIZE, kv_cols // HEAD_SIZE
    groups = heads_q // heads_kv
    units = w_gate.shape[1] // CHUNKS

    rounds = net.rounds
    job_qkv = rounds.add(
        net.gather_weights(jnp.concatenate([w_query, key_weight, value_weight], axis=1)), 2
    )
    job_out = rounds.add(net.gather_weights(w_out.T), 3)
    ffn_jobs = []
    for chunk in range(CHUNKS):
        cut = slice(chunk * units, (chunk + 1) * units)
        buf = jnp.concatenate([w_gate[:, cut], w_up[:, cut], w_down[cut, :].T], axis=1)
        ffn_jobs.append(rounds.add(net.gather_weights(buf), 4))
    for _ in range(3):
        rounds.pump()
    x_own = net.to_local(hidden_in)
    x_bf = net.free(net.gather_rows(x_own)).reshape(rows, width)
    g_own, x_bf = lax.optimization_barrier((net.to_local(cotangent), x_bf))
    g_steps = Steps(net.gather_rows(g_own))
    packed = jnp.concatenate(
        [attn_gain, ffn_gain, query_norm_gain, key_gain], axis=0
    )
    gains = net.gather_gains(packed).astype(F32)
    gain_one = net.gains_local(gains[:, :share])
    gain_two = net.gains_local(gains[:, share : 2 * share])
    gain_q = net.gains_plain(gains[:, 2 * share : 2 * share + head_share])
    gain_k = net.gains_plain(gains[:, 2 * share + head_share :])

    segment = net.row_order(segment_ids)
    offsets = net.row_order(positions)
    valid = net.row_order(pad_mask)
    row_ids = net.row_order(jnp.arange(seq_len, dtype=jnp.int32))
    cosine, sine = rotary(offsets)
    valid_col = valid.reshape(rows, 1).astype(F32)
    unit_all, _ = unit_of(x_bf.astype(F32))
    (a1,) = net.mix(g_steps, (unit_all * gain_one).astype(BF16))
    w_qkv = job_qkv.value
    (qkv,) = rounds.pump(dot_nn(a1, w_qkv))
    q_raw = qkv[:, :q_cols].reshape(micro, seq_len, heads_q, HEAD_SIZE)
    k_raw = qkv[:, q_cols : q_cols + kv_cols].reshape(micro, seq_len, heads_kv, HEAD_SIZE)
    value = (
        qkv[:, q_cols + kv_cols :].astype(BF16).reshape(micro, seq_len, heads_kv, HEAD_SIZE)
    )
    q_unit, q_recip = unit_of(q_raw)
    k_unit, k_recip = unit_of(k_raw)
    query = (
        rotate(q_unit * gain_q, cosine, sine)
        .astype(BF16)
        .reshape(micro, seq_len, heads_kv, groups, HEAD_SIZE)
    )
    key = rotate(k_unit * gain_k, cosine, sine).astype(BF16)
    query, key = rounds.pump(query, key)
    allowed = (
        (segment[:, :, None] == segment[:, None, :])
        & (row_ids[None, None, :] <= row_ids[None, :, None])
        & ((valid[:, None, :] > 0) | (row_ids[None, None, :] == row_ids[None, :, None]))
    )[:, None, None]
    scores = scale * jnp.einsum("mqkgd,mtkd->mkgqt", query, key, preferred_element_type=F32)
    masked = jnp.where(allowed, scores, -1e30)
    lse = jax.nn.logsumexp(masked, axis=-1, keepdims=True)
    probs = jnp.where(allowed, jnp.exp(masked - lse), 0.0)
    probs_bf = probs.astype(BF16)
    mixed = jnp.einsum("mkgqt,mtkd->mqkgd", probs_bf, value, preferred_element_type=F32)
    (mixed_bf,) = rounds.pump((mixed.reshape(rows, q_cols) * valid_col).astype(BF16))
    w_out_t = job_out.value
    attn_part = dot_nt(mixed_bf, w_out_t).astype(BF16).reshape(micro, seq_len, width)
    resid = x_own.astype(F32) + net.run(net.scatter_rows(attn_part))
    unit_two, recip_two = unit_of(resid)
    a2_own = (unit_two * gain_two).astype(BF16)
    a2 = net.run(net.gather_rows(a2_own)).reshape(rows, width)
    g_all = net.free(g_steps).reshape(rows, width)

    da2, inners = None, []
    grad_jobs = []
    for chunk in range(CHUNKS):
        w_chunk = ffn_jobs[chunk].value
        w_gu, w_down_t = w_chunk[:, : 2 * units], w_chunk[:, 2 * units :]
        gate_up = dot_nn(a2, w_gu)
        d_inner = dot_nn(g_all, w_down_t)
        (gate_up,) = rounds.pump(gate_up)
        gate, upper = gate_up[:, :units], gate_up[:, units:]
        sigma = jax.nn.sigmoid(gate)
        swish = gate * sigma
        inner = (swish * upper).astype(BF16)
        d_gate = (d_inner * upper * sigma * (1.0 + gate * (1.0 - sigma))).astype(BF16)
        d_upper = (d_inner * swish).astype(BF16)
        d_gu = jnp.concatenate([d_gate, d_upper], axis=1)
        inner, d_gu = rounds.pump(inner, d_gu)
        inners.append(inner)
        part_da2 = dot_nt(d_gu, w_gu)
        da2 = part_da2 if da2 is None else da2 + part_da2
        grad_jobs.append(rounds.add(net.scatter_grads([(a2, d_gu), (g_all, inner)]), 4))
    da2, *inners = lax.optimization_barrier((da2.astype(BF16), *inners))
    d_normed_two = net.run(net.scatter_rows(da2.reshape(micro, seq_len, width)))
    mlp = sum(
        dot_nt(inner, job.value[:, 2 * units :]) for inner, job in zip(inners, ffn_jobs)
    )
    d_resid = g_own.astype(F32) + norm_back(d_normed_two, unit_two, recip_two, gain_two)
    acc_ffn_gain = jnp.sum(d_normed_two * unit_two, axis=(0, 1))
    d_resid_all = net.run(net.gather_rows(d_resid.astype(BF16))).reshape(rows, width)
    d_resid_all, mlp = lax.optimization_barrier((d_resid_all, mlp.astype(BF16)))
    mlp_steps = Steps(net.scatter_rows(mlp.reshape(micro, seq_len, width)))
    job_grad_out = rounds.add(net.scatter_grads([(d_resid_all, mixed_bf)]), 4)

    d_mixed = dot_nn(d_resid_all, w_out_t).astype(BF16) * valid_col.astype(BF16)
    (d_mixed,) = net.mix(mlp_steps, d_mixed)
    d_mixed = d_mixed.reshape(micro, seq_len, heads_kv, groups, HEAD_SIZE)
    d_probs = jnp.einsum("mqkgd,mtkd->mkgqt", d_mixed, value, preferred_element_type=F32)
    delta = jnp.sum(probs * d_probs, axis=-1, keepdims=True)
    (d_scores,) = net.mix(mlp_steps, (probs * (d_probs - delta)).astype(BF16))
    layer_out = net.from_local((resid + mlp_steps.value).astype(BF16))
    d_query = scale * jnp.einsum("mkgqt,mtkd->mqkgd", d_scores, key, preferred_element_type=F32)
    d_key = scale * jnp.einsum("mkgqt,mqkgd->mtkd", d_scores, query, preferred_element_type=F32)
    d_value = jnp.einsum("mkgqt,mqkgd->mtkd", probs_bf, d_mixed, preferred_element_type=F32)
    d_query, d_key, d_value = rounds.pump(d_query, d_key, d_value)
    d_query = rotate(
        d_query.reshape(micro, seq_len, heads_q, HEAD_SIZE), cosine, -sine
    )
    d_key = rotate(d_key, cosine, -sine)
    acc_q_gain = jnp.sum(d_query * q_unit, axis=(0, 1, 2))
    acc_k_gain = jnp.sum(d_key * k_unit, axis=(0, 1, 2))
    d_qkv = jnp.concatenate(
        [
            norm_back(d_query, q_unit, q_recip, gain_q).astype(BF16).reshape(rows, q_cols),
            norm_back(d_key, k_unit, k_recip, gain_k).astype(BF16).reshape(rows, kv_cols),
            d_value.astype(BF16).reshape(rows, kv_cols),
        ],
        axis=1,
    )
    (d_qkv,) = rounds.pump(d_qkv)
    job_grad_qkv = rounds.add(net.scatter_grads([(a1, d_qkv)]), 4)
    (da1,) = rounds.pump(dot_nt(d_qkv, w_qkv))
    acc_attn_gain = jnp.sum(da1 * unit_all, axis=0)
    d_normed = net.run(net.scatter_rows(da1.astype(BF16).reshape(micro, seq_len, width)))
    unit_one, recip_one = unit_of(x_own.astype(F32))
    input_grad = net.from_local(
        (d_resid + norm_back(d_normed, unit_one, recip_one, gain_one)).astype(BF16)
    )

    sums = net.sum_all(
        jnp.concatenate(
            [
                net.plain_vector(acc_attn_gain),
                net.plain_vector(acc_ffn_gain),
                acc_q_gain,
                acc_k_gain,
            ]
        )
    )
    rounds.drain()
    grad_qkv = job_grad_qkv.value
    grads_ffn = [job.value for job in grad_jobs]

    def own_part(start, size):
        return lax.dynamic_slice_in_dim(sums, start + net.me * size, size, 0)

    return (
        layer_out,
        input_grad,
        own_part(0, share),
        grad_qkv[:, :q_cols],
        grad_qkv[:, q_cols : q_cols + kv_cols],
        grad_qkv[:, q_cols + kv_cols :],
        own_part(2 * width, head_share),
        own_part(2 * width + HEAD_SIZE, head_share),
        job_grad_out.value.T,
        own_part(width, share),
        jnp.concatenate([g[:, :units] for g in grads_ffn], axis=1),
        jnp.concatenate([g[:, units : 2 * units] for g in grads_ffn], axis=1),
        jnp.concatenate([g[:, 2 * units :] for g in grads_ffn], axis=1).T,
    )


def solution(mesh):
    dp, tensor = mesh.shape["dp"], mesh.shape["tensor"]
    kind = Links if (dp, tensor) == (8, 4) else Direct
    weight, weight_t = P("dp", "tensor"), P("tensor", "dp")
    acts, ids = P(None, ("dp", "tensor"), None), P(None, "dp")
    gain = P("dp")

    def step(*args):
        return on_device(lambda: kind(dp, tensor), *args)

    return jax.shard_map(
        step,
        mesh=mesh,
        in_specs=(
            acts,
            acts,
            ids,
            ids,
            ids,
            gain,
            weight,
            weight,
            weight,
            gain,
            gain,
            weight_t,
            gain,
            weight,
            weight,
            weight_t,
        ),
        out_specs=(
            acts,
            acts,
            gain,
            weight,
            weight,
            weight,
            gain,
            gain,
            weight_t,
            gain,
            weight,
            weight,
            weight_t,
        ),
        check_vma=False,
    )
```

```python
import functools
import math

import jax
import jax.numpy as jnp
from jax import lax
from jax.experimental import pallas as pl
from jax.experimental.pallas import tpu as pltpu
from jax.sharding import PartitionSpec as P

HEAD_SIZE = 128
EPS = 1e-06
THETA = 1000000.0
CHUNKS = 3
F32 = jnp.float32
BF16 = jnp.bfloat16

ORDER = (0, 2, 4, 6, 1, 3, 5, 7)
PAIR = [(d, d ^ 2) for d in range(8)]
ACROSS = [(d, d ^ 4) for d in range(8)]
CORE = [(d, d ^ 1) for d in range(8)]
INNER = [(2, 4), (3, 5), (4, 2), (5, 3)]
OUTWARD = [(2, 0), (3, 1), (4, 6), (5, 7)]
INWARD = [(0, 2), (1, 3), (6, 4), (7, 5)]
XNEXT = [(t, t ^ 1) for t in range(4)]
YNEXT = [(t, t ^ 2) for t in range(4)]


def add_rounded(left, right):
    return (left.astype(F32) + right.astype(F32)).astype(BF16)


def dot_nn(left, right):
    return jnp.dot(left, right, preferred_element_type=F32)


def dot_nt(left, right):
    return lax.dot_general(left, right, (((1,), (1,)), ((), ())), preferred_element_type=F32)


def dot_tn(left, right):
    return lax.dot_general(left, right, (((0,), (0,)), ((), ())), preferred_element_type=F32)


def block_move(table, rows):
    micro, count, width = rows.shape
    blocks = table.shape[0]
    size = width // blocks

    def body(table_ref, in_ref, out_ref):
        for i in range(blocks):
            start = pl.multiple_of(table_ref[i] * size, size)
            out_ref[:, :, i * size : (i + 1) * size] = in_ref[:, :, pl.ds(start, size)]

    return pl.pallas_call(
        body,
        out_shape=jax.ShapeDtypeStruct(rows.shape, rows.dtype),
        grid_spec=pltpu.PrefetchScalarGridSpec(
            num_scalar_prefetch=1,
            grid=(micro,),
            in_specs=[pl.BlockSpec((1, count, width), lambda i, ref: (i, 0, 0))],
            out_specs=pl.BlockSpec((1, count, width), lambda i, ref: (i, 0, 0)),
        ),
        cost_estimate=pl.CostEstimate(
            flops=0, bytes_accessed=4 * micro * count * width, transcendentals=0
        ),
    )(table, rows)


def turn(rows, cosine, sine):
    return rows * cosine + pltpu.roll(rows, HEAD_SIZE // 2, 1) * sine


def allowed_bias(col_ref, row_ref):
    segment, row_id, valid = row_ref[0, 0:1, :], row_ref[0, 1:2, :], row_ref[0, 2:3, :]
    segment_col, row_id_col = col_ref[:, 0:1], col_ref[:, 1:2]
    allowed = (
        (segment_col == segment)
        & (row_id <= row_id_col)
        & ((valid > 0) | (row_id == row_id_col))
    )
    return jnp.where(allowed, 0.0, -1e30)


def head(index):
    return slice(index * HEAD_SIZE, (index + 1) * HEAD_SIZE)


def softmax_rows(query, key, bias):
    scores = dot_nt(query, key) * (1.0 / math.sqrt(HEAD_SIZE)) + bias
    shifted = jnp.exp(scores - jnp.max(scores, axis=-1, keepdims=True))
    return shifted * (1.0 / jnp.sum(shifted, axis=-1, keepdims=True))


def attention_forward(
    heads_q, heads_kv, qkv_ref, cos_ref, sin_ref, col_ref, row_ref, gain_q_ref, gain_k_ref, out_ref
):
    cosine, sine = cos_ref[...], sin_ref[...]
    bias = allowed_bias(col_ref, row_ref)
    valid = col_ref[:, 2:3].astype(F32)
    groups = heads_q // heads_kv
    for kv in range(heads_kv):
        k_unit, _ = unit_of(qkv_ref[:, head(heads_q + kv)])
        key = turn(k_unit * gain_k_ref[...], cosine, sine).astype(BF16)
        value = qkv_ref[:, head(heads_q + heads_kv + kv)].astype(BF16)
        for h in range(kv * groups, (kv + 1) * groups):
            q_unit, _ = unit_of(qkv_ref[:, head(h)])
            query = turn(q_unit * gain_q_ref[...], cosine, sine).astype(BF16)
            probs = softmax_rows(query, key, bias).astype(BF16)
            out_ref[:, head(h)] = (dot_nn(probs, value) * valid).astype(BF16)


def attention_backward(
    heads_q,
    heads_kv,
    qkv_ref,
    grad_ref,
    cos_ref,
    sin_ref,
    col_ref,
    row_ref,
    gain_q_ref,
    gain_k_ref,
    out_ref,
    sums_ref,
):
    cosine, sine = cos_ref[...], sin_ref[...]
    bias = allowed_bias(col_ref, row_ref)
    valid = col_ref[:, 2:3].astype(BF16)
    groups = heads_q // heads_kv
    scale = 1.0 / math.sqrt(HEAD_SIZE)
    gain_q, gain_k = gain_q_ref[...], gain_k_ref[...]
    sum_q = sum_k = jnp.zeros((1, HEAD_SIZE), F32)
    for kv in range(heads_kv):
        k_unit, k_recip = unit_of(qkv_ref[:, head(heads_q + kv)])
        key = turn(k_unit * gain_k, cosine, sine).astype(BF16)
        value = qkv_ref[:, head(heads_q + heads_kv + kv)].astype(BF16)
        d_key = d_value = None
        for h in range(kv * groups, (kv + 1) * groups):
            q_unit, q_recip = unit_of(qkv_ref[:, head(h)])
            query = turn(q_unit * gain_q, cosine, sine).astype(BF16)
            probs = softmax_rows(query, key, bias)
            d_mixed = grad_ref[:, head(h)] * valid
            d_probs = dot_nt(d_mixed, value)
            delta = jnp.sum(probs * d_probs, axis=-1, keepdims=True)
            d_scores = (probs * (d_probs - delta)).astype(BF16)
            d_query = turn(scale * dot_nn(d_scores, key), cosine, -sine)
            sum_q = sum_q + jnp.sum(d_query * q_unit, axis=0, keepdims=True)
            out_ref[:, head(h)] = norm_back(d_query, q_unit, q_recip, gain_q).astype(BF16)
            part_key, part_value = dot_tn(d_scores, query), dot_tn(probs.astype(BF16), d_mixed)
            d_key = part_key if d_key is None else d_key + part_key
            d_value = part_value if d_value is None else d_value + part_value
        d_key = turn(scale * d_key, cosine, -sine)
        sum_k = sum_k + jnp.sum(d_key * k_unit, axis=0, keepdims=True)
        out_ref[:, head(heads_q + kv)] = norm_back(d_key, k_unit, k_recip, gain_k).astype(BF16)
        out_ref[:, head(heads_q + heads_kv + kv)] = d_value.astype(BF16)
    sums_ref[0, 0:1, :] = sum_q
    sums_ref[0, 1:2, :] = sum_k


def attention_call(body, micro, heads_q, heads_kv, wide, tables, out_shape, out_specs, passes):
    seq_len = wide[0].shape[0] // micro

    def rows_of(array):
        return pl.BlockSpec((seq_len, array.shape[1]), lambda i: (i, 0))

    def whole(array):
        return pl.BlockSpec(array.shape, lambda i: (0, 0))

    cosine, sine, col, row, gain_q, gain_k = tables
    return pl.pallas_call(
        functools.partial(body, heads_q, heads_kv),
        out_shape=out_shape,
        grid=(micro,),
        in_specs=[rows_of(array) for array in (*wide, cosine, sine, col)]
        + [
            pl.BlockSpec((1,) + row.shape[1:], lambda i: (i, 0, 0)),
            whole(gain_q),
            whole(gain_k),
        ],
        out_specs=out_specs,
        cost_estimate=pl.CostEstimate(
            flops=2 * passes * micro * heads_q * seq_len * seq_len * HEAD_SIZE,
            bytes_accessed=sum(array.size * array.dtype.itemsize for array in wide) * 2,
            transcendentals=micro * heads_q * seq_len * seq_len,
        ),
    )(*wide, *tables)


class ZLane:
    def __init__(self, me, own, out, send_sems, recv_sems):
        self.me, self.own, self.out = me, own, out
        self.send_sems, self.recv_sems = send_sems, recv_sems

    def copy(self, index, source, slot, device):
        return pltpu.make_async_remote_copy(
            src_ref=source,
            dst_ref=self.out.at[slot],
            send_sem=self.send_sems.at[index],
            recv_sem=self.recv_sems.at[slot],
            device_id={"dp": device},
            device_id_type=pl.DeviceIdType.MESH,
        )

    def parts(self, slot):
        return self.own if slot == 0 else self.out.at[slot]

    def along(self, slot):
        index, to_slot, bits = {0: (1, 3, 6), 1: (2, 2, 6), 3: (3, 2, 2), 2: (4, 3, 2)}[slot]
        return self.copy(index, self.parts(slot), to_slot, self.me ^ bits)

    def across(self, slot):
        return self.copy(5 + slot, self.parts(slot), 4 + slot, self.me ^ 1)

    def pair(self):
        return self.copy(0, self.own, 1, self.me ^ 2)

    def arrived(self, slot):
        self.copy(0, self.own, slot, self.me ^ 2).wait_recv()

    def begin(self, inner):
        self.pair().start()

        @pl.when(inner)
        def _():
            self.along(0).start()

        self.across(0).start()

    def middle(self, inner):
        self.arrived(1)

        @pl.when(inner)
        def _():
            self.along(1).start()
            self.arrived(3)
            self.along(3).start()
            self.across(3).start()

        self.across(1).start()

    def last(self, inner):
        self.arrived(2)

        @pl.when(inner)
        def _():
            self.along(2).start()

        self.across(2).start()

        @pl.when(jnp.logical_not(inner))
        def _():
            self.arrived(3)
            self.across(3).start()

    def end(self, inner):
        self.pair().wait_send()
        for slot in range(4):
            self.across(slot).wait_send()
            self.arrived(4 + slot)

        @pl.when(inner)
        def _():
            for slot in range(4):
                self.along(slot).wait_send()


def first_gathers(
    x_ref, qkv_ref, out_ref, gain_ref, x_all, qkv_all, out_all, gain_all, local_sems, *sems
):
    me, own = lax.axis_index("dp"), lax.axis_index("tensor")
    z = me // 2
    inner = (z == 1) | (z == 2)
    barrier = pltpu.get_barrier_semaphore()
    peers = [{"dp": me ^ bits} for bits in (1, 2, 6)]
    peers += [{"tensor": own ^ bit} for bit in (1, 2)]
    for device in peers:
        pl.semaphore_signal(barrier, device_id=device, device_id_type=pl.DeviceIdType.MESH)
    pl.semaphore_wait(barrier, len(peers))

    x_send, x_recv, qkv_send, qkv_recv, out_send, out_recv, gain_send, gain_recv = sems
    local = [
        pltpu.make_async_copy(source, target, local_sems.at[i])
        for i, (source, target) in enumerate(
            (
                (x_ref.at[0], x_all.at[0, 0]),
                (x_ref.at[1], x_all.at[1, 0]),
                (qkv_ref, qkv_all.at[0]),
                (out_ref, out_all.at[0]),
                (gain_ref, gain_all.at[0]),
            )
        )
    ]

    def plane(index, source, part, slot, bit):
        return pltpu.make_async_remote_copy(
            src_ref=source,
            dst_ref=x_all.at[part, slot],
            send_sem=x_send.at[index],
            recv_sem=x_recv.at[index],
            device_id={"tensor": own ^ bit},
            device_id_type=pl.DeviceIdType.MESH,
        )

    qkv_lane = ZLane(me, qkv_ref, qkv_all, qkv_send, qkv_recv)
    out_lane = ZLane(me, out_ref, out_all, out_send, out_recv)
    gain_lane = ZLane(me, gain_ref, gain_all, gain_send, gain_recv)
    x_first = plane(0, x_ref.at[0], 0, 1, 1)
    y_second = plane(1, x_ref.at[1], 1, 2, 2)
    x_second = plane(2, x_ref.at[1], 1, 1, 1)
    y_first = plane(3, x_ref.at[0], 0, 2, 2)
    d_first = plane(4, x_all.at[0, 1], 0, 3, 2)
    d_second = plane(5, x_all.at[1, 2], 1, 3, 1)
    gain_lane.begin(inner)
    qkv_lane.begin(inner)
    for copy in (x_first, y_second, x_second, y_first):
        copy.start()
    for copy in local:
        copy.start()
    gain_lane.middle(inner)
    gain_lane.last(inner)
    x_first.wait_recv()
    d_first.start()
    y_second.wait_recv()
    d_second.start()
    qkv_lane.middle(inner)
    out_lane.begin(inner)
    qkv_lane.last(inner)
    out_lane.middle(inner)
    out_lane.last(inner)
    for copy in (x_second, y_first, d_first, d_second):
        copy.wait_recv()
    for copy in (x_first, y_second, x_second, y_first, d_first, d_second):
        copy.wait_send()
    for copy in local:
        copy.wait()
    gain_lane.end(inner)
    qkv_lane.end(inner)
    out_lane.end(inner)


class Job:
    def __init__(self, gen, open_at):
        self.gen, self.open_at = gen, open_at
        self.rounds, self.flight, self.value, self.done = 0, (), None, False

    def step(self, results, anchor=()):
        try:
            sends = self.gen.send(results)
        except StopIteration as stop:
            self.value, self.done, self.flight = stop.value, True, ()
            return
        arrays = [array for array, _ in sends]
        if anchor:
            arrays = lax.optimization_barrier((*arrays, *anchor))[: len(arrays)]
        self.flight = tuple(
            lax.ppermute(array, "dp", perm) for array, (_, perm) in zip(arrays, sends)
        )
        self.rounds += 1

    @property
    def open(self):
        return self.done or self.rounds >= self.open_at


class Rounds:
    def __init__(self):
        self.live, self.queue = [], []

    def add(self, gen, open_at):
        job = Job(gen, open_at)
        self.queue.append(job)
        return job

    def pump(self, *values):
        flight = [array for job in self.live for array in job.flight]
        if flight:
            out = lax.optimization_barrier((*values, *flight))
            values, flight = out[: len(values)], list(out[len(values) :])
            for job in self.live:
                count = len(job.flight)
                results, flight = flight[:count], flight[count:]
                job.step(results)
            self.live = [job for job in self.live if not job.done]
        while self.queue and all(job.open for job in self.live):
            job = self.queue.pop(0)
            job.step(None, values[:1])
            if not job.done:
                self.live.append(job)
        return values

    def drain(self):
        while self.live or self.queue:
            self.pump()


class Steps:
    def __init__(self, gen):
        self.gen, self.pending, self.value = gen, (), None
        self.feed(None)

    def feed(self, results):
        try:
            self.pending = self.gen.send(results)
        except StopIteration as stop:
            self.value, self.pending = stop.value, ()


class Direct:
    def __init__(self, dp, tensor):
        self.dp, self.tensor = dp, tensor
        self.me = lax.axis_index("dp")
        self.own = lax.axis_index("tensor")
        self.rounds = Rounds()

    def mix(self, steps, *values):
        out = self.rounds.pump(*values, *steps.pending)
        if steps.pending:
            steps.feed(out[len(values) :])
        return out[: len(values)]

    def run(self, gen):
        steps = Steps(gen)
        while steps.pending:
            self.mix(steps)
        return steps.value

    def free(self, gen):
        steps = gen if isinstance(gen, Steps) else Steps(gen)
        while steps.pending:
            steps.feed(lax.optimization_barrier(steps.pending))
        return steps.value

    def to_local(self, rows):
        return rows

    def from_local(self, rows):
        return rows

    def row_order(self, value):
        return value

    def gains_local(self, blocks):
        return blocks.reshape(-1)

    def gains_plain(self, blocks):
        return blocks.reshape(-1)

    def plain_vector(self, vector):
        return vector

    def sum_all(self, vector):
        return lax.psum(vector, ("dp", "tensor"))

    def gather_weights(self, buf):
        return list(lax.all_gather(buf, "dp", axis=0))
        yield

    def first_gathers(self, rows, *weights):
        gathered = self.free(self.gather_rows(rows))
        return gathered, *(lax.all_gather(array, "dp", axis=0) for array in weights)

    def scatter_grads(self, parts):
        full = jnp.concatenate([dot_tn(l, r).astype(BF16) for l, r in parts], axis=1)
        return lax.psum_scatter(full, "dp", scatter_dimension=0, tiled=True).astype(F32)
        yield

    def gather_rows(self, rows):
        return lax.all_gather(rows, "tensor", axis=1, tiled=True)
        yield

    def scatter_rows(self, partial):
        return lax.psum_scatter(partial, "tensor", scatter_dimension=1, tiled=True).astype(F32)
        yield


class Links(Direct):
    def __init__(self, dp, tensor):
        super().__init__(dp, tensor)
        z = self.me // 2
        self.inner = (z == 1) | (z == 2)
        self.blocks = self.me ^ jnp.array(ORDER, jnp.int32)
        hit = (self.me ^ jnp.arange(8, dtype=jnp.int32))[:, None] == jnp.array(ORDER, jnp.int32)
        self.hit = hit
        self.places = jnp.sum(jnp.where(hit, jnp.arange(8, dtype=jnp.int32)[None, :], 0), axis=1)

    def to_local(self, rows):
        return block_move(self.blocks, rows)

    def from_local(self, rows):
        return block_move(self.places, rows)

    def row_order(self, value):
        parts = list(jnp.split(value, 4, axis=-1))
        for bit in (1, 2):
            swap = (self.own & bit) != 0
            parts = [jnp.where(swap, parts[j ^ bit], parts[j]) for j in range(4)]
        return jnp.concatenate(parts, axis=-1)

    def gains_plain(self, blocks):
        return jnp.sum(jnp.where(self.hit[:, :, None], blocks[None], 0), axis=1).reshape(-1)

    def plain_vector(self, vector):
        return self.gains_plain(vector.reshape(8, -1))

    def sum_all(self, vector):
        for axis, perm in (
            ("tensor", XNEXT),
            ("tensor", YNEXT),
            ("dp", CORE),
            ("dp", PAIR),
            ("dp", ACROSS),
        ):
            vector = vector + lax.ppermute(vector, axis, perm)
        return vector

    def gather_weights(self, buf):
        pair, over_own, other = yield [(buf, PAIR), (buf, INNER), (buf, CORE)]
        over_pair, out_own, other_pair = yield [(pair, INNER), (over_own, OUTWARD), (pair, CORE)]
        two = jnp.where(self.inner, over_pair, out_own)
        out_pair, other_two = yield [(over_pair, OUTWARD), (two, CORE)]
        three = jnp.where(self.inner, over_own, out_pair)
        other_three = lax.ppermute(three, "dp", CORE)
        return [buf, pair, two, three, other, other_pair, other_two, other_three]

    def first_gathers(self, rows, *weights):
        micro, count, width = rows.shape
        hbm = pl.BlockSpec(memory_space=pl.ANY)
        lanes = len(weights)
        return pl.pallas_call(
            first_gathers,
            out_shape=(
                jax.ShapeDtypeStruct((micro, 4, count, width), rows.dtype),
                *(jax.ShapeDtypeStruct((8,) + w.shape, w.dtype) for w in weights),
            ),
            in_specs=[hbm] * (1 + lanes),
            out_specs=[hbm] * (1 + lanes),
            scratch_shapes=[
                pltpu.SemaphoreType.DMA((copies,)) for copies in (5, 6, 6, *(9, 8) * lanes)
            ],
            compiler_params=pltpu.CompilerParams(collective_id=0, has_side_effects=True),
        )(rows, *weights)

    def scatter_grads(self, parts):
        away, half = [], parts[0][0].shape[1] // 2
        for left, right in parts:
            away.append(dot_tn(left[:, half:], right).astype(BF16))
        summed = [
            (dot_tn(left[:, :half], right) + lax.ppermute(array, "dp", CORE).astype(F32)).astype(BF16)
            for (left, right), array in zip(parts, away)
        ]
        own, pair, two, three = jnp.split(jnp.concatenate(summed, axis=1), 4, axis=0)
        (got,) = yield [(three, INWARD)]
        two_sum = add_rounded(two, got)
        got, got_inner = yield [(two, INWARD), (two_sum, INNER)]
        three, pair = add_rounded(three, got), add_rounded(pair, got_inner)
        got_inner, got_pair = yield [(three, INNER), (pair, PAIR)]
        return own.astype(F32) + got_inner.astype(F32) + got_pair.astype(F32)

    def gather_rows(self, rows):
        near_x, near_y = yield (
            lax.ppermute(rows, "tensor", XNEXT),
            lax.ppermute(rows, "tensor", YNEXT),
        )
        diag_first, diag_second = yield (
            lax.ppermute(near_x[0], "tensor", YNEXT),
            lax.ppermute(near_y[1], "tensor", XNEXT),
        )
        return jnp.concatenate([rows, near_x, near_y, jnp.stack([diag_first, diag_second])], axis=1)

    def scatter_rows(self, partial):
        first, second = (jnp.split(partial[i], 4, axis=0) for i in range(2))
        near_first, near_second = yield (
            lax.ppermute(jnp.stack([first[1], first[3]]), "tensor", XNEXT),
            lax.ppermute(jnp.stack([second[2], second[3]]), "tensor", YNEXT),
        )
        far_first, far_second = yield (
            lax.ppermute(add_rounded(first[2], near_first[1]), "tensor", YNEXT),
            lax.ppermute(add_rounded(second[1], near_second[1]), "tensor", XNEXT),
        )
        return jnp.stack(
            [
                first[0].astype(F32) + near_first[0].astype(F32) + far_first.astype(F32),
                second[0].astype(F32) + near_second[0].astype(F32) + far_second.astype(F32),
            ]
        )


def unit_of(rows):
    recip = lax.rsqrt(jnp.mean(rows * rows, axis=-1, keepdims=True) + EPS)
    return rows * recip, recip


def norm_back(upstream, unit, recip, gain):
    scaled = upstream * gain
    return recip * (scaled - unit * jnp.mean(scaled * unit, axis=-1, keepdims=True))


def rotary(offsets):
    freqs = jnp.exp(
        jnp.arange(0, HEAD_SIZE, 2).astype(F32) * (-math.log(THETA) / HEAD_SIZE)
    )
    angles = offsets.astype(F32)[..., None] * freqs
    cosine, sine = jnp.cos(angles), jnp.sin(angles)
    return jnp.concatenate([cosine, cosine], -1), jnp.concatenate([-sine, sine], -1)


def on_device(
    net,
    hidden_in,
    cotangent,
    segment_ids,
    positions,
    pad_mask,
    attn_gain,
    w_query,
    key_weight,
    value_weight,
    query_norm_gain,
    key_gain,
    w_out,
    ffn_gain,
    w_gate,
    w_up,
    w_down,
):
    net = net()
    micro, own_rows, width = hidden_in.shape
    seq_len = segment_ids.shape[1]
    rows = micro * seq_len
    share = attn_gain.shape[0]
    head_share = query_norm_gain.shape[0]
    q_cols, kv_cols = w_query.shape[1], key_weight.shape[1]
    heads_q, heads_kv = q_cols // HEAD_SIZE, kv_cols // HEAD_SIZE
    units = w_gate.shape[1] // CHUNKS

    rounds = net.rounds
    x_own = net.to_local(hidden_in)
    packed = jnp.concatenate([attn_gain, ffn_gain, query_norm_gain, key_gain], axis=0)
    pad = -packed.shape[0] % 2048
    packed = jnp.pad(packed, (0, pad)).reshape(-1, 128)
    x_all, w_qkv, w_out_t, gains = net.first_gathers(
        x_own, jnp.concatenate([w_query, key_weight, value_weight], axis=1), w_out.T, packed
    )
    w_qkv = w_qkv.reshape(width, -1)
    w_out_t = w_out_t.reshape(width, -1)
    gains = gains.reshape(gains.shape[0], -1).astype(F32)
    x_bf = x_all.reshape(rows, width)
    later = (segment_ids, positions, pad_mask, cotangent, w_gate, w_up, w_down)
    x_bf, *later = lax.optimization_barrier((x_bf, *later))
    segment_ids, positions, pad_mask, cotangent, *ffn_weights = later
    ffn_jobs = []

    def gather_chunk(chunk, w_gate, w_up, w_down):
        cut = slice(chunk * units, (chunk + 1) * units)
        buf = jnp.concatenate([w_gate[:, cut], w_up[:, cut], w_down[cut, :].T], axis=1)
        ffn_jobs.append(rounds.add(net.gather_weights(buf), 4))

    gather_chunk(0, *ffn_weights)
    (x_bf,) = rounds.pump(x_bf)
    g_own, x_bf = lax.optimization_barrier((net.to_local(cotangent), x_bf))
    g_steps = Steps(net.gather_rows(g_own))
    gain_one = net.gains_local(gains[:, :share])
    gain_two = net.gains_local(gains[:, share : 2 * share])
    gain_q = net.gains_plain(gains[:, 2 * share : 2 * share + head_share])
    gain_k = net.gains_plain(gains[:, 2 * share + head_share : 2 * (share + head_share)])

    segment = net.row_order(segment_ids)
    offsets = net.row_order(positions)
    valid = net.row_order(pad_mask)
    row_ids = net.row_order(jnp.arange(seq_len, dtype=jnp.int32))
    cosine, sine = rotary(offsets.reshape(rows))
    ids = jnp.stack([segment, jnp.broadcast_to(row_ids, segment.shape), valid], axis=1)
    ids_col = jnp.stack([ids[:, i].reshape(rows) for i in range(3)], axis=1)
    tables = (cosine, sine, ids_col, ids, gain_q.reshape(1, -1), gain_k.reshape(1, -1))
    unit_all, _ = unit_of(x_bf.astype(F32))
    a1 = (unit_all * gain_one).astype(BF16)
    (qkv,) = net.mix(g_steps, dot_nn(a1, w_qkv))
    mixed_bf = attention_call(
        attention_forward,
        micro,
        heads_q,
        heads_kv,
        (qkv,),
        tables,
        jax.ShapeDtypeStruct((rows, q_cols), BF16),
        pl.BlockSpec((seq_len, q_cols), lambda i: (i, 0)),
        2,
    )
    (mixed_bf,) = net.mix(g_steps, mixed_bf)
    mixed_bf, *ffn_weights = lax.optimization_barrier((mixed_bf, *ffn_weights))
    for chunk in range(1, CHUNKS):
        gather_chunk(chunk, *ffn_weights)
    attn_part = dot_nt(mixed_bf, w_out_t).astype(BF16).reshape(micro, seq_len, width)
    resid = x_own.astype(F32) + net.run(net.scatter_rows(attn_part))
    unit_two, recip_two = unit_of(resid)
    a2_own = (unit_two * gain_two).astype(BF16)
    a2 = net.run(net.gather_rows(a2_own)).reshape(rows, width)
    g_all = net.free(g_steps).reshape(rows, width)

    da2, inners, w_chunks = None, [], []
    grad_jobs = []
    for chunk in range(CHUNKS):
        w_chunk = jnp.concatenate(ffn_jobs[chunk].value, axis=0)
        w_chunks.append(w_chunk)
        w_gu, w_down_t = w_chunk[:, : 2 * units], w_chunk[:, 2 * units :]
        gate_up = dot_nn(a2, w_gu)
        d_inner = dot_nn(g_all, w_down_t)
        (gate_up,) = rounds.pump(gate_up)
        gate, upper = gate_up[:, :units], gate_up[:, units:]
        sigma = jax.nn.sigmoid(gate)
        swish = gate * sigma
        inner = (swish * upper).astype(BF16)
        d_gate = (d_inner * upper * sigma * (1.0 + gate * (1.0 - sigma))).astype(BF16)
        d_upper = (d_inner * swish).astype(BF16)
        d_gu = jnp.concatenate([d_gate, d_upper], axis=1)
        inner, d_gu = rounds.pump(inner, d_gu)
        inners.append(inner)
        part_da2 = dot_nt(d_gu, w_gu)
        da2 = part_da2 if da2 is None else da2 + part_da2
        grad_jobs.append(rounds.add(net.scatter_grads([(a2, d_gu), (g_all, inner)]), 3 if chunk == CHUNKS - 1 else 4))
    da2, *inners = lax.optimization_barrier((da2.astype(BF16), *inners))
    d_normed_two = net.run(net.scatter_rows(da2.reshape(micro, seq_len, width)))
    mlp = sum(
        dot_nt(inner, w_chunk[:, 2 * units :]) for inner, w_chunk in zip(inners, w_chunks)
    )
    d_resid = g_own.astype(F32) + norm_back(d_normed_two, unit_two, recip_two, gain_two)
    acc_ffn_gain = jnp.sum(d_normed_two * unit_two, axis=(0, 1))
    d_resid_all = net.run(net.gather_rows(d_resid.astype(BF16))).reshape(rows, width)
    d_resid_all, mlp = lax.optimization_barrier((d_resid_all, mlp.astype(BF16)))
    mlp_steps = Steps(net.scatter_rows(mlp.reshape(micro, seq_len, width)))
    job_grad_out = rounds.add(net.scatter_grads([(d_resid_all, mixed_bf)]), 3)

    (d_mixed,) = net.mix(mlp_steps, dot_nn(d_resid_all, w_out_t).astype(BF16))
    d_qkv, head_sums = attention_call(
        attention_backward,
        micro,
        heads_q,
        heads_kv,
        (qkv, d_mixed),
        tables,
        (
            jax.ShapeDtypeStruct(qkv.shape, BF16),
            jax.ShapeDtypeStruct((micro, 2, HEAD_SIZE), F32),
        ),
        (
            pl.BlockSpec((seq_len, qkv.shape[1]), lambda i: (i, 0)),
            pl.BlockSpec((1, 2, HEAD_SIZE), lambda i: (i, 0, 0)),
        ),
        5,
    )
    acc_q_gain, acc_k_gain = jnp.sum(head_sums, axis=0)
    (d_qkv,) = net.mix(mlp_steps, d_qkv)
    layer_out = net.from_local((resid + net.free(mlp_steps)).astype(BF16))
    job_grad_qkv = rounds.add(net.scatter_grads([(a1, d_qkv)]), 4)
    (da1,) = rounds.pump(dot_nt(d_qkv, w_qkv))
    acc_attn_gain = jnp.sum(da1 * unit_all, axis=0)
    d_normed = net.run(net.scatter_rows(da1.astype(BF16).reshape(micro, seq_len, width)))
    unit_one, recip_one = unit_of(x_own.astype(F32))
    input_grad = net.from_local(
        (d_resid + norm_back(d_normed, unit_one, recip_one, gain_one)).astype(BF16)
    )

    sums = net.sum_all(
        jnp.concatenate(
            [
                net.plain_vector(acc_attn_gain),
                net.plain_vector(acc_ffn_gain),
                acc_q_gain,
                acc_k_gain,
            ]
        )
    )
    rounds.drain()
    grad_qkv = job_grad_qkv.value
    grads_ffn = [job.value for job in grad_jobs]

    def own_part(start, size):
        return lax.dynamic_slice_in_dim(sums, start + net.me * size, size, 0)

    return (
        layer_out,
        input_grad,
        own_part(0, share),
        grad_qkv[:, :q_cols],
        grad_qkv[:, q_cols : q_cols + kv_cols],
        grad_qkv[:, q_cols + kv_cols :],
        own_part(2 * width, head_share),
        own_part(2 * width + HEAD_SIZE, head_share),
        job_grad_out.value.T,
        own_part(width, share),
        jnp.concatenate([g[:, :units] for g in grads_ffn], axis=1),
        jnp.concatenate([g[:, units : 2 * units] for g in grads_ffn], axis=1),
        jnp.concatenate([g[:, 2 * units :] for g in grads_ffn], axis=1).T,
    )


def solution(mesh):
    dp, tensor = mesh.shape["dp"], mesh.shape["tensor"]
    kind = Links if (dp, tensor) == (8, 4) else Direct
    weight, weight_t = P("dp", "tensor"), P("tensor", "dp")
    acts, ids = P(None, ("dp", "tensor"), None), P(None, "dp")
    gain = P("dp")

    def step(*args):
        return on_device(lambda: kind(dp, tensor), *args)

    return jax.shard_map(
        step,
        mesh=mesh,
        in_specs=(
            acts,
            acts,
            ids,
            ids,
            ids,
            gain,
            weight,
            weight,
            weight,
            gain,
            gain,
            weight_t,
            gain,
            weight,
            weight,
            weight_t,
        ),
        out_specs=(
            acts,
            acts,
            gain,
            weight,
            weight,
            weight,
            gain,
            gain,
            weight_t,
            gain,
            weight,
            weight,
            weight_t,
        ),
        check_vma=False,
    )
```

```python
import functools
import math

import jax
import jax.numpy as jnp
from jax import lax
from jax.experimental import pallas as pl
from jax.experimental.pallas import tpu as pltpu
from jax.sharding import PartitionSpec as P

HEAD_SIZE = 128
EPS = 1e-06
THETA = 1000000.0
CHUNKS = 2
F32 = jnp.float32
BF16 = jnp.bfloat16

ORDER = (0, 2, 4, 6, 1, 3, 5, 7)
PAIR = [(d, d ^ 2) for d in range(8)]
ACROSS = [(d, d ^ 4) for d in range(8)]
CORE = [(d, d ^ 1) for d in range(8)]
INNER = [(2, 4), (3, 5), (4, 2), (5, 3)]
OUTWARD = [(2, 0), (3, 1), (4, 6), (5, 7)]
INWARD = [(0, 2), (1, 3), (6, 4), (7, 5)]
XNEXT = [(t, t ^ 1) for t in range(4)]
YNEXT = [(t, t ^ 2) for t in range(4)]


def add_rounded(left, right):
    return (left.astype(F32) + right.astype(F32)).astype(BF16)


def dot_nn(left, right):
    return jnp.dot(left, right, preferred_element_type=F32)


def dot_nt(left, right):
    return lax.dot_general(left, right, (((1,), (1,)), ((), ())), preferred_element_type=F32)


def dot_tn(left, right):
    return lax.dot_general(left, right, (((0,), (0,)), ((), ())), preferred_element_type=F32)


def block_move(table, rows):
    micro, count, width = rows.shape
    blocks = table.shape[0]
    size = width // blocks

    def body(table_ref, in_ref, out_ref):
        for i in range(blocks):
            start = pl.multiple_of(table_ref[i] * size, size)
            out_ref[:, :, i * size : (i + 1) * size] = in_ref[:, :, pl.ds(start, size)]

    return pl.pallas_call(
        body,
        out_shape=jax.ShapeDtypeStruct(rows.shape, rows.dtype),
        grid_spec=pltpu.PrefetchScalarGridSpec(
            num_scalar_prefetch=1,
            grid=(micro,),
            in_specs=[pl.BlockSpec((1, count, width), lambda i, ref: (i, 0, 0))],
            out_specs=pl.BlockSpec((1, count, width), lambda i, ref: (i, 0, 0)),
        ),
        cost_estimate=pl.CostEstimate(
            flops=0, bytes_accessed=4 * micro * count * width, transcendentals=0
        ),
    )(table, rows)


def turn(rows, cosine, sine):
    return rows * cosine + pltpu.roll(rows, HEAD_SIZE // 2, 1) * sine


def allowed_bias(col_ref, row_ref):
    segment, row_id, valid = row_ref[0, 0:1, :], row_ref[0, 1:2, :], row_ref[0, 2:3, :]
    segment_col, row_id_col = col_ref[:, 0:1], col_ref[:, 1:2]
    allowed = (
        (segment_col == segment)
        & (row_id <= row_id_col)
        & ((valid > 0) | (row_id == row_id_col))
    )
    return jnp.where(allowed, 0.0, -1e30)


def head(index):
    return slice(index * HEAD_SIZE, (index + 1) * HEAD_SIZE)


def softmax_rows(query, key, bias):
    scores = dot_nt(query, key) * (1.0 / math.sqrt(HEAD_SIZE)) + bias
    shifted = jnp.exp(scores - jnp.max(scores, axis=-1, keepdims=True))
    return shifted * (1.0 / jnp.sum(shifted, axis=-1, keepdims=True))


def attention_forward(
    heads_q, heads_kv, qkv_ref, cos_ref, sin_ref, col_ref, row_ref, gain_q_ref, gain_k_ref, out_ref
):
    cosine, sine = cos_ref[...], sin_ref[...]
    bias = allowed_bias(col_ref, row_ref)
    valid = col_ref[:, 2:3].astype(F32)
    groups = heads_q // heads_kv
    for kv in range(heads_kv):
        k_unit, _ = unit_of(qkv_ref[:, head(heads_q + kv)])
        key = turn(k_unit * gain_k_ref[...], cosine, sine).astype(BF16)
        value = qkv_ref[:, head(heads_q + heads_kv + kv)].astype(BF16)
        for h in range(kv * groups, (kv + 1) * groups):
            q_unit, _ = unit_of(qkv_ref[:, head(h)])
            query = turn(q_unit * gain_q_ref[...], cosine, sine).astype(BF16)
            probs = softmax_rows(query, key, bias).astype(BF16)
            out_ref[:, head(h)] = (dot_nn(probs, value) * valid).astype(BF16)


def attention_backward(
    heads_q,
    heads_kv,
    qkv_ref,
    grad_ref,
    cos_ref,
    sin_ref,
    col_ref,
    row_ref,
    gain_q_ref,
    gain_k_ref,
    out_ref,
    sums_ref,
):
    cosine, sine = cos_ref[...], sin_ref[...]
    bias = allowed_bias(col_ref, row_ref)
    valid = col_ref[:, 2:3].astype(BF16)
    groups = heads_q // heads_kv
    scale = 1.0 / math.sqrt(HEAD_SIZE)
    gain_q, gain_k = gain_q_ref[...], gain_k_ref[...]
    sum_q = sum_k = jnp.zeros((1, HEAD_SIZE), F32)
    for kv in range(heads_kv):
        k_unit, k_recip = unit_of(qkv_ref[:, head(heads_q + kv)])
        key = turn(k_unit * gain_k, cosine, sine).astype(BF16)
        value = qkv_ref[:, head(heads_q + heads_kv + kv)].astype(BF16)
        d_key = d_value = None
        for h in range(kv * groups, (kv + 1) * groups):
            q_unit, q_recip = unit_of(qkv_ref[:, head(h)])
            query = turn(q_unit * gain_q, cosine, sine).astype(BF16)
            probs = softmax_rows(query, key, bias)
            d_mixed = grad_ref[:, head(h)] * valid
            d_probs = dot_nt(d_mixed, value)
            delta = jnp.sum(probs * d_probs, axis=-1, keepdims=True)
            d_scores = (probs * (d_probs - delta)).astype(BF16)
            d_query = turn(scale * dot_nn(d_scores, key), cosine, -sine)
            sum_q = sum_q + jnp.sum(d_query * q_unit, axis=0, keepdims=True)
            out_ref[:, head(h)] = norm_back(d_query, q_unit, q_recip, gain_q).astype(BF16)
            part_key, part_value = dot_tn(d_scores, query), dot_tn(probs.astype(BF16), d_mixed)
            d_key = part_key if d_key is None else d_key + part_key
            d_value = part_value if d_value is None else d_value + part_value
        d_key = turn(scale * d_key, cosine, -sine)
        sum_k = sum_k + jnp.sum(d_key * k_unit, axis=0, keepdims=True)
        out_ref[:, head(heads_q + kv)] = norm_back(d_key, k_unit, k_recip, gain_k).astype(BF16)
        out_ref[:, head(heads_q + heads_kv + kv)] = d_value.astype(BF16)
    sums_ref[0, 0:1, :] = sum_q
    sums_ref[0, 1:2, :] = sum_k


def attention_call(body, micro, heads_q, heads_kv, wide, tables, out_shape, out_specs, passes):
    seq_len = wide[0].shape[0] // micro

    def rows_of(array):
        return pl.BlockSpec((seq_len, array.shape[1]), lambda i: (i, 0))

    def whole(array):
        return pl.BlockSpec(array.shape, lambda i: (0, 0))

    cosine, sine, col, row, gain_q, gain_k = tables
    return pl.pallas_call(
        functools.partial(body, heads_q, heads_kv),
        out_shape=out_shape,
        grid=(micro,),
        in_specs=[rows_of(array) for array in (*wide, cosine, sine, col)]
        + [
            pl.BlockSpec((1,) + row.shape[1:], lambda i: (i, 0, 0)),
            whole(gain_q),
            whole(gain_k),
        ],
        out_specs=out_specs,
        cost_estimate=pl.CostEstimate(
            flops=2 * passes * micro * heads_q * seq_len * seq_len * HEAD_SIZE,
            bytes_accessed=sum(array.size * array.dtype.itemsize for array in wide) * 2,
            transcendentals=micro * heads_q * seq_len * seq_len,
        ),
    )(*wide, *tables)


class ZLane:
    def __init__(self, me, own, out, send_sems, recv_sems):
        self.me, self.own, self.out = me, own, out
        self.send_sems, self.recv_sems = send_sems, recv_sems

    def copy(self, index, source, slot, device):
        return pltpu.make_async_remote_copy(
            src_ref=source,
            dst_ref=self.out.at[slot],
            send_sem=self.send_sems.at[index],
            recv_sem=self.recv_sems.at[slot],
            device_id={"dp": device},
            device_id_type=pl.DeviceIdType.MESH,
        )

    def parts(self, slot):
        return self.own if slot == 0 else self.out.at[slot]

    def along(self, slot):
        index, to_slot, bits = {0: (1, 3, 6), 1: (2, 2, 6), 3: (3, 2, 2), 2: (4, 3, 2)}[slot]
        return self.copy(index, self.parts(slot), to_slot, self.me ^ bits)

    def across(self, slot):
        return self.copy(5 + slot, self.parts(slot), 4 + slot, self.me ^ 1)

    def pair(self):
        return self.copy(0, self.own, 1, self.me ^ 2)

    def arrived(self, slot):
        self.copy(0, self.own, slot, self.me ^ 2).wait_recv()

    def begin(self, inner):
        self.pair().start()

        @pl.when(inner)
        def _():
            self.along(0).start()

        self.across(0).start()

    def middle(self, inner):
        self.arrived(1)

        @pl.when(inner)
        def _():
            self.along(1).start()
            self.arrived(3)
            self.along(3).start()
            self.across(3).start()

        self.across(1).start()

    def last(self, inner):
        self.arrived(2)

        @pl.when(inner)
        def _():
            self.along(2).start()

        self.across(2).start()

        @pl.when(jnp.logical_not(inner))
        def _():
            self.arrived(3)
            self.across(3).start()

    def end(self, inner):
        self.pair().wait_send()
        for slot in range(4):
            self.across(slot).wait_send()
            self.arrived(4 + slot)

        @pl.when(inner)
        def _():
            for slot in range(4):
                self.along(slot).wait_send()


def first_gathers(
    x_ref, qkv_ref, out_ref, gain_ref, x_all, qkv_all, out_all, gain_all, local_sems, *sems
):
    me, own = lax.axis_index("dp"), lax.axis_index("tensor")
    z = me // 2
    inner = (z == 1) | (z == 2)
    barrier = pltpu.get_barrier_semaphore()
    peers = [{"dp": me ^ bits} for bits in (1, 2, 6)]
    peers += [{"tensor": own ^ bit} for bit in (1, 2)]
    for device in peers:
        pl.semaphore_signal(barrier, device_id=device, device_id_type=pl.DeviceIdType.MESH)
    pl.semaphore_wait(barrier, len(peers))

    x_send, x_recv, qkv_send, qkv_recv, out_send, out_recv, gain_send, gain_recv = sems
    local = [
        pltpu.make_async_copy(source, target, local_sems.at[i])
        for i, (source, target) in enumerate(
            (
                (x_ref.at[0], x_all.at[0, 0]),
                (x_ref.at[1], x_all.at[1, 0]),
                (qkv_ref, qkv_all.at[0]),
                (out_ref, out_all.at[0]),
                (gain_ref, gain_all.at[0]),
            )
        )
    ]

    def plane(index, source, part, slot, bit):
        return pltpu.make_async_remote_copy(
            src_ref=source,
            dst_ref=x_all.at[part, slot],
            send_sem=x_send.at[index],
            recv_sem=x_recv.at[index],
            device_id={"tensor": own ^ bit},
            device_id_type=pl.DeviceIdType.MESH,
        )

    qkv_lane = ZLane(me, qkv_ref, qkv_all, qkv_send, qkv_recv)
    out_lane = ZLane(me, out_ref, out_all, out_send, out_recv)
    gain_lane = ZLane(me, gain_ref, gain_all, gain_send, gain_recv)
    x_first = plane(0, x_ref.at[0], 0, 1, 1)
    y_second = plane(1, x_ref.at[1], 1, 2, 2)
    x_second = plane(2, x_ref.at[1], 1, 1, 1)
    y_first = plane(3, x_ref.at[0], 0, 2, 2)
    d_first = plane(4, x_all.at[0, 1], 0, 3, 2)
    d_second = plane(5, x_all.at[1, 2], 1, 3, 1)
    gain_lane.begin(inner)
    qkv_lane.begin(inner)
    for copy in (x_first, y_second, x_second, y_first):
        copy.start()
    for copy in local:
        copy.start()
    gain_lane.middle(inner)
    gain_lane.last(inner)
    x_first.wait_recv()
    d_first.start()
    y_second.wait_recv()
    d_second.start()
    qkv_lane.middle(inner)
    out_lane.begin(inner)
    qkv_lane.last(inner)
    out_lane.middle(inner)
    out_lane.last(inner)
    for copy in (x_second, y_first, d_first, d_second):
        copy.wait_recv()
    for copy in (x_first, y_second, x_second, y_first, d_first, d_second):
        copy.wait_send()
    for copy in local:
        copy.wait()
    gain_lane.end(inner)
    qkv_lane.end(inner)
    out_lane.end(inner)


class Copies:
    def __init__(self, send_sems, recv_sems):
        self.send_sems, self.recv_sems, self.count = send_sems, recv_sems, 0

    def make(self, source, target, device):
        index = self.count
        self.count += 1
        return pltpu.make_async_remote_copy(
            src_ref=source,
            dst_ref=target,
            send_sem=self.send_sems.at[index],
            recv_sem=self.recv_sems.at[index],
            device_id=device,
            device_id_type=pl.DeviceIdType.MESH,
        )


def greet(peers):
    barrier = pltpu.get_barrier_semaphore()
    for device in peers:
        pl.semaphore_signal(barrier, device_id=device, device_id_type=pl.DeviceIdType.MESH)
    pl.semaphore_wait(barrier, len(peers))


class PlaneSum:
    def __init__(self, copies, own, part_ref, near, far_send, far):
        x, y = {"tensor": own ^ 1}, {"tensor": own ^ 2}
        self.part, self.near, self.far_send, self.far_got = part_ref, near, far_send, far
        self.diag, self.direct, self.far = [], [], []
        for i, (device, other, block) in enumerate(((x, y, 1), (y, x, 2))):
            self.diag.append(copies.make(self.rows(i, 3), near.at[i, 1], device))
            self.direct.append(copies.make(self.rows(i, block), near.at[i, 0], device))
            self.far.append(copies.make(far_send.at[i], far.at[i], other))

    def rows(self, i, block):
        count = self.far_got.shape[1]
        return self.part.at[i, block * count : (block + 1) * count]

    def begin(self):
        for copy in (*self.diag, *self.direct):
            copy.start()

    def middle(self):
        for i in range(2):
            self.diag[i].wait_recv()
            self.far_send[i] = add_rounded(self.rows(i, 2 - i)[...], self.near[i, 1])
            self.far[i].start()

    def arrive(self, i):
        self.direct[i].wait_recv()
        self.far[i].wait_recv()
        return (
            self.rows(i, 0)[...].astype(F32)
            + self.near[i, 0].astype(F32)
            + self.far_got[i].astype(F32)
        )

    def end(self):
        for copy in (*self.diag, *self.direct, *self.far):
            copy.wait_send()


class LineSum:
    def __init__(self, copies, me, inner, in_ref, sent, got):
        self.inner, self.part, self.sent, self.got = inner, in_ref, sent, got
        pair, over = {"dp": me ^ 2}, {"dp": me ^ 6}
        self.inward = [
            copies.make(self.block(3), got.at[0], pair),
            copies.make(self.block(2), got.at[1], pair),
        ]
        self.over = [
            copies.make(sent.at[0], got.at[2], over),
            copies.make(sent.at[1], got.at[3], over),
        ]
        self.pair = copies.make(sent.at[2], got.at[4], pair)

    def block(self, index):
        count = self.got.shape[1]
        return self.part.at[index * count : (index + 1) * count]

    def begin(self):
        @pl.when(jnp.logical_not(self.inner))
        def _():
            for copy in self.inward:
                copy.start()
            self.sent[2] = self.block(1)[...]
            self.pair.start()

    def middle(self):
        @pl.when(self.inner)
        def _():
            self.inward[0].wait_recv()
            self.sent[0] = add_rounded(self.block(2)[...], self.got[0])
            self.over[0].start()

    def last(self):
        @pl.when(self.inner)
        def _():
            self.inward[1].wait_recv()
            self.sent[1] = add_rounded(self.block(3)[...], self.got[1])
            self.over[1].start()
            self.over[0].wait_recv()
            self.sent[2] = add_rounded(self.block(1)[...], self.got[2])
            self.pair.start()

    def end(self, out_ref):
        self.pair.wait_recv()
        out_ref[...] = self.block(0)[...].astype(F32) + self.got[4].astype(F32)

        @pl.when(self.inner)
        def _():
            self.over[1].wait_recv()
            out_ref[...] += self.got[3].astype(F32)
            for copy in self.over:
                copy.wait_send()

        @pl.when(jnp.logical_not(self.inner))
        def _():
            for copy in self.inward:
                copy.wait_send()

        self.pair.wait_send()


class PlaneShare:
    def __init__(self, copies, own, mine, out, local_sem):
        x, y = {"tensor": own ^ 1}, {"tensor": own ^ 2}
        self.local = pltpu.make_async_copy(mine, out.at[:, 0], local_sem)
        self.near = [
            copies.make(mine.at[0], out.at[0, 1], x),
            copies.make(mine.at[1], out.at[1, 2], y),
            copies.make(mine.at[1], out.at[1, 1], x),
            copies.make(mine.at[0], out.at[0, 2], y),
        ]
        self.diag = [
            copies.make(out.at[0, 1], out.at[0, 3], y),
            copies.make(out.at[1, 2], out.at[1, 3], x),
        ]

    def begin(self):
        for copy in self.near:
            copy.start()
        self.local.start()

    def middle(self):
        for i in range(2):
            self.near[i].wait_recv()
            self.diag[i].start()

    def end(self):
        for copy in (*self.near[2:], *self.diag):
            copy.wait_recv()
        for copy in (*self.near, *self.diag):
            copy.wait_send()
        self.local.wait()


def places():
    me, own = lax.axis_index("dp"), lax.axis_index("tensor")
    z = me // 2
    greet(
        (
            *({"tensor": own ^ 1}, {"tensor": own ^ 2}),
            *({"dp": me ^ 1}, {"dp": me ^ 2}, {"dp": me ^ 6}),
        )
    )
    return me, own, (z == 1) | (z == 2)


def middle_forward(
    part_ref,
    x_ref,
    gain_ref,
    buf_ref,
    resid_ref,
    rows_ref,
    bufs_ref,
    near,
    far_send,
    far,
    mine,
    local_sems,
    send_sems,
    recv_sems,
    line_send,
    line_recv,
):
    me, own, inner = places()
    copies = Copies(send_sems, recv_sems)
    line = ZLane(me, buf_ref, bufs_ref, line_send, line_recv)
    plane = PlaneSum(copies, own, part_ref, near, far_send, far)
    share = PlaneShare(copies, own, mine, rows_ref, local_sems.at[0])
    kept = pltpu.make_async_copy(buf_ref, bufs_ref.at[0], local_sems.at[1])
    plane.begin()
    line.begin(inner)
    kept.start()
    plane.middle()
    for i in range(2):
        resid = x_ref[i].astype(F32) + plane.arrive(i)
        resid_ref[i] = resid
        mine[i] = (unit_of(resid)[0] * gain_ref[...]).astype(BF16)
    share.begin()
    line.middle(inner)
    share.middle()
    line.last(inner)
    share.end()
    plane.end()
    kept.wait()
    line.end(inner)


def middle_backward(
    part_ref,
    g_ref,
    resid_ref,
    gain_ref,
    line_ref,
    out_ref,
    rows_ref,
    sum_ref,
    line_out,
    near,
    far_send,
    far,
    mine,
    line_sent,
    line_got,
    local_sems,
    send_sems,
    recv_sems,
):
    me, own, inner = places()
    copies = Copies(send_sems, recv_sems)
    line = LineSum(copies, me, inner, line_ref, line_sent, line_got)
    plane = PlaneSum(copies, own, part_ref, near, far_send, far)
    share = PlaneShare(copies, own, mine, rows_ref, local_sems.at[0])
    plane.begin()
    line.begin()
    plane.middle()
    line.middle()
    sum_ref[...] = jnp.zeros_like(sum_ref)
    for i in range(2):
        unit, recip = unit_of(resid_ref[i])
        upstream = plane.arrive(i)
        sum_ref[...] += jnp.sum(upstream * unit, axis=0, keepdims=True)
        total = g_ref[i].astype(F32) + norm_back(upstream, unit, recip, gain_ref[...])
        out_ref[i] = total
        mine[i] = total.astype(BF16)
    share.begin()
    line.last()
    share.middle()
    line.end(line_out)
    share.end()
    plane.end()


class Job:
    def __init__(self, gen, open_at):
        self.gen, self.open_at = gen, open_at
        self.rounds, self.flight, self.value, self.done = 0, (), None, False

    def step(self, results, anchor=()):
        try:
            sends = self.gen.send(results)
        except StopIteration as stop:
            self.value, self.done, self.flight = stop.value, True, ()
            return
        arrays = [array for array, _ in sends]
        if anchor:
            arrays = lax.optimization_barrier((*arrays, *anchor))[: len(arrays)]
        self.flight = tuple(
            lax.ppermute(array, "dp", perm) for array, (_, perm) in zip(arrays, sends)
        )
        self.rounds += 1

    @property
    def open(self):
        return self.done or self.rounds >= self.open_at


class Rounds:
    def __init__(self):
        self.live, self.queue = [], []

    def add(self, gen, open_at):
        job = Job(gen, open_at)
        self.queue.append(job)
        return job

    def pump(self, *values):
        flight = [array for job in self.live for array in job.flight]
        if flight:
            out = lax.optimization_barrier((*values, *flight))
            values, flight = out[: len(values)], list(out[len(values) :])
            for job in self.live:
                count = len(job.flight)
                results, flight = flight[:count], flight[count:]
                job.step(results)
            self.live = [job for job in self.live if not job.done]
        while self.queue and all(job.open for job in self.live):
            job = self.queue.pop(0)
            job.step(None, values[:1])
            if not job.done:
                self.live.append(job)
        return values

    def drain(self):
        while self.live or self.queue:
            self.pump()


class Steps:
    def __init__(self, gen):
        self.gen, self.pending, self.value = gen, (), None
        self.feed(None)

    def feed(self, results):
        try:
            self.pending = self.gen.send(results)
        except StopIteration as stop:
            self.value, self.pending = stop.value, ()


class Direct:
    def __init__(self, dp, tensor):
        self.dp, self.tensor = dp, tensor
        self.me = lax.axis_index("dp")
        self.own = lax.axis_index("tensor")
        self.rounds = Rounds()

    def mix(self, steps, *values):
        out = self.rounds.pump(*values, *steps.pending)
        if steps.pending:
            steps.feed(out[len(values) :])
        return out[: len(values)]

    def run(self, gen):
        steps = Steps(gen)
        while steps.pending:
            self.mix(steps)
        return steps.value

    def free(self, gen):
        steps = gen if isinstance(gen, Steps) else Steps(gen)
        while steps.pending:
            steps.feed(lax.optimization_barrier(steps.pending))
        return steps.value

    def to_local(self, rows):
        return rows

    def from_local(self, rows):
        return rows

    def row_order(self, value):
        return value

    def gains_local(self, blocks):
        return blocks.reshape(-1)

    def gains_plain(self, blocks):
        return blocks.reshape(-1)

    def plain_vector(self, vector):
        return vector

    def sum_all(self, vector):
        return lax.psum(vector, ("dp", "tensor"))

    def gather_weights(self, buf):
        return list(lax.all_gather(buf, "dp", axis=0))
        yield

    def first_gathers(self, rows, *weights):
        gathered = self.free(self.gather_rows(rows))
        return gathered, *(lax.all_gather(array, "dp", axis=0) for array in weights)

    def middle_forward(self, part, x_own, gain, buf):
        resid = x_own.astype(F32) + self.free(self.scatter_rows(part))
        rows = self.free(self.gather_rows((unit_of(resid)[0] * gain).astype(BF16)))
        return resid, rows, lax.all_gather(buf, "dp", axis=0)

    def middle_backward(self, part, g_own, resid, gain, line):
        unit, recip = unit_of(resid)
        upstream = self.free(self.scatter_rows(part))
        total = g_own.astype(F32) + norm_back(upstream, unit, recip, gain)
        rows = self.free(self.gather_rows(total.astype(BF16)))
        return total, rows, jnp.sum(upstream * unit, axis=(0, 1)), line

    def scatter_here(self, parts):
        job = Job(self.scatter_grads(parts), 0)
        job.step(None)
        return job.value

    def scatter_grads(self, parts):
        full = jnp.concatenate([dot_tn(l, r).astype(BF16) for l, r in parts], axis=1)
        return lax.psum_scatter(full, "dp", scatter_dimension=0, tiled=True).astype(F32)
        yield

    def gather_rows(self, rows):
        return lax.all_gather(rows, "tensor", axis=1, tiled=True)
        yield

    def scatter_rows(self, partial):
        return lax.psum_scatter(partial, "tensor", scatter_dimension=1, tiled=True).astype(F32)
        yield


class Links(Direct):
    def __init__(self, dp, tensor):
        super().__init__(dp, tensor)
        z = self.me // 2
        self.inner = (z == 1) | (z == 2)
        self.blocks = self.me ^ jnp.array(ORDER, jnp.int32)
        hit = (self.me ^ jnp.arange(8, dtype=jnp.int32))[:, None] == jnp.array(ORDER, jnp.int32)
        self.hit = hit
        self.places = jnp.sum(jnp.where(hit, jnp.arange(8, dtype=jnp.int32)[None, :], 0), axis=1)

    def to_local(self, rows):
        return block_move(self.blocks, rows)

    def from_local(self, rows):
        return block_move(self.places, rows)

    def row_order(self, value):
        parts = list(jnp.split(value, 4, axis=-1))
        for bit in (1, 2):
            swap = (self.own & bit) != 0
            parts = [jnp.where(swap, parts[j ^ bit], parts[j]) for j in range(4)]
        return jnp.concatenate(parts, axis=-1)

    def gains_plain(self, blocks):
        return jnp.sum(jnp.where(self.hit[:, :, None], blocks[None], 0), axis=1).reshape(-1)

    def plain_vector(self, vector):
        return self.gains_plain(vector.reshape(8, -1))

    def sum_all(self, vector):
        for axis, perm in (
            ("tensor", XNEXT),
            ("tensor", YNEXT),
            ("dp", CORE),
            ("dp", PAIR),
            ("dp", ACROSS),
        ):
            vector = vector + lax.ppermute(vector, axis, perm)
        return vector

    def gather_weights(self, buf):
        pair, over_own, other = yield [(buf, PAIR), (buf, INNER), (buf, CORE)]
        over_pair, out_own, other_pair = yield [(pair, INNER), (over_own, OUTWARD), (pair, CORE)]
        two = jnp.where(self.inner, over_pair, out_own)
        out_pair, other_two = yield [(over_pair, OUTWARD), (two, CORE)]
        three = jnp.where(self.inner, over_own, out_pair)
        other_three = lax.ppermute(three, "dp", CORE)
        return [buf, pair, two, three, other, other_pair, other_two, other_three]

    def first_gathers(self, rows, *weights):
        micro, count, width = rows.shape
        hbm = pl.BlockSpec(memory_space=pl.ANY)
        lanes = len(weights)
        return pl.pallas_call(
            first_gathers,
            out_shape=(
                jax.ShapeDtypeStruct((micro, 4, count, width), rows.dtype),
                *(jax.ShapeDtypeStruct((8,) + w.shape, w.dtype) for w in weights),
            ),
            in_specs=[hbm] * (1 + lanes),
            out_specs=[hbm] * (1 + lanes),
            scratch_shapes=[
                pltpu.SemaphoreType.DMA((copies,)) for copies in (5, 6, 6, *(9, 8) * lanes)
            ],
            compiler_params=pltpu.CompilerParams(collective_id=0, has_side_effects=True),
        )(rows, *weights)

    def middle_call(self, body, operands, outputs, places, line, line_sems, scratch, identity):
        micro, count, width = self.rows
        vmem, hbm = pl.BlockSpec(memory_space=pltpu.VMEM), pl.BlockSpec(memory_space=pl.ANY)
        return pl.pallas_call(
            body,
            out_shape=outputs,
            in_specs=[vmem] * (len(operands) - 1) + [line],
            out_specs=[hbm if place else vmem for place in places],
            scratch_shapes=[
                pltpu.VMEM((micro, 2, count, width), BF16),
                *[pltpu.VMEM(self.rows, BF16)] * 3,
                *scratch,
                *[pltpu.SemaphoreType.DMA((copies,)) for copies in line_sems],
            ],
            compiler_params=pltpu.CompilerParams(collective_id=identity, has_side_effects=True),
        )(*operands)

    def middle_forward(self, part, x_own, gain, buf):
        self.rows = micro, count, width = x_own.shape
        return self.middle_call(
            middle_forward,
            (part, x_own, gain.reshape(1, -1), buf),
            (
                jax.ShapeDtypeStruct(self.rows, F32),
                jax.ShapeDtypeStruct((micro, 4, count, width), BF16),
                jax.ShapeDtypeStruct((8,) + buf.shape, BF16),
            ),
            (False, True, True),
            pl.BlockSpec(memory_space=pl.ANY),
            (2, 12, 12, 9, 8),
            (),
            2,
        )

    def middle_backward(self, part, g_own, resid, gain, line):
        self.rows = micro, count, width = g_own.shape
        block = (line.shape[0] // 4, line.shape[1])
        total, rows, sums, grads = self.middle_call(
            middle_backward,
            (part, g_own, resid, gain.reshape(1, -1), line),
            (
                jax.ShapeDtypeStruct(self.rows, F32),
                jax.ShapeDtypeStruct((micro, 4, count, width), BF16),
                jax.ShapeDtypeStruct((1, width), F32),
                jax.ShapeDtypeStruct(block, F32),
            ),
            (False, True, False, False),
            pl.BlockSpec(memory_space=pltpu.VMEM),
            (1, 17, 17),
            (pltpu.VMEM((3,) + block, BF16), pltpu.VMEM((5,) + block, BF16)),
            3,
        )
        return total, rows, sums.reshape(-1), grads

    def scatter_here(self, parts):
        summed, half = [], parts[0][0].shape[1] // 2
        for left, right in parts:
            away = lax.ppermute(dot_tn(left[:, half:], right).astype(BF16), "dp", CORE)
            summed.append((dot_tn(left[:, :half], right) + away.astype(F32)).astype(BF16))
        return jnp.concatenate(summed, axis=1)

    def scatter_grads(self, parts):
        away, half = [], parts[0][0].shape[1] // 2
        for left, right in parts:
            away.append(dot_tn(left[:, half:], right).astype(BF16))
        summed = [
            (dot_tn(left[:, :half], right) + lax.ppermute(array, "dp", CORE).astype(F32)).astype(BF16)
            for (left, right), array in zip(parts, away)
        ]
        own, pair, two, three = jnp.split(jnp.concatenate(summed, axis=1), 4, axis=0)
        (got,) = yield [(three, INWARD)]
        two_sum = add_rounded(two, got)
        got, got_inner = yield [(two, INWARD), (two_sum, INNER)]
        three, pair = add_rounded(three, got), add_rounded(pair, got_inner)
        got_inner, got_pair = yield [(three, INNER), (pair, PAIR)]
        return own.astype(F32) + got_inner.astype(F32) + got_pair.astype(F32)

    def gather_rows(self, rows):
        near_x, near_y = yield (
            lax.ppermute(rows, "tensor", XNEXT),
            lax.ppermute(rows, "tensor", YNEXT),
        )
        diag_first, diag_second = yield (
            lax.ppermute(near_x[0], "tensor", YNEXT),
            lax.ppermute(near_y[1], "tensor", XNEXT),
        )
        return jnp.concatenate([rows, near_x, near_y, jnp.stack([diag_first, diag_second])], axis=1)

    def scatter_rows(self, partial):
        first, second = (jnp.split(partial[i], 4, axis=0) for i in range(2))
        near_first, near_second = yield (
            lax.ppermute(jnp.stack([first[1], first[3]]), "tensor", XNEXT),
            lax.ppermute(jnp.stack([second[2], second[3]]), "tensor", YNEXT),
        )
        far_first, far_second = yield (
            lax.ppermute(add_rounded(first[2], near_first[1]), "tensor", YNEXT),
            lax.ppermute(add_rounded(second[1], near_second[1]), "tensor", XNEXT),
        )
        return jnp.stack(
            [
                first[0].astype(F32) + near_first[0].astype(F32) + far_first.astype(F32),
                second[0].astype(F32) + near_second[0].astype(F32) + far_second.astype(F32),
            ]
        )


def unit_of(rows):
    recip = lax.rsqrt(jnp.mean(rows * rows, axis=-1, keepdims=True) + EPS)
    return rows * recip, recip


def norm_back(upstream, unit, recip, gain):
    scaled = upstream * gain
    return recip * (scaled - unit * jnp.mean(scaled * unit, axis=-1, keepdims=True))


def rotary(offsets):
    freqs = jnp.exp(
        jnp.arange(0, HEAD_SIZE, 2).astype(F32) * (-math.log(THETA) / HEAD_SIZE)
    )
    angles = offsets.astype(F32)[..., None] * freqs
    cosine, sine = jnp.cos(angles), jnp.sin(angles)
    return jnp.concatenate([cosine, cosine], -1), jnp.concatenate([-sine, sine], -1)


def on_device(
    net,
    hidden_in,
    cotangent,
    segment_ids,
    positions,
    pad_mask,
    attn_gain,
    w_query,
    key_weight,
    value_weight,
    query_norm_gain,
    key_gain,
    w_out,
    ffn_gain,
    w_gate,
    w_up,
    w_down,
):
    net = net()
    micro, own_rows, width = hidden_in.shape
    seq_len = segment_ids.shape[1]
    rows = micro * seq_len
    share = attn_gain.shape[0]
    head_share = query_norm_gain.shape[0]
    q_cols, kv_cols = w_query.shape[1], key_weight.shape[1]
    heads_q, heads_kv = q_cols // HEAD_SIZE, kv_cols // HEAD_SIZE
    units = w_gate.shape[1] // CHUNKS

    rounds = net.rounds
    x_own = net.to_local(hidden_in)
    packed = jnp.concatenate([attn_gain, ffn_gain, query_norm_gain, key_gain], axis=0)
    pad = -packed.shape[0] % 2048
    packed = jnp.pad(packed, (0, pad)).reshape(-1, 128)
    x_all, w_qkv, w_out_t, gains = net.first_gathers(
        x_own, jnp.concatenate([w_query, key_weight, value_weight], axis=1), w_out.T, packed
    )
    w_qkv = w_qkv.reshape(width, -1)
    w_out_t = w_out_t.reshape(width, -1)
    gains = gains.reshape(gains.shape[0], -1).astype(F32)
    x_bf = x_all.reshape(rows, width)
    later = (segment_ids, positions, pad_mask, cotangent, w_gate, w_up, w_down)
    x_bf, *later = lax.optimization_barrier((x_bf, *later))
    segment_ids, positions, pad_mask, cotangent, *ffn_weights = later
    w_gate, w_up, w_down = ffn_weights
    ffn_bufs = []
    for chunk in range(CHUNKS):
        cut = slice(chunk * units, (chunk + 1) * units)
        ffn_bufs.append(jnp.concatenate([w_gate[:, cut], w_up[:, cut], w_down[cut, :].T], axis=1))
    job_first = rounds.add(net.gather_weights(ffn_bufs[0]), 4)
    (x_bf,) = rounds.pump(x_bf)
    g_own, x_bf = lax.optimization_barrier((net.to_local(cotangent), x_bf))
    g_steps = Steps(net.gather_rows(g_own))
    gain_one = net.gains_local(gains[:, :share])
    gain_two = net.gains_local(gains[:, share : 2 * share])
    gain_q = net.gains_plain(gains[:, 2 * share : 2 * share + head_share])
    gain_k = net.gains_plain(gains[:, 2 * share + head_share : 2 * (share + head_share)])

    segment = net.row_order(segment_ids)
    offsets = net.row_order(positions)
    valid = net.row_order(pad_mask)
    row_ids = net.row_order(jnp.arange(seq_len, dtype=jnp.int32))
    cosine, sine = rotary(offsets.reshape(rows))
    ids = jnp.stack([segment, jnp.broadcast_to(row_ids, segment.shape), valid], axis=1)
    ids_col = jnp.stack([ids[:, i].reshape(rows) for i in range(3)], axis=1)
    tables = (cosine, sine, ids_col, ids, gain_q.reshape(1, -1), gain_k.reshape(1, -1))
    unit_all, _ = unit_of(x_bf.astype(F32))
    a1 = (unit_all * gain_one).astype(BF16)
    (qkv,) = net.mix(g_steps, dot_nn(a1, w_qkv))
    mixed_bf = attention_call(
        attention_forward,
        micro,
        heads_q,
        heads_kv,
        (qkv,),
        tables,
        jax.ShapeDtypeStruct((rows, q_cols), BF16),
        pl.BlockSpec((seq_len, q_cols), lambda i: (i, 0)),
        2,
    )
    (mixed_bf,) = net.mix(g_steps, mixed_bf)
    attn_part = dot_nt(mixed_bf, w_out_t).astype(BF16).reshape(micro, seq_len, width)
    resid, a2, w_second = net.middle_forward(attn_part, x_own, gain_two, ffn_bufs[1])
    (a2,) = rounds.pump(a2.reshape(rows, width))
    w_chunks = [jnp.concatenate(job_first.value, axis=0), w_second.reshape(width, -1)]
    g_all = net.free(g_steps).reshape(rows, width)

    da2, inners = None, []
    for chunk in range(CHUNKS):
        w_chunk = w_chunks[chunk]
        w_gu, w_down_t = w_chunk[:, : 2 * units], w_chunk[:, 2 * units :]
        gate_up = dot_nn(a2, w_gu)
        d_inner = dot_nn(g_all, w_down_t)
        (gate_up,) = rounds.pump(gate_up)
        gate, upper = gate_up[:, :units], gate_up[:, units:]
        sigma = jax.nn.sigmoid(gate)
        swish = gate * sigma
        inner = (swish * upper).astype(BF16)
        d_gate = (d_inner * upper * sigma * (1.0 + gate * (1.0 - sigma))).astype(BF16)
        d_upper = (d_inner * swish).astype(BF16)
        d_gu = jnp.concatenate([d_gate, d_upper], axis=1)
        inner, d_gu = rounds.pump(inner, d_gu)
        inners.append(inner)
        part_da2 = dot_nt(d_gu, w_gu)
        da2 = part_da2 if da2 is None else da2 + part_da2
        parts = [(a2, d_gu), (g_all, inner)]
        if chunk == 0:
            job_grad = rounds.add(net.scatter_grads(parts), 4)
    line = net.scatter_here(parts)
    mlp = sum(
        dot_nt(inner, w_chunk[:, 2 * units :]) for inner, w_chunk in zip(inners, w_chunks)
    )
    da2, mlp = rounds.pump(da2.astype(BF16), mlp.astype(BF16))
    d_resid, d_resid_all, acc_ffn_gain, grad_second = net.middle_backward(
        da2.reshape(micro, seq_len, width), g_own, resid, gain_two, line
    )
    (d_resid_all,) = rounds.pump(d_resid_all.reshape(rows, width))
    d_resid_all, mlp = lax.optimization_barrier((d_resid_all, mlp.astype(BF16)))
    mlp_steps = Steps(net.scatter_rows(mlp.reshape(micro, seq_len, width)))
    job_grad_out = rounds.add(net.scatter_grads([(d_resid_all, mixed_bf)]), 3)

    (d_mixed,) = net.mix(mlp_steps, dot_nn(d_resid_all, w_out_t).astype(BF16))
    d_qkv, head_sums = attention_call(
        attention_backward,
        micro,
        heads_q,
        heads_kv,
        (qkv, d_mixed),
        tables,
        (
            jax.ShapeDtypeStruct(qkv.shape, BF16),
            jax.ShapeDtypeStruct((micro, 2, HEAD_SIZE), F32),
        ),
        (
            pl.BlockSpec((seq_len, qkv.shape[1]), lambda i: (i, 0)),
            pl.BlockSpec((1, 2, HEAD_SIZE), lambda i: (i, 0, 0)),
        ),
        5,
    )
    acc_q_gain, acc_k_gain = jnp.sum(head_sums, axis=0)
    (d_qkv,) = net.mix(mlp_steps, d_qkv)
    layer_out = net.from_local((resid + net.free(mlp_steps)).astype(BF16))
    job_grad_qkv = rounds.add(net.scatter_grads([(a1, d_qkv)]), 4)
    (da1,) = rounds.pump(dot_nt(d_qkv, w_qkv))
    acc_attn_gain = jnp.sum(da1 * unit_all, axis=0)
    d_normed = net.run(net.scatter_rows(da1.astype(BF16).reshape(micro, seq_len, width)))
    unit_one, recip_one = unit_of(x_own.astype(F32))
    input_grad = net.from_local(
        (d_resid + norm_back(d_normed, unit_one, recip_one, gain_one)).astype(BF16)
    )

    sums = net.sum_all(
        jnp.concatenate(
            [
                net.plain_vector(acc_attn_gain),
                net.plain_vector(acc_ffn_gain),
                acc_q_gain,
                acc_k_gain,
            ]
        )
    )
    rounds.drain()
    grad_qkv = job_grad_qkv.value
    grads_ffn = [job_grad.value, grad_second]

    def own_part(start, size):
        return lax.dynamic_slice_in_dim(sums, start + net.me * size, size, 0)

    return (
        layer_out,
        input_grad,
        own_part(0, share),
        grad_qkv[:, :q_cols],
        grad_qkv[:, q_cols : q_cols + kv_cols],
        grad_qkv[:, q_cols + kv_cols :],
        own_part(2 * width, head_share),
        own_part(2 * width + HEAD_SIZE, head_share),
        job_grad_out.value.T,
        own_part(width, share),
        jnp.concatenate([g[:, :units] for g in grads_ffn], axis=1),
        jnp.concatenate([g[:, units : 2 * units] for g in grads_ffn], axis=1),
        jnp.concatenate([g[:, 2 * units :] for g in grads_ffn], axis=1).T,
    )


def solution(mesh):
    dp, tensor = mesh.shape["dp"], mesh.shape["tensor"]
    kind = Links if (dp, tensor) == (8, 4) else Direct
    weight, weight_t = P("dp", "tensor"), P("tensor", "dp")
    acts, ids = P(None, ("dp", "tensor"), None), P(None, "dp")
    gain = P("dp")

    def step(*args):
        return on_device(lambda: kind(dp, tensor), *args)

    return jax.shard_map(
        step,
        mesh=mesh,
        in_specs=(
            acts,
            acts,
            ids,
            ids,
            ids,
            gain,
            weight,
            weight,
            weight,
            gain,
            gain,
            weight_t,
            gain,
            weight,
            weight,
            weight_t,
        ),
        out_specs=(
            acts,
            acts,
            gain,
            weight,
            weight,
            weight,
            gain,
            gain,
            weight_t,
            gain,
            weight,
            weight,
            weight_t,
        ),
        check_vma=False,
    )
```

```python
import functools
import math

import jax
import jax.numpy as jnp
from jax import lax
from jax.experimental import pallas as pl
from jax.experimental.pallas import tpu as pltpu
from jax.sharding import PartitionSpec as P

HEAD_SIZE = 128
EPS = 1e-06
THETA = 1000000.0
CHUNKS = 3
F32 = jnp.float32
BF16 = jnp.bfloat16

ORDER = (0, 2, 4, 6, 1, 3, 5, 7)
PAIR = [(d, d ^ 2) for d in range(8)]
ACROSS = [(d, d ^ 4) for d in range(8)]
CORE = [(d, d ^ 1) for d in range(8)]
INNER = [(2, 4), (3, 5), (4, 2), (5, 3)]
OUTWARD = [(2, 0), (3, 1), (4, 6), (5, 7)]
INWARD = [(0, 2), (1, 3), (6, 4), (7, 5)]
XNEXT = [(t, t ^ 1) for t in range(4)]
YNEXT = [(t, t ^ 2) for t in range(4)]


def add_rounded(left, right):
    return (left.astype(F32) + right.astype(F32)).astype(BF16)


def dot_nn(left, right):
    return jnp.dot(left, right, preferred_element_type=F32)


def dot_nt(left, right):
    return lax.dot_general(left, right, (((1,), (1,)), ((), ())), preferred_element_type=F32)


def dot_tn(left, right):
    return lax.dot_general(left, right, (((0,), (0,)), ((), ())), preferred_element_type=F32)


def block_move(table, rows):
    micro, count, width = rows.shape
    blocks = table.shape[0]
    size = width // blocks

    def body(table_ref, in_ref, out_ref):
        for i in range(blocks):
            start = pl.multiple_of(table_ref[i] * size, size)
            out_ref[:, :, i * size : (i + 1) * size] = in_ref[:, :, pl.ds(start, size)]

    return pl.pallas_call(
        body,
        out_shape=jax.ShapeDtypeStruct(rows.shape, rows.dtype),
        grid_spec=pltpu.PrefetchScalarGridSpec(
            num_scalar_prefetch=1,
            grid=(micro,),
            in_specs=[pl.BlockSpec((1, count, width), lambda i, ref: (i, 0, 0))],
            out_specs=pl.BlockSpec((1, count, width), lambda i, ref: (i, 0, 0)),
        ),
        cost_estimate=pl.CostEstimate(
            flops=0, bytes_accessed=4 * micro * count * width, transcendentals=0
        ),
    )(table, rows)


def turn(rows, cosine, sine):
    return rows * cosine + pltpu.roll(rows, HEAD_SIZE // 2, 1) * sine


def allowed_bias(col_ref, row_ref):
    segment, row_id, valid = row_ref[0, 0:1, :], row_ref[0, 1:2, :], row_ref[0, 2:3, :]
    segment_col, row_id_col = col_ref[:, 0:1], col_ref[:, 1:2]
    allowed = (
        (segment_col == segment)
        & (row_id <= row_id_col)
        & ((valid > 0) | (row_id == row_id_col))
    )
    return jnp.where(allowed, 0.0, -1e30)


def head(index):
    return slice(index * HEAD_SIZE, (index + 1) * HEAD_SIZE)


def softmax_rows(query, key, bias):
    scores = dot_nt(query, key) * (1.0 / math.sqrt(HEAD_SIZE)) + bias
    shifted = jnp.exp(scores - jnp.max(scores, axis=-1, keepdims=True))
    return shifted * (1.0 / jnp.sum(shifted, axis=-1, keepdims=True))


def attention_forward(
    heads_q, heads_kv, qkv_ref, cos_ref, sin_ref, col_ref, row_ref, gain_q_ref, gain_k_ref, out_ref
):
    cosine, sine = cos_ref[...], sin_ref[...]
    bias = allowed_bias(col_ref, row_ref)
    valid = col_ref[:, 2:3].astype(F32)
    groups = heads_q // heads_kv
    for kv in range(heads_kv):
        k_unit, _ = unit_of(qkv_ref[:, head(heads_q + kv)])
        key = turn(k_unit * gain_k_ref[...], cosine, sine).astype(BF16)
        value = qkv_ref[:, head(heads_q + heads_kv + kv)].astype(BF16)
        for h in range(kv * groups, (kv + 1) * groups):
            q_unit, _ = unit_of(qkv_ref[:, head(h)])
            query = turn(q_unit * gain_q_ref[...], cosine, sine).astype(BF16)
            probs = softmax_rows(query, key, bias).astype(BF16)
            out_ref[:, head(h)] = (dot_nn(probs, value) * valid).astype(BF16)


def attention_backward(
    heads_q,
    heads_kv,
    qkv_ref,
    grad_ref,
    cos_ref,
    sin_ref,
    col_ref,
    row_ref,
    gain_q_ref,
    gain_k_ref,
    out_ref,
    sums_ref,
):
    cosine, sine = cos_ref[...], sin_ref[...]
    bias = allowed_bias(col_ref, row_ref)
    valid = col_ref[:, 2:3].astype(BF16)
    groups = heads_q // heads_kv
    scale = 1.0 / math.sqrt(HEAD_SIZE)
    gain_q, gain_k = gain_q_ref[...], gain_k_ref[...]
    sum_q = sum_k = jnp.zeros((1, HEAD_SIZE), F32)
    for kv in range(heads_kv):
        k_unit, k_recip = unit_of(qkv_ref[:, head(heads_q + kv)])
        key = turn(k_unit * gain_k, cosine, sine).astype(BF16)
        value = qkv_ref[:, head(heads_q + heads_kv + kv)].astype(BF16)
        d_key = d_value = None
        for h in range(kv * groups, (kv + 1) * groups):
            q_unit, q_recip = unit_of(qkv_ref[:, head(h)])
            query = turn(q_unit * gain_q, cosine, sine).astype(BF16)
            probs = softmax_rows(query, key, bias)
            d_mixed = grad_ref[:, head(h)] * valid
            d_probs = dot_nt(d_mixed, value)
            delta = jnp.sum(probs * d_probs, axis=-1, keepdims=True)
            d_scores = (probs * (d_probs - delta)).astype(BF16)
            d_query = turn(scale * dot_nn(d_scores, key), cosine, -sine)
            sum_q = sum_q + jnp.sum(d_query * q_unit, axis=0, keepdims=True)
            out_ref[:, head(h)] = norm_back(d_query, q_unit, q_recip, gain_q).astype(BF16)
            part_key, part_value = dot_tn(d_scores, query), dot_tn(probs.astype(BF16), d_mixed)
            d_key = part_key if d_key is None else d_key + part_key
            d_value = part_value if d_value is None else d_value + part_value
        d_key = turn(scale * d_key, cosine, -sine)
        sum_k = sum_k + jnp.sum(d_key * k_unit, axis=0, keepdims=True)
        out_ref[:, head(heads_q + kv)] = norm_back(d_key, k_unit, k_recip, gain_k).astype(BF16)
        out_ref[:, head(heads_q + heads_kv + kv)] = d_value.astype(BF16)
    sums_ref[0, 0:1, :] = sum_q
    sums_ref[0, 1:2, :] = sum_k


def attention_call(body, micro, heads_q, heads_kv, wide, tables, out_shape, out_specs, passes):
    seq_len = wide[0].shape[0] // micro

    def rows_of(array):
        return pl.BlockSpec((seq_len, array.shape[1]), lambda i: (i, 0))

    def whole(array):
        return pl.BlockSpec(array.shape, lambda i: (0, 0))

    cosine, sine, col, row, gain_q, gain_k = tables
    return pl.pallas_call(
        functools.partial(body, heads_q, heads_kv),
        out_shape=out_shape,
        grid=(micro,),
        in_specs=[rows_of(array) for array in (*wide, cosine, sine, col)]
        + [
            pl.BlockSpec((1,) + row.shape[1:], lambda i: (i, 0, 0)),
            whole(gain_q),
            whole(gain_k),
        ],
        out_specs=out_specs,
        cost_estimate=pl.CostEstimate(
            flops=2 * passes * micro * heads_q * seq_len * seq_len * HEAD_SIZE,
            bytes_accessed=sum(array.size * array.dtype.itemsize for array in wide) * 2,
            transcendentals=micro * heads_q * seq_len * seq_len,
        ),
    )(*wide, *tables)


class ZLane:
    def __init__(self, me, own, out, send_sems, recv_sems):
        self.me, self.own, self.out = me, own, out
        self.send_sems, self.recv_sems = send_sems, recv_sems

    def copy(self, index, source, slot, device):
        return pltpu.make_async_remote_copy(
            src_ref=source,
            dst_ref=self.out.at[slot],
            send_sem=self.send_sems.at[index],
            recv_sem=self.recv_sems.at[slot],
            device_id={"dp": device},
            device_id_type=pl.DeviceIdType.MESH,
        )

    def parts(self, slot):
        return self.own if slot == 0 else self.out.at[slot]

    def along(self, slot):
        index, to_slot, bits = {0: (1, 3, 6), 1: (2, 2, 6), 3: (3, 2, 2), 2: (4, 3, 2)}[slot]
        return self.copy(index, self.parts(slot), to_slot, self.me ^ bits)

    def across(self, slot):
        return self.copy(5 + slot, self.parts(slot), 4 + slot, self.me ^ 1)

    def pair(self):
        return self.copy(0, self.own, 1, self.me ^ 2)

    def arrived(self, slot):
        self.copy(0, self.own, slot, self.me ^ 2).wait_recv()

    def begin(self, inner):
        self.pair().start()

        @pl.when(inner)
        def _():
            self.along(0).start()

        self.across(0).start()

    def middle(self, inner):
        self.arrived(1)

        @pl.when(inner)
        def _():
            self.along(1).start()
            self.arrived(3)
            self.along(3).start()
            self.across(3).start()

        self.across(1).start()

    def last(self, inner):
        self.arrived(2)

        @pl.when(inner)
        def _():
            self.along(2).start()

        self.across(2).start()

        @pl.when(jnp.logical_not(inner))
        def _():
            self.arrived(3)
            self.across(3).start()

    def end(self, inner):
        self.pair().wait_send()
        for slot in range(4):
            self.across(slot).wait_send()
            self.arrived(4 + slot)

        @pl.when(inner)
        def _():
            for slot in range(4):
                self.along(slot).wait_send()


def first_gathers(
    x_ref, qkv_ref, out_ref, gain_ref, x_all, qkv_all, out_all, gain_all, local_sems, *sems
):
    me, own = lax.axis_index("dp"), lax.axis_index("tensor")
    z = me // 2
    inner = (z == 1) | (z == 2)
    barrier = pltpu.get_barrier_semaphore()
    peers = [{"dp": me ^ bits} for bits in (1, 2, 6)]
    peers += [{"tensor": own ^ bit} for bit in (1, 2)]
    for device in peers:
        pl.semaphore_signal(barrier, device_id=device, device_id_type=pl.DeviceIdType.MESH)
    pl.semaphore_wait(barrier, len(peers))

    x_send, x_recv, qkv_send, qkv_recv, out_send, out_recv, gain_send, gain_recv = sems
    local = [
        pltpu.make_async_copy(source, target, local_sems.at[i])
        for i, (source, target) in enumerate(
            (
                (x_ref.at[0], x_all.at[0, 0]),
                (x_ref.at[1], x_all.at[1, 0]),
                (qkv_ref, qkv_all.at[0]),
                (out_ref, out_all.at[0]),
                (gain_ref, gain_all.at[0]),
            )
        )
    ]

    def plane(index, source, part, slot, bit):
        return pltpu.make_async_remote_copy(
            src_ref=source,
            dst_ref=x_all.at[part, slot],
            send_sem=x_send.at[index],
            recv_sem=x_recv.at[index],
            device_id={"tensor": own ^ bit},
            device_id_type=pl.DeviceIdType.MESH,
        )

    qkv_lane = ZLane(me, qkv_ref, qkv_all, qkv_send, qkv_recv)
    out_lane = ZLane(me, out_ref, out_all, out_send, out_recv)
    gain_lane = ZLane(me, gain_ref, gain_all, gain_send, gain_recv)
    x_first = plane(0, x_ref.at[0], 0, 1, 1)
    y_second = plane(1, x_ref.at[1], 1, 2, 2)
    x_second = plane(2, x_ref.at[1], 1, 1, 1)
    y_first = plane(3, x_ref.at[0], 0, 2, 2)
    d_first = plane(4, x_all.at[0, 1], 0, 3, 2)
    d_second = plane(5, x_all.at[1, 2], 1, 3, 1)
    gain_lane.begin(inner)
    qkv_lane.begin(inner)
    for copy in (x_first, y_second, x_second, y_first):
        copy.start()
    for copy in local:
        copy.start()
    gain_lane.middle(inner)
    gain_lane.last(inner)
    x_first.wait_recv()
    d_first.start()
    y_second.wait_recv()
    d_second.start()
    qkv_lane.middle(inner)
    out_lane.begin(inner)
    qkv_lane.last(inner)
    out_lane.middle(inner)
    out_lane.last(inner)
    for copy in (x_second, y_first, d_first, d_second):
        copy.wait_recv()
    for copy in (x_first, y_second, x_second, y_first, d_first, d_second):
        copy.wait_send()
    for copy in local:
        copy.wait()
    gain_lane.end(inner)
    qkv_lane.end(inner)
    out_lane.end(inner)


class Copies:
    def __init__(self, send_sems, recv_sems):
        self.send_sems, self.recv_sems, self.count = send_sems, recv_sems, 0

    def make(self, source, target, device):
        index = self.count
        self.count += 1
        return pltpu.make_async_remote_copy(
            src_ref=source,
            dst_ref=target,
            send_sem=self.send_sems.at[index],
            recv_sem=self.recv_sems.at[index],
            device_id=device,
            device_id_type=pl.DeviceIdType.MESH,
        )


def greet(peers):
    barrier = pltpu.get_barrier_semaphore()
    for device in peers:
        pl.semaphore_signal(barrier, device_id=device, device_id_type=pl.DeviceIdType.MESH)
    pl.semaphore_wait(barrier, len(peers))


class PlaneSum:
    def __init__(self, copies, own, part_ref, near, far_send, far):
        x, y = {"tensor": own ^ 1}, {"tensor": own ^ 2}
        self.part, self.near, self.far_send, self.far_got = part_ref, near, far_send, far
        self.diag, self.direct, self.far = [], [], []
        for i, (device, other, block) in enumerate(((x, y, 1), (y, x, 2))):
            self.diag.append(copies.make(self.rows(i, 3), near.at[i, 1], device))
            self.direct.append(copies.make(self.rows(i, block), near.at[i, 0], device))
            self.far.append(copies.make(far_send.at[i], far.at[i], other))

    def rows(self, i, block):
        count = self.far_got.shape[1]
        return self.part.at[i, block * count : (block + 1) * count]

    def begin(self):
        for copy in (*self.diag, *self.direct):
            copy.start()

    def middle(self):
        for i in range(2):
            self.diag[i].wait_recv()
            self.far_send[i] = add_rounded(self.rows(i, 2 - i)[...], self.near[i, 1])
            self.far[i].start()

    def arrive(self, i):
        self.direct[i].wait_recv()
        self.far[i].wait_recv()
        return (
            self.rows(i, 0)[...].astype(F32)
            + self.near[i, 0].astype(F32)
            + self.far_got[i].astype(F32)
        )

    def end(self):
        for copy in (*self.diag, *self.direct, *self.far):
            copy.wait_send()


class LineSum:
    def __init__(self, copies, me, inner, in_ref, sent, got):
        self.inner, self.part, self.sent, self.got = inner, in_ref, sent, got
        pair, over = {"dp": me ^ 2}, {"dp": me ^ 6}
        self.inward = [
            copies.make(self.block(3), got.at[0], pair),
            copies.make(self.block(2), got.at[1], pair),
        ]
        self.over = [
            copies.make(sent.at[0], got.at[2], over),
            copies.make(sent.at[1], got.at[3], over),
        ]
        self.pair = copies.make(sent.at[2], got.at[4], pair)

    def block(self, index):
        count = self.got.shape[1]
        return self.part.at[index * count : (index + 1) * count]

    def begin(self):
        @pl.when(jnp.logical_not(self.inner))
        def _():
            for copy in self.inward:
                copy.start()
            self.sent[2] = self.block(1)[...]
            self.pair.start()

    def middle(self):
        @pl.when(self.inner)
        def _():
            self.inward[0].wait_recv()
            self.sent[0] = add_rounded(self.block(2)[...], self.got[0])
            self.over[0].start()

    def last(self):
        @pl.when(self.inner)
        def _():
            self.inward[1].wait_recv()
            self.sent[1] = add_rounded(self.block(3)[...], self.got[1])
            self.over[1].start()
            self.over[0].wait_recv()
            self.sent[2] = add_rounded(self.block(1)[...], self.got[2])
            self.pair.start()

    def end(self, out_ref):
        self.pair.wait_recv()
        out_ref[...] = self.block(0)[...].astype(F32) + self.got[4].astype(F32)

        @pl.when(self.inner)
        def _():
            self.over[1].wait_recv()
            out_ref[...] += self.got[3].astype(F32)
            for copy in self.over:
                copy.wait_send()

        @pl.when(jnp.logical_not(self.inner))
        def _():
            for copy in self.inward:
                copy.wait_send()

        self.pair.wait_send()


class PlaneShare:
    def __init__(self, copies, own, mine, out, local_sem):
        x, y = {"tensor": own ^ 1}, {"tensor": own ^ 2}
        self.local = pltpu.make_async_copy(mine, out.at[:, 0], local_sem)
        self.near = [
            copies.make(mine.at[0], out.at[0, 1], x),
            copies.make(mine.at[1], out.at[1, 2], y),
            copies.make(mine.at[1], out.at[1, 1], x),
            copies.make(mine.at[0], out.at[0, 2], y),
        ]
        self.diag = [
            copies.make(out.at[0, 1], out.at[0, 3], y),
            copies.make(out.at[1, 2], out.at[1, 3], x),
        ]

    def begin(self):
        for copy in self.near:
            copy.start()
        self.local.start()

    def middle(self):
        for i in range(2):
            self.near[i].wait_recv()
            self.diag[i].start()

    def end(self):
        for copy in (*self.near[2:], *self.diag):
            copy.wait_recv()
        for copy in (*self.near, *self.diag):
            copy.wait_send()
        self.local.wait()


def places():
    me, own = lax.axis_index("dp"), lax.axis_index("tensor")
    z = me // 2
    greet(
        (
            *({"tensor": own ^ 1}, {"tensor": own ^ 2}),
            *({"dp": me ^ 1}, {"dp": me ^ 2}, {"dp": me ^ 6}),
        )
    )
    return me, own, (z == 1) | (z == 2)


def middle_forward(
    part_ref,
    x_ref,
    gain_ref,
    buf_ref,
    resid_ref,
    rows_ref,
    bufs_ref,
    near,
    far_send,
    far,
    mine,
    local_sems,
    send_sems,
    recv_sems,
    line_send,
    line_recv,
):
    me, own, inner = places()
    copies = Copies(send_sems, recv_sems)
    line = ZLane(me, buf_ref, bufs_ref, line_send, line_recv)
    plane = PlaneSum(copies, own, part_ref, near, far_send, far)
    share = PlaneShare(copies, own, mine, rows_ref, local_sems.at[0])
    kept = pltpu.make_async_copy(buf_ref, bufs_ref.at[0], local_sems.at[1])
    plane.begin()
    line.begin(inner)
    kept.start()
    plane.middle()
    for i in range(2):
        resid = x_ref[i].astype(F32) + plane.arrive(i)
        resid_ref[i] = resid
        mine[i] = (unit_of(resid)[0] * gain_ref[...]).astype(BF16)
    share.begin()
    line.middle(inner)
    share.middle()
    line.last(inner)
    share.end()
    plane.end()
    kept.wait()
    line.end(inner)


def middle_backward(
    part_ref,
    g_ref,
    resid_ref,
    gain_ref,
    line_ref,
    out_ref,
    rows_ref,
    sum_ref,
    line_out,
    near,
    far_send,
    far,
    mine,
    line_sent,
    line_got,
    local_sems,
    send_sems,
    recv_sems,
):
    me, own, inner = places()
    copies = Copies(send_sems, recv_sems)
    line = LineSum(copies, me, inner, line_ref, line_sent, line_got)
    plane = PlaneSum(copies, own, part_ref, near, far_send, far)
    share = PlaneShare(copies, own, mine, rows_ref, local_sems.at[0])
    plane.begin()
    line.begin()
    plane.middle()
    line.middle()
    sum_ref[...] = jnp.zeros_like(sum_ref)
    for i in range(2):
        unit, recip = unit_of(resid_ref[i])
        upstream = plane.arrive(i)
        sum_ref[...] += jnp.sum(upstream * unit, axis=0, keepdims=True)
        total = g_ref[i].astype(F32) + norm_back(upstream, unit, recip, gain_ref[...])
        out_ref[i] = total
        mine[i] = total.astype(BF16)
    share.begin()
    line.last()
    share.middle()
    line.end(line_out)
    share.end()
    plane.end()


class Job:
    def __init__(self, gen, open_at):
        self.gen, self.open_at = gen, open_at
        self.rounds, self.flight, self.value, self.done = 0, (), None, False

    def step(self, results, anchor=()):
        try:
            sends = self.gen.send(results)
        except StopIteration as stop:
            self.value, self.done, self.flight = stop.value, True, ()
            return
        arrays = [array for array, _ in sends]
        if anchor:
            arrays = lax.optimization_barrier((*arrays, *anchor))[: len(arrays)]
        self.flight = tuple(
            lax.ppermute(array, "dp", perm) for array, (_, perm) in zip(arrays, sends)
        )
        self.rounds += 1

    @property
    def open(self):
        return self.done or self.rounds >= self.open_at


class Rounds:
    def __init__(self):
        self.live, self.queue = [], []

    def add(self, gen, open_at):
        job = Job(gen, open_at)
        self.queue.append(job)
        return job

    def pump(self, *values):
        flight = [array for job in self.live for array in job.flight]
        if flight:
            out = lax.optimization_barrier((*values, *flight))
            values, flight = out[: len(values)], list(out[len(values) :])
            for job in self.live:
                count = len(job.flight)
                results, flight = flight[:count], flight[count:]
                job.step(results)
            self.live = [job for job in self.live if not job.done]
        while self.queue and all(job.open for job in self.live):
            job = self.queue.pop(0)
            job.step(None, values[:1])
            if not job.done:
                self.live.append(job)
        return values

    def drain(self):
        while self.live or self.queue:
            self.pump()


class Steps:
    def __init__(self, gen):
        self.gen, self.pending, self.value = gen, (), None
        self.feed(None)

    def feed(self, results):
        try:
            self.pending = self.gen.send(results)
        except StopIteration as stop:
            self.value, self.pending = stop.value, ()


class Direct:
    def __init__(self, dp, tensor):
        self.dp, self.tensor = dp, tensor
        self.me = lax.axis_index("dp")
        self.own = lax.axis_index("tensor")
        self.rounds = Rounds()

    def mix(self, steps, *values):
        out = self.rounds.pump(*values, *steps.pending)
        if steps.pending:
            steps.feed(out[len(values) :])
        return out[: len(values)]

    def run(self, gen):
        steps = Steps(gen)
        while steps.pending:
            self.mix(steps)
        return steps.value

    def free(self, gen):
        steps = gen if isinstance(gen, Steps) else Steps(gen)
        while steps.pending:
            steps.feed(lax.optimization_barrier(steps.pending))
        return steps.value

    def to_local(self, rows):
        return rows

    def from_local(self, rows):
        return rows

    def row_order(self, value):
        return value

    def gains_local(self, blocks):
        return blocks.reshape(-1)

    def gains_plain(self, blocks):
        return blocks.reshape(-1)

    def plain_vector(self, vector):
        return vector

    def sum_all(self, vector):
        return lax.psum(vector, ("dp", "tensor"))

    def gather_weights(self, buf):
        return list(lax.all_gather(buf, "dp", axis=0))
        yield

    def first_gathers(self, rows, *weights):
        gathered = self.free(self.gather_rows(rows))
        return gathered, *(lax.all_gather(array, "dp", axis=0) for array in weights)

    def middle_forward(self, part, x_own, gain, buf):
        resid = x_own.astype(F32) + self.free(self.scatter_rows(part))
        rows = self.free(self.gather_rows((unit_of(resid)[0] * gain).astype(BF16)))
        return resid, rows, lax.all_gather(buf, "dp", axis=0)

    def middle_backward(self, part, g_own, resid, gain, line):
        unit, recip = unit_of(resid)
        upstream = self.free(self.scatter_rows(part))
        total = g_own.astype(F32) + norm_back(upstream, unit, recip, gain)
        rows = self.free(self.gather_rows(total.astype(BF16)))
        return total, rows, jnp.sum(upstream * unit, axis=(0, 1)), line

    def scatter_line(self, summed):
        return summed
        yield

    def scatter_here(self, parts):
        job = Job(self.scatter_grads(parts), 0)
        job.step(None)
        return job.value

    def scatter_grads(self, parts):
        full = jnp.concatenate([dot_tn(l, r).astype(BF16) for l, r in parts], axis=1)
        return lax.psum_scatter(full, "dp", scatter_dimension=0, tiled=True).astype(F32)
        yield

    def gather_rows(self, rows):
        return lax.all_gather(rows, "tensor", axis=1, tiled=True)
        yield

    def scatter_rows(self, partial):
        return lax.psum_scatter(partial, "tensor", scatter_dimension=1, tiled=True).astype(F32)
        yield


class Links(Direct):
    def __init__(self, dp, tensor):
        super().__init__(dp, tensor)
        z = self.me // 2
        self.inner = (z == 1) | (z == 2)
        self.blocks = self.me ^ jnp.array(ORDER, jnp.int32)
        hit = (self.me ^ jnp.arange(8, dtype=jnp.int32))[:, None] == jnp.array(ORDER, jnp.int32)
        self.hit = hit
        self.places = jnp.sum(jnp.where(hit, jnp.arange(8, dtype=jnp.int32)[None, :], 0), axis=1)

    def to_local(self, rows):
        return block_move(self.blocks, rows)

    def from_local(self, rows):
        return block_move(self.places, rows)

    def row_order(self, value):
        parts = list(jnp.split(value, 4, axis=-1))
        for bit in (1, 2):
            swap = (self.own & bit) != 0
            parts = [jnp.where(swap, parts[j ^ bit], parts[j]) for j in range(4)]
        return jnp.concatenate(parts, axis=-1)

    def gains_plain(self, blocks):
        return jnp.sum(jnp.where(self.hit[:, :, None], blocks[None], 0), axis=1).reshape(-1)

    def plain_vector(self, vector):
        return self.gains_plain(vector.reshape(8, -1))

    def sum_all(self, vector):
        for axis, perm in (
            ("tensor", XNEXT),
            ("tensor", YNEXT),
            ("dp", CORE),
            ("dp", PAIR),
            ("dp", ACROSS),
        ):
            vector = vector + lax.ppermute(vector, axis, perm)
        return vector

    def gather_weights(self, buf):
        pair, over_own, other = yield [(buf, PAIR), (buf, INNER), (buf, CORE)]
        over_pair, out_own, other_pair = yield [(pair, INNER), (over_own, OUTWARD), (pair, CORE)]
        two = jnp.where(self.inner, over_pair, out_own)
        out_pair, other_two = yield [(over_pair, OUTWARD), (two, CORE)]
        three = jnp.where(self.inner, over_own, out_pair)
        other_three = lax.ppermute(three, "dp", CORE)
        return [buf, pair, two, three, other, other_pair, other_two, other_three]

    def first_gathers(self, rows, *weights):
        micro, count, width = rows.shape
        hbm = pl.BlockSpec(memory_space=pl.ANY)
        lanes = len(weights)
        return pl.pallas_call(
            first_gathers,
            out_shape=(
                jax.ShapeDtypeStruct((micro, 4, count, width), rows.dtype),
                *(jax.ShapeDtypeStruct((8,) + w.shape, w.dtype) for w in weights),
            ),
            in_specs=[hbm] * (1 + lanes),
            out_specs=[hbm] * (1 + lanes),
            scratch_shapes=[
                pltpu.SemaphoreType.DMA((copies,)) for copies in (5, 6, 6, *(9, 8) * lanes)
            ],
            compiler_params=pltpu.CompilerParams(collective_id=0, has_side_effects=True),
        )(rows, *weights)

    def middle_call(self, body, operands, outputs, places, line, line_sems, scratch, identity):
        micro, count, width = self.rows
        vmem, hbm = pl.BlockSpec(memory_space=pltpu.VMEM), pl.BlockSpec(memory_space=pl.ANY)
        return pl.pallas_call(
            body,
            out_shape=outputs,
            in_specs=[vmem] * (len(operands) - 1) + [line],
            out_specs=[hbm if place else vmem for place in places],
            scratch_shapes=[
                pltpu.VMEM((micro, 2, count, width), BF16),
                *[pltpu.VMEM(self.rows, BF16)] * 3,
                *scratch,
                *[pltpu.SemaphoreType.DMA((copies,)) for copies in line_sems],
            ],
            compiler_params=pltpu.CompilerParams(collective_id=identity, has_side_effects=True),
        )(*operands)

    def middle_forward(self, part, x_own, gain, buf):
        self.rows = micro, count, width = x_own.shape
        return self.middle_call(
            middle_forward,
            (part, x_own, gain.reshape(1, -1), buf),
            (
                jax.ShapeDtypeStruct(self.rows, F32),
                jax.ShapeDtypeStruct((micro, 4, count, width), BF16),
                jax.ShapeDtypeStruct((8,) + buf.shape, BF16),
            ),
            (False, True, True),
            pl.BlockSpec(memory_space=pl.ANY),
            (2, 12, 12, 9, 8),
            (),
            2,
        )

    def middle_backward(self, part, g_own, resid, gain, line):
        self.rows = micro, count, width = g_own.shape
        block = (line.shape[0] // 4, line.shape[1])
        total, rows, sums, grads = self.middle_call(
            middle_backward,
            (part, g_own, resid, gain.reshape(1, -1), line),
            (
                jax.ShapeDtypeStruct(self.rows, F32),
                jax.ShapeDtypeStruct((micro, 4, count, width), BF16),
                jax.ShapeDtypeStruct((1, width), F32),
                jax.ShapeDtypeStruct(block, F32),
            ),
            (False, True, False, False),
            pl.BlockSpec(memory_space=pltpu.VMEM),
            (1, 17, 17),
            (pltpu.VMEM((3,) + block, BF16), pltpu.VMEM((5,) + block, BF16)),
            3,
        )
        return total, rows, sums.reshape(-1), grads

    def scatter_here(self, parts):
        summed, half = [], parts[0][0].shape[1] // 2
        for left, right in parts:
            away = lax.ppermute(dot_tn(left[:, half:], right).astype(BF16), "dp", CORE)
            summed.append((dot_tn(left[:, :half], right) + away.astype(F32)).astype(BF16))
        return jnp.concatenate(summed, axis=1)

    def scatter_grads(self, parts):
        return self.scatter_line(self.scatter_here(parts))

    def scatter_line(self, summed):
        own, pair, two, three = jnp.split(summed, 4, axis=0)
        (got,) = yield [(three, INWARD)]
        two_sum = add_rounded(two, got)
        got, got_inner = yield [(two, INWARD), (two_sum, INNER)]
        three, pair = add_rounded(three, got), add_rounded(pair, got_inner)
        got_inner, got_pair = yield [(three, INNER), (pair, PAIR)]
        return own.astype(F32) + got_inner.astype(F32) + got_pair.astype(F32)

    def gather_rows(self, rows):
        near_x, near_y = yield (
            lax.ppermute(rows, "tensor", XNEXT),
            lax.ppermute(rows, "tensor", YNEXT),
        )
        diag_first, diag_second = yield (
            lax.ppermute(near_x[0], "tensor", YNEXT),
            lax.ppermute(near_y[1], "tensor", XNEXT),
        )
        return jnp.concatenate([rows, near_x, near_y, jnp.stack([diag_first, diag_second])], axis=1)

    def scatter_rows(self, partial):
        first, second = (jnp.split(partial[i], 4, axis=0) for i in range(2))
        near_first, near_second = yield (
            lax.ppermute(jnp.stack([first[1], first[3]]), "tensor", XNEXT),
            lax.ppermute(jnp.stack([second[2], second[3]]), "tensor", YNEXT),
        )
        far_first, far_second = yield (
            lax.ppermute(add_rounded(first[2], near_first[1]), "tensor", YNEXT),
            lax.ppermute(add_rounded(second[1], near_second[1]), "tensor", XNEXT),
        )
        return jnp.stack(
            [
                first[0].astype(F32) + near_first[0].astype(F32) + far_first.astype(F32),
                second[0].astype(F32) + near_second[0].astype(F32) + far_second.astype(F32),
            ]
        )


def unit_of(rows):
    recip = lax.rsqrt(jnp.mean(rows * rows, axis=-1, keepdims=True) + EPS)
    return rows * recip, recip


def norm_back(upstream, unit, recip, gain):
    scaled = upstream * gain
    return recip * (scaled - unit * jnp.mean(scaled * unit, axis=-1, keepdims=True))


def rotary(offsets):
    freqs = jnp.exp(
        jnp.arange(0, HEAD_SIZE, 2).astype(F32) * (-math.log(THETA) / HEAD_SIZE)
    )
    angles = offsets.astype(F32)[..., None] * freqs
    cosine, sine = jnp.cos(angles), jnp.sin(angles)
    return jnp.concatenate([cosine, cosine], -1), jnp.concatenate([-sine, sine], -1)


def on_device(
    net,
    hidden_in,
    cotangent,
    segment_ids,
    positions,
    pad_mask,
    attn_gain,
    w_query,
    key_weight,
    value_weight,
    query_norm_gain,
    key_gain,
    w_out,
    ffn_gain,
    w_gate,
    w_up,
    w_down,
):
    net = net()
    micro, own_rows, width = hidden_in.shape
    seq_len = segment_ids.shape[1]
    rows = micro * seq_len
    share = attn_gain.shape[0]
    head_share = query_norm_gain.shape[0]
    q_cols, kv_cols = w_query.shape[1], key_weight.shape[1]
    heads_q, heads_kv = q_cols // HEAD_SIZE, kv_cols // HEAD_SIZE
    units = w_gate.shape[1] // CHUNKS

    rounds = net.rounds
    x_own = net.to_local(hidden_in)
    packed = jnp.concatenate([attn_gain, ffn_gain, query_norm_gain, key_gain], axis=0)
    pad = -packed.shape[0] % 2048
    packed = jnp.pad(packed, (0, pad)).reshape(-1, 128)
    x_all, w_qkv, w_out_t, gains = net.first_gathers(
        x_own, jnp.concatenate([w_query, key_weight, value_weight], axis=1), w_out.T, packed
    )
    w_qkv = w_qkv.reshape(width, -1)
    w_out_t = w_out_t.reshape(width, -1)
    gains = gains.reshape(gains.shape[0], -1).astype(F32)
    x_bf = x_all.reshape(rows, width)
    later = (segment_ids, positions, pad_mask, cotangent, w_gate, w_up, w_down)
    x_bf, *later = lax.optimization_barrier((x_bf, *later))
    segment_ids, positions, pad_mask, cotangent, *ffn_weights = later
    w_gate, w_up, w_down = ffn_weights
    ffn_bufs = []
    for chunk in range(CHUNKS):
        cut = slice(chunk * units, (chunk + 1) * units)
        ffn_bufs.append(jnp.concatenate([w_gate[:, cut], w_up[:, cut], w_down[cut, :].T], axis=1))
    job_first = rounds.add(net.gather_weights(ffn_bufs[0]), 4)
    (x_bf,) = rounds.pump(x_bf)
    g_own, x_bf = lax.optimization_barrier((net.to_local(cotangent), x_bf))
    g_steps = Steps(net.gather_rows(g_own))
    gain_one = net.gains_local(gains[:, :share])
    gain_two = net.gains_local(gains[:, share : 2 * share])
    gain_q = net.gains_plain(gains[:, 2 * share : 2 * share + head_share])
    gain_k = net.gains_plain(gains[:, 2 * share + head_share : 2 * (share + head_share)])

    segment = net.row_order(segment_ids)
    offsets = net.row_order(positions)
    valid = net.row_order(pad_mask)
    row_ids = net.row_order(jnp.arange(seq_len, dtype=jnp.int32))
    cosine, sine = rotary(offsets.reshape(rows))
    ids = jnp.stack([segment, jnp.broadcast_to(row_ids, segment.shape), valid], axis=1)
    ids_col = jnp.stack([ids[:, i].reshape(rows) for i in range(3)], axis=1)
    tables = (cosine, sine, ids_col, ids, gain_q.reshape(1, -1), gain_k.reshape(1, -1))
    unit_all, _ = unit_of(x_bf.astype(F32))
    a1 = (unit_all * gain_one).astype(BF16)
    (qkv,) = net.mix(g_steps, dot_nn(a1, w_qkv))
    mixed_bf = attention_call(
        attention_forward,
        micro,
        heads_q,
        heads_kv,
        (qkv,),
        tables,
        jax.ShapeDtypeStruct((rows, q_cols), BF16),
        pl.BlockSpec((seq_len, q_cols), lambda i: (i, 0)),
        2,
    )
    (mixed_bf,) = net.mix(g_steps, mixed_bf)
    attn_part = dot_nt(mixed_bf, w_out_t).astype(BF16).reshape(micro, seq_len, width)
    resid, a2, w_second = net.middle_forward(attn_part, x_own, gain_two, ffn_bufs[1])
    job_third = rounds.add(net.gather_weights(ffn_bufs[2]), 4)
    (a2,) = rounds.pump(a2.reshape(rows, width))
    w_chunks = [jnp.concatenate(job_first.value, axis=0), w_second.reshape(width, -1)]
    g_all = net.free(g_steps).reshape(rows, width)

    da2, inners, grad_jobs = None, [], []
    for chunk in range(CHUNKS):
        if chunk == 2:
            w_chunks.append(jnp.concatenate(job_third.value, axis=0))
        w_chunk = w_chunks[chunk]
        w_gu, w_down_t = w_chunk[:, : 2 * units], w_chunk[:, 2 * units :]
        gate_up = dot_nn(a2, w_gu)
        d_inner = dot_nn(g_all, w_down_t)
        (gate_up,) = rounds.pump(gate_up)
        gate, upper = gate_up[:, :units], gate_up[:, units:]
        sigma = jax.nn.sigmoid(gate)
        swish = gate * sigma
        inner = (swish * upper).astype(BF16)
        d_gate = (d_inner * upper * sigma * (1.0 + gate * (1.0 - sigma))).astype(BF16)
        d_upper = (d_inner * swish).astype(BF16)
        d_gu = jnp.concatenate([d_gate, d_upper], axis=1)
        inner, d_gu = rounds.pump(inner, d_gu)
        inners.append(inner)
        part_da2 = dot_nt(d_gu, w_gu)
        da2 = part_da2 if da2 is None else da2 + part_da2
        parts = [(a2, d_gu), (g_all, inner)]
        if chunk < 2:
            grad_jobs.append(rounds.add(net.scatter_grads(parts), 4))
    line = net.scatter_here(parts)
    mlp = sum(
        dot_nt(inner, w_chunk[:, 2 * units :]) for inner, w_chunk in zip(inners, w_chunks)
    )
    da2, mlp = rounds.pump(da2.astype(BF16), mlp.astype(BF16))
    d_resid, d_resid_all, acc_ffn_gain, grad_third = net.middle_backward(
        da2.reshape(micro, seq_len, width), g_own, resid, gain_two, line
    )
    (d_resid_all,) = rounds.pump(d_resid_all.reshape(rows, width))
    d_resid_all, mlp = lax.optimization_barrier((d_resid_all, mlp.astype(BF16)))
    mlp_steps = Steps(net.scatter_rows(mlp.reshape(micro, seq_len, width)))
    line_out = net.scatter_here([(d_resid_all, mixed_bf)])
    job_grad_out = rounds.add(net.scatter_line(line_out), 3)

    d_mixed = dot_nn(d_resid_all, w_out_t).astype(BF16)
    d_mixed, _ = lax.optimization_barrier((d_mixed, line_out))
    (d_mixed,) = net.mix(mlp_steps, d_mixed)
    d_qkv, head_sums = attention_call(
        attention_backward,
        micro,
        heads_q,
        heads_kv,
        (qkv, d_mixed),
        tables,
        (
            jax.ShapeDtypeStruct(qkv.shape, BF16),
            jax.ShapeDtypeStruct((micro, 2, HEAD_SIZE), F32),
        ),
        (
            pl.BlockSpec((seq_len, qkv.shape[1]), lambda i: (i, 0)),
            pl.BlockSpec((1, 2, HEAD_SIZE), lambda i: (i, 0, 0)),
        ),
        5,
    )
    acc_q_gain, acc_k_gain = jnp.sum(head_sums, axis=0)
    (d_qkv,) = net.mix(mlp_steps, d_qkv)
    layer_out = net.from_local((resid + net.free(mlp_steps)).astype(BF16))
    line_qkv = net.scatter_here([(a1, d_qkv)])
    job_grad_qkv = rounds.add(net.scatter_line(line_qkv), 3)
    da1, _ = lax.optimization_barrier((dot_nt(d_qkv, w_qkv), line_qkv))
    (da1,) = rounds.pump(da1)
    acc_attn_gain = jnp.sum(da1 * unit_all, axis=0)
    d_normed = net.run(net.scatter_rows(da1.astype(BF16).reshape(micro, seq_len, width)))
    unit_one, recip_one = unit_of(x_own.astype(F32))
    input_grad = net.from_local(
        (d_resid + norm_back(d_normed, unit_one, recip_one, gain_one)).astype(BF16)
    )

    sums = net.sum_all(
        jnp.concatenate(
            [
                net.plain_vector(acc_attn_gain),
                net.plain_vector(acc_ffn_gain),
                acc_q_gain,
                acc_k_gain,
            ]
        )
    )
    rounds.drain()
    grad_qkv = job_grad_qkv.value
    grads_ffn = [*(job.value for job in grad_jobs), grad_third]

    def own_part(start, size):
        return lax.dynamic_slice_in_dim(sums, start + net.me * size, size, 0)

    return (
        layer_out,
        input_grad,
        own_part(0, share),
        grad_qkv[:, :q_cols],
        grad_qkv[:, q_cols : q_cols + kv_cols],
        grad_qkv[:, q_cols + kv_cols :],
        own_part(2 * width, head_share),
        own_part(2 * width + HEAD_SIZE, head_share),
        job_grad_out.value.T,
        own_part(width, share),
        jnp.concatenate([g[:, :units] for g in grads_ffn], axis=1),
        jnp.concatenate([g[:, units : 2 * units] for g in grads_ffn], axis=1),
        jnp.concatenate([g[:, 2 * units :] for g in grads_ffn], axis=1).T,
    )


def solution(mesh):
    dp, tensor = mesh.shape["dp"], mesh.shape["tensor"]
    kind = Links if (dp, tensor) == (8, 4) else Direct
    weight, weight_t = P("dp", "tensor"), P("tensor", "dp")
    acts, ids = P(None, ("dp", "tensor"), None), P(None, "dp")
    gain = P("dp")

    def step(*args):
        return on_device(lambda: kind(dp, tensor), *args)

    return jax.shard_map(
        step,
        mesh=mesh,
        in_specs=(
            acts,
            acts,
            ids,
            ids,
            ids,
            gain,
            weight,
            weight,
            weight,
            gain,
            gain,
            weight_t,
            gain,
            weight,
            weight,
            weight_t,
        ),
        out_specs=(
            acts,
            acts,
            gain,
            weight,
            weight,
            weight,
            gain,
            gain,
            weight_t,
            gain,
            weight,
            weight,
            weight_t,
        ),
        check_vma=False,
    )
```

```python
import functools
import math

import jax
import jax.numpy as jnp
from jax import lax
from jax.experimental import pallas as pl
from jax.experimental.pallas import tpu as pltpu
from jax.sharding import PartitionSpec as P

HEAD_SIZE = 128
EPS = 1e-06
THETA = 1000000.0
CHUNKS = 2
F32 = jnp.float32
BF16 = jnp.bfloat16

ORDER = (0, 2, 4, 6, 1, 3, 5, 7)
PAIR = [(d, d ^ 2) for d in range(8)]
ACROSS = [(d, d ^ 4) for d in range(8)]
CORE = [(d, d ^ 1) for d in range(8)]
INNER = [(2, 4), (3, 5), (4, 2), (5, 3)]
OUTWARD = [(2, 0), (3, 1), (4, 6), (5, 7)]
INWARD = [(0, 2), (1, 3), (6, 4), (7, 5)]
XNEXT = [(t, t ^ 1) for t in range(4)]
YNEXT = [(t, t ^ 2) for t in range(4)]


def add_rounded(left, right):
    return (left.astype(F32) + right.astype(F32)).astype(BF16)


def dot_nn(left, right):
    return jnp.dot(left, right, preferred_element_type=F32)


def dot_nt(left, right):
    return lax.dot_general(left, right, (((1,), (1,)), ((), ())), preferred_element_type=F32)


def dot_tn(left, right):
    return lax.dot_general(left, right, (((0,), (0,)), ((), ())), preferred_element_type=F32)


def block_move(table, rows):
    micro, count, width = rows.shape
    blocks = table.shape[0]
    size = width // blocks

    def body(table_ref, in_ref, out_ref):
        for i in range(blocks):
            start = pl.multiple_of(table_ref[i] * size, size)
            out_ref[:, :, i * size : (i + 1) * size] = in_ref[:, :, pl.ds(start, size)]

    return pl.pallas_call(
        body,
        out_shape=jax.ShapeDtypeStruct(rows.shape, rows.dtype),
        grid_spec=pltpu.PrefetchScalarGridSpec(
            num_scalar_prefetch=1,
            grid=(micro,),
            in_specs=[pl.BlockSpec((1, count, width), lambda i, ref: (i, 0, 0))],
            out_specs=pl.BlockSpec((1, count, width), lambda i, ref: (i, 0, 0)),
        ),
        cost_estimate=pl.CostEstimate(
            flops=0, bytes_accessed=4 * micro * count * width, transcendentals=0
        ),
    )(table, rows)


def turn(rows, cosine, sine):
    return rows * cosine + pltpu.roll(rows, HEAD_SIZE // 2, 1) * sine


def allowed_bias(col_ref, row_ref):
    segment, row_id, valid = row_ref[0, 0:1, :], row_ref[0, 1:2, :], row_ref[0, 2:3, :]
    segment_col, row_id_col = col_ref[:, 0:1], col_ref[:, 1:2]
    allowed = (
        (segment_col == segment)
        & (row_id <= row_id_col)
        & ((valid > 0) | (row_id == row_id_col))
    )
    return jnp.where(allowed, 0.0, -1e30)


def head(index):
    return slice(index * HEAD_SIZE, (index + 1) * HEAD_SIZE)


def softmax_rows(query, key, bias):
    scores = dot_nt(query, key) * (1.0 / math.sqrt(HEAD_SIZE)) + bias
    shifted = jnp.exp(scores - jnp.max(scores, axis=-1, keepdims=True))
    return shifted * (1.0 / jnp.sum(shifted, axis=-1, keepdims=True))


def attention_forward(
    heads_q, heads_kv, qkv_ref, cos_ref, sin_ref, col_ref, row_ref, gain_q_ref, gain_k_ref, out_ref
):
    cosine, sine = cos_ref[...], sin_ref[...]
    bias = allowed_bias(col_ref, row_ref)
    valid = col_ref[:, 2:3].astype(F32)
    groups = heads_q // heads_kv
    for kv in range(heads_kv):
        k_unit, _ = unit_of(qkv_ref[:, head(heads_q + kv)])
        key = turn(k_unit * gain_k_ref[...], cosine, sine).astype(BF16)
        value = qkv_ref[:, head(heads_q + heads_kv + kv)].astype(BF16)
        for h in range(kv * groups, (kv + 1) * groups):
            q_unit, _ = unit_of(qkv_ref[:, head(h)])
            query = turn(q_unit * gain_q_ref[...], cosine, sine).astype(BF16)
            probs = softmax_rows(query, key, bias).astype(BF16)
            out_ref[:, head(h)] = (dot_nn(probs, value) * valid).astype(BF16)


def attention_backward(
    heads_q,
    heads_kv,
    qkv_ref,
    grad_ref,
    cos_ref,
    sin_ref,
    col_ref,
    row_ref,
    gain_q_ref,
    gain_k_ref,
    out_ref,
    sums_ref,
):
    cosine, sine = cos_ref[...], sin_ref[...]
    bias = allowed_bias(col_ref, row_ref)
    valid = col_ref[:, 2:3].astype(BF16)
    groups = heads_q // heads_kv
    scale = 1.0 / math.sqrt(HEAD_SIZE)
    gain_q, gain_k = gain_q_ref[...], gain_k_ref[...]
    sum_q = sum_k = jnp.zeros((1, HEAD_SIZE), F32)
    for kv in range(heads_kv):
        k_unit, k_recip = unit_of(qkv_ref[:, head(heads_q + kv)])
        key = turn(k_unit * gain_k, cosine, sine).astype(BF16)
        value = qkv_ref[:, head(heads_q + heads_kv + kv)].astype(BF16)
        d_key = d_value = None
        for h in range(kv * groups, (kv + 1) * groups):
            q_unit, q_recip = unit_of(qkv_ref[:, head(h)])
            query = turn(q_unit * gain_q, cosine, sine).astype(BF16)
            probs = softmax_rows(query, key, bias)
            d_mixed = grad_ref[:, head(h)] * valid
            d_probs = dot_nt(d_mixed, value)
            delta = jnp.sum(probs * d_probs, axis=-1, keepdims=True)
            d_scores = (probs * (d_probs - delta)).astype(BF16)
            d_query = turn(scale * dot_nn(d_scores, key), cosine, -sine)
            sum_q = sum_q + jnp.sum(d_query * q_unit, axis=0, keepdims=True)
            out_ref[:, head(h)] = norm_back(d_query, q_unit, q_recip, gain_q).astype(BF16)
            part_key, part_value = dot_tn(d_scores, query), dot_tn(probs.astype(BF16), d_mixed)
            d_key = part_key if d_key is None else d_key + part_key
            d_value = part_value if d_value is None else d_value + part_value
        d_key = turn(scale * d_key, cosine, -sine)
        sum_k = sum_k + jnp.sum(d_key * k_unit, axis=0, keepdims=True)
        out_ref[:, head(heads_q + kv)] = norm_back(d_key, k_unit, k_recip, gain_k).astype(BF16)
        out_ref[:, head(heads_q + heads_kv + kv)] = d_value.astype(BF16)
    sums_ref[0, 0:1, :] = sum_q
    sums_ref[0, 1:2, :] = sum_k


def attention_call(
    body, micro, heads_q, heads_kv, wide, tables, out_shape, out_specs, passes, first=0
):
    seq_len = tables[3].shape[2]

    def rows_of(array):
        return pl.BlockSpec((seq_len, array.shape[1]), lambda i: (i + first, 0))

    def whole(array):
        return pl.BlockSpec(array.shape, lambda i: (0, 0))

    cosine, sine, col, row, gain_q, gain_k = tables
    return pl.pallas_call(
        functools.partial(body, heads_q, heads_kv),
        out_shape=out_shape,
        grid=(micro,),
        in_specs=[rows_of(array) for array in (*wide, cosine, sine, col)]
        + [
            pl.BlockSpec((1,) + row.shape[1:], lambda i: (i + first, 0, 0)),
            whole(gain_q),
            whole(gain_k),
        ],
        out_specs=out_specs,
        cost_estimate=pl.CostEstimate(
            flops=2 * passes * micro * heads_q * seq_len * seq_len * HEAD_SIZE,
            bytes_accessed=sum(array.size * array.dtype.itemsize for array in wide) * 2,
            transcendentals=micro * heads_q * seq_len * seq_len,
        ),
    )(*wide, *tables)


class ZLane:
    def __init__(self, me, own, out, send_sems, recv_sems):
        self.me, self.own, self.out = me, own, out
        self.send_sems, self.recv_sems = send_sems, recv_sems

    def copy(self, index, source, slot, device):
        return pltpu.make_async_remote_copy(
            src_ref=source,
            dst_ref=self.out.at[slot],
            send_sem=self.send_sems.at[index],
            recv_sem=self.recv_sems.at[slot],
            device_id={"dp": device},
            device_id_type=pl.DeviceIdType.MESH,
        )

    def parts(self, slot):
        return self.own if slot == 0 else self.out.at[slot]

    def along(self, slot):
        index, to_slot, bits = {0: (1, 3, 6), 1: (2, 2, 6), 3: (3, 2, 2), 2: (4, 3, 2)}[slot]
        return self.copy(index, self.parts(slot), to_slot, self.me ^ bits)

    def across(self, slot):
        return self.copy(5 + slot, self.parts(slot), 4 + slot, self.me ^ 1)

    def pair(self):
        return self.copy(0, self.own, 1, self.me ^ 2)

    def arrived(self, slot):
        self.copy(0, self.own, slot, self.me ^ 2).wait_recv()

    def begin(self, inner):
        self.pair().start()

        @pl.when(inner)
        def _():
            self.along(0).start()

        self.across(0).start()

    def middle(self, inner):
        self.arrived(1)

        @pl.when(inner)
        def _():
            self.along(1).start()
            self.arrived(3)
            self.along(3).start()
            self.across(3).start()

        self.across(1).start()

    def last(self, inner):
        self.arrived(2)

        @pl.when(inner)
        def _():
            self.along(2).start()

        self.across(2).start()

        @pl.when(jnp.logical_not(inner))
        def _():
            self.arrived(3)
            self.across(3).start()

    def end(self, inner):
        self.pair().wait_send()
        for slot in range(4):
            self.across(slot).wait_send()
            self.arrived(4 + slot)

        @pl.when(inner)
        def _():
            for slot in range(4):
                self.along(slot).wait_send()


def first_gathers(
    x_ref, qkv_ref, out_ref, gain_ref, x_all, qkv_all, out_all, gain_all, local_sems, *sems
):
    me, own = lax.axis_index("dp"), lax.axis_index("tensor")
    z = me // 2
    inner = (z == 1) | (z == 2)
    barrier = pltpu.get_barrier_semaphore()
    peers = [{"dp": me ^ bits} for bits in (1, 2, 6)]
    peers += [{"tensor": own ^ bit} for bit in (1, 2)]
    for device in peers:
        pl.semaphore_signal(barrier, device_id=device, device_id_type=pl.DeviceIdType.MESH)
    pl.semaphore_wait(barrier, len(peers))

    x_send, x_recv, qkv_send, qkv_recv, out_send, out_recv, gain_send, gain_recv = sems
    local = [
        pltpu.make_async_copy(source, target, local_sems.at[i])
        for i, (source, target) in enumerate(
            (
                (x_ref.at[0], x_all.at[0, 0]),
                (x_ref.at[1], x_all.at[1, 0]),
                (qkv_ref, qkv_all.at[0]),
                (out_ref, out_all.at[0]),
                (gain_ref, gain_all.at[0]),
            )
        )
    ]

    def plane(index, source, part, slot, bit):
        return pltpu.make_async_remote_copy(
            src_ref=source,
            dst_ref=x_all.at[part, slot],
            send_sem=x_send.at[index],
            recv_sem=x_recv.at[index],
            device_id={"tensor": own ^ bit},
            device_id_type=pl.DeviceIdType.MESH,
        )

    qkv_lane = ZLane(me, qkv_ref, qkv_all, qkv_send, qkv_recv)
    out_lane = ZLane(me, out_ref, out_all, out_send, out_recv)
    gain_lane = ZLane(me, gain_ref, gain_all, gain_send, gain_recv)
    x_first = plane(0, x_ref.at[0], 0, 1, 1)
    y_second = plane(1, x_ref.at[1], 1, 2, 2)
    x_second = plane(2, x_ref.at[1], 1, 1, 1)
    y_first = plane(3, x_ref.at[0], 0, 2, 2)
    d_first = plane(4, x_all.at[0, 1], 0, 3, 2)
    d_second = plane(5, x_all.at[1, 2], 1, 3, 1)
    gain_lane.begin(inner)
    qkv_lane.begin(inner)
    for copy in (x_first, y_second, x_second, y_first):
        copy.start()
    for copy in local:
        copy.start()
    gain_lane.middle(inner)
    gain_lane.last(inner)
    x_first.wait_recv()
    d_first.start()
    y_second.wait_recv()
    d_second.start()
    qkv_lane.middle(inner)
    out_lane.begin(inner)
    qkv_lane.last(inner)
    out_lane.middle(inner)
    out_lane.last(inner)
    for copy in (x_second, y_first, d_first, d_second):
        copy.wait_recv()
    for copy in (x_first, y_second, x_second, y_first, d_first, d_second):
        copy.wait_send()
    for copy in local:
        copy.wait()
    gain_lane.end(inner)
    qkv_lane.end(inner)
    out_lane.end(inner)


class Copies:
    def __init__(self, send_sems, recv_sems):
        self.send_sems, self.recv_sems, self.count = send_sems, recv_sems, 0

    def make(self, source, target, device):
        index = self.count
        self.count += 1
        return pltpu.make_async_remote_copy(
            src_ref=source,
            dst_ref=target,
            send_sem=self.send_sems.at[index],
            recv_sem=self.recv_sems.at[index],
            device_id=device,
            device_id_type=pl.DeviceIdType.MESH,
        )


def greet(peers):
    barrier = pltpu.get_barrier_semaphore()
    for device in peers:
        pl.semaphore_signal(barrier, device_id=device, device_id_type=pl.DeviceIdType.MESH)
    pl.semaphore_wait(barrier, len(peers))


class PlaneSum:
    def __init__(self, copies, own, part_ref, near, far_send, far):
        x, y = {"tensor": own ^ 1}, {"tensor": own ^ 2}
        self.part, self.near, self.far_send, self.far_got = part_ref, near, far_send, far
        self.diag, self.direct, self.far = [], [], []
        for i, (device, other, block) in enumerate(((x, y, 1), (y, x, 2))):
            self.diag.append(copies.make(self.rows(i, 3), near.at[i, 1], device))
            self.direct.append(copies.make(self.rows(i, block), near.at[i, 0], device))
            self.far.append(copies.make(far_send.at[i], far.at[i], other))

    def rows(self, i, block):
        count = self.far_got.shape[1]
        return self.part.at[i, block * count : (block + 1) * count]

    def begin(self):
        for copy in (*self.diag, *self.direct):
            copy.start()

    def middle(self):
        for i in range(2):
            self.diag[i].wait_recv()
            self.far_send[i] = add_rounded(self.rows(i, 2 - i)[...], self.near[i, 1])
            self.far[i].start()

    def arrive(self, i):
        self.direct[i].wait_recv()
        self.far[i].wait_recv()
        return (
            self.rows(i, 0)[...].astype(F32)
            + self.near[i, 0].astype(F32)
            + self.far_got[i].astype(F32)
        )

    def end(self):
        for copy in (*self.diag, *self.direct, *self.far):
            copy.wait_send()


class LineSum:
    def __init__(self, copies, me, inner, in_ref, sent, got):
        self.inner, self.part, self.sent, self.got = inner, in_ref, sent, got
        pair, over = {"dp": me ^ 2}, {"dp": me ^ 6}
        self.inward = [
            copies.make(self.block(3), got.at[0], pair),
            copies.make(self.block(2), got.at[1], pair),
        ]
        self.over = [
            copies.make(sent.at[0], got.at[2], over),
            copies.make(sent.at[1], got.at[3], over),
        ]
        self.pair = copies.make(sent.at[2], got.at[4], pair)

    def block(self, index):
        count = self.got.shape[1]
        return self.part.at[index * count : (index + 1) * count]

    def begin(self):
        @pl.when(jnp.logical_not(self.inner))
        def _():
            for copy in self.inward:
                copy.start()
            self.sent[2] = self.block(1)[...]
            self.pair.start()

    def middle(self):
        @pl.when(self.inner)
        def _():
            self.inward[0].wait_recv()
            self.sent[0] = add_rounded(self.block(2)[...], self.got[0])
            self.over[0].start()

    def last(self):
        @pl.when(self.inner)
        def _():
            self.inward[1].wait_recv()
            self.sent[1] = add_rounded(self.block(3)[...], self.got[1])
            self.over[1].start()
            self.over[0].wait_recv()
            self.sent[2] = add_rounded(self.block(1)[...], self.got[2])
            self.pair.start()

    def end(self, out_ref):
        self.pair.wait_recv()
        out_ref[...] = self.block(0)[...].astype(F32) + self.got[4].astype(F32)

        @pl.when(self.inner)
        def _():
            self.over[1].wait_recv()
            out_ref[...] += self.got[3].astype(F32)
            for copy in self.over:
                copy.wait_send()

        @pl.when(jnp.logical_not(self.inner))
        def _():
            for copy in self.inward:
                copy.wait_send()

        self.pair.wait_send()


class PlaneShare:
    def __init__(self, copies, own, mine, out, local_sem):
        x, y = {"tensor": own ^ 1}, {"tensor": own ^ 2}
        self.local = pltpu.make_async_copy(mine, out.at[:, 0], local_sem)
        self.near = [
            copies.make(mine.at[0], out.at[0, 1], x),
            copies.make(mine.at[1], out.at[1, 2], y),
            copies.make(mine.at[1], out.at[1, 1], x),
            copies.make(mine.at[0], out.at[0, 2], y),
        ]
        self.diag = [
            copies.make(out.at[0, 1], out.at[0, 3], y),
            copies.make(out.at[1, 2], out.at[1, 3], x),
        ]

    def begin(self):
        for copy in self.near:
            copy.start()
        self.local.start()

    def middle(self):
        for i in range(2):
            self.near[i].wait_recv()
            self.diag[i].start()

    def end(self):
        for copy in (*self.near[2:], *self.diag):
            copy.wait_recv()
        for copy in (*self.near, *self.diag):
            copy.wait_send()
        self.local.wait()


def places():
    me, own = lax.axis_index("dp"), lax.axis_index("tensor")
    z = me // 2
    greet(
        (
            *({"tensor": own ^ 1}, {"tensor": own ^ 2}),
            *({"dp": me ^ 1}, {"dp": me ^ 2}, {"dp": me ^ 6}),
        )
    )
    return me, own, (z == 1) | (z == 2)


def middle_forward(
    part_ref,
    x_ref,
    gain_ref,
    buf_ref,
    resid_ref,
    rows_ref,
    bufs_ref,
    near,
    far_send,
    far,
    mine,
    local_sems,
    send_sems,
    recv_sems,
    line_send,
    line_recv,
):
    me, own, inner = places()
    copies = Copies(send_sems, recv_sems)
    line = ZLane(me, buf_ref, bufs_ref, line_send, line_recv)
    plane = PlaneSum(copies, own, part_ref, near, far_send, far)
    share = PlaneShare(copies, own, mine, rows_ref, local_sems.at[0])
    kept = pltpu.make_async_copy(buf_ref, bufs_ref.at[0], local_sems.at[1])
    plane.begin()
    line.begin(inner)
    kept.start()
    plane.middle()
    for i in range(2):
        resid = x_ref[i].astype(F32) + plane.arrive(i)
        resid_ref[i] = resid
        mine[i] = (unit_of(resid)[0] * gain_ref[...]).astype(BF16)
    share.begin()
    line.middle(inner)
    share.middle()
    line.last(inner)
    share.end()
    plane.end()
    kept.wait()
    line.end(inner)


def middle_backward(
    part_ref,
    g_ref,
    resid_ref,
    gain_ref,
    line_ref,
    out_ref,
    rows_ref,
    sum_ref,
    line_out,
    near,
    far_send,
    far,
    mine,
    line_sent,
    line_got,
    local_sems,
    send_sems,
    recv_sems,
):
    me, own, inner = places()
    copies = Copies(send_sems, recv_sems)
    line = LineSum(copies, me, inner, line_ref, line_sent, line_got)
    plane = PlaneSum(copies, own, part_ref, near, far_send, far)
    share = PlaneShare(copies, own, mine, rows_ref, local_sems.at[0])
    plane.begin()
    line.begin()
    plane.middle()
    line.middle()
    sum_ref[...] = jnp.zeros_like(sum_ref)
    for i in range(2):
        unit, recip = unit_of(resid_ref[i])
        upstream = plane.arrive(i)
        sum_ref[...] += jnp.sum(upstream * unit, axis=0, keepdims=True)
        total = g_ref[i].astype(F32) + norm_back(upstream, unit, recip, gain_ref[...])
        out_ref[i] = total
        mine[i] = total.astype(BF16)
    share.begin()
    line.last()
    share.middle()
    line.end(line_out)
    share.end()
    plane.end()


class Job:
    def __init__(self, gen, open_at):
        self.gen, self.open_at = gen, open_at
        self.rounds, self.flight, self.value, self.done = 0, (), None, False

    def step(self, results, anchor=()):
        try:
            sends = self.gen.send(results)
        except StopIteration as stop:
            self.value, self.done, self.flight = stop.value, True, ()
            return
        arrays = [array for array, _ in sends]
        if anchor:
            arrays = lax.optimization_barrier((*arrays, *anchor))[: len(arrays)]
        self.flight = tuple(
            lax.ppermute(array, "dp", perm) for array, (_, perm) in zip(arrays, sends)
        )
        self.rounds += 1

    @property
    def open(self):
        return self.done or self.rounds >= self.open_at


class Rounds:
    def __init__(self):
        self.live, self.queue = [], []

    def add(self, gen, open_at):
        job = Job(gen, open_at)
        self.queue.append(job)
        return job

    def pump(self, *values):
        flight = [array for job in self.live for array in job.flight]
        if flight:
            out = lax.optimization_barrier((*values, *flight))
            values, flight = out[: len(values)], list(out[len(values) :])
            for job in self.live:
                count = len(job.flight)
                results, flight = flight[:count], flight[count:]
                job.step(results)
            self.live = [job for job in self.live if not job.done]
        while self.queue and all(job.open for job in self.live):
            job = self.queue.pop(0)
            job.step(None, values[:1])
            if not job.done:
                self.live.append(job)
        return values

    def drain(self):
        while self.live or self.queue:
            self.pump()


class Steps:
    def __init__(self, gen):
        self.gen, self.pending, self.value = gen, (), None
        self.feed(None)

    def feed(self, results):
        try:
            self.pending = self.gen.send(results)
        except StopIteration as stop:
            self.value, self.pending = stop.value, ()


class Direct:
    def __init__(self, dp, tensor):
        self.dp, self.tensor = dp, tensor
        self.me = lax.axis_index("dp")
        self.own = lax.axis_index("tensor")
        self.rounds = Rounds()

    def mix(self, steps, *values):
        out = self.rounds.pump(*values, *steps.pending)
        if steps.pending:
            steps.feed(out[len(values) :])
        return out[: len(values)]

    def run(self, gen):
        steps = Steps(gen)
        while steps.pending:
            self.mix(steps)
        return steps.value

    def free(self, gen):
        steps = gen if isinstance(gen, Steps) else Steps(gen)
        while steps.pending:
            steps.feed(lax.optimization_barrier(steps.pending))
        return steps.value

    def to_local(self, rows):
        return rows

    def from_local(self, rows):
        return rows

    def row_order(self, value):
        return value

    def gains_local(self, blocks):
        return blocks.reshape(-1)

    def gains_plain(self, blocks):
        return blocks.reshape(-1)

    def plain_vector(self, vector):
        return vector

    def sum_all(self, vector):
        return lax.psum(vector, ("dp", "tensor"))

    def gather_weights(self, buf):
        return list(lax.all_gather(buf, "dp", axis=0))
        yield

    def first_gathers(self, rows, *weights):
        gathered = self.free(self.gather_rows(rows))
        return gathered, *(lax.all_gather(array, "dp", axis=0) for array in weights)

    def middle_forward(self, part, x_own, gain, buf):
        resid = x_own.astype(F32) + self.free(self.scatter_rows(part))
        rows = self.free(self.gather_rows((unit_of(resid)[0] * gain).astype(BF16)))
        return resid, rows, lax.all_gather(buf, "dp", axis=0)

    def middle_backward(self, part, g_own, resid, gain, line):
        unit, recip = unit_of(resid)
        upstream = self.free(self.scatter_rows(part))
        total = g_own.astype(F32) + norm_back(upstream, unit, recip, gain)
        rows = self.free(self.gather_rows(total.astype(BF16)))
        return total, rows, jnp.sum(upstream * unit, axis=(0, 1)), line

    def scatter_line(self, summed):
        return summed
        yield

    def scatter_here(self, parts):
        job = Job(self.scatter_grads(parts), 0)
        job.step(None)
        return job.value

    def scatter_grads(self, parts):
        full = jnp.concatenate([dot_tn(l, r).astype(BF16) for l, r in parts], axis=1)
        return lax.psum_scatter(full, "dp", scatter_dimension=0, tiled=True).astype(F32)
        yield

    def gather_rows(self, rows):
        return lax.all_gather(rows, "tensor", axis=1, tiled=True)
        yield

    def scatter_rows(self, partial):
        return lax.psum_scatter(partial, "tensor", scatter_dimension=1, tiled=True).astype(F32)
        yield


class Links(Direct):
    def __init__(self, dp, tensor):
        super().__init__(dp, tensor)
        z = self.me // 2
        self.inner = (z == 1) | (z == 2)
        self.blocks = self.me ^ jnp.array(ORDER, jnp.int32)
        hit = (self.me ^ jnp.arange(8, dtype=jnp.int32))[:, None] == jnp.array(ORDER, jnp.int32)
        self.hit = hit
        self.places = jnp.sum(jnp.where(hit, jnp.arange(8, dtype=jnp.int32)[None, :], 0), axis=1)

    def to_local(self, rows):
        return block_move(self.blocks, rows)

    def from_local(self, rows):
        return block_move(self.places, rows)

    def row_order(self, value):
        parts = list(jnp.split(value, 4, axis=-1))
        for bit in (1, 2):
            swap = (self.own & bit) != 0
            parts = [jnp.where(swap, parts[j ^ bit], parts[j]) for j in range(4)]
        return jnp.concatenate(parts, axis=-1)

    def gains_plain(self, blocks):
        return jnp.sum(jnp.where(self.hit[:, :, None], blocks[None], 0), axis=1).reshape(-1)

    def plain_vector(self, vector):
        return self.gains_plain(vector.reshape(8, -1))

    def sum_all(self, vector):
        for axis, perm in (
            ("tensor", XNEXT),
            ("tensor", YNEXT),
            ("dp", CORE),
            ("dp", PAIR),
            ("dp", ACROSS),
        ):
            vector = vector + lax.ppermute(vector, axis, perm)
        return vector

    def gather_weights(self, buf):
        pair, over_own, other = yield [(buf, PAIR), (buf, INNER), (buf, CORE)]
        over_pair, out_own, other_pair = yield [(pair, INNER), (over_own, OUTWARD), (pair, CORE)]
        two = jnp.where(self.inner, over_pair, out_own)
        out_pair, other_two = yield [(over_pair, OUTWARD), (two, CORE)]
        three = jnp.where(self.inner, over_own, out_pair)
        other_three = lax.ppermute(three, "dp", CORE)
        return [buf, pair, two, three, other, other_pair, other_two, other_three]

    def first_gathers(self, rows, *weights):
        micro, count, width = rows.shape
        hbm = pl.BlockSpec(memory_space=pl.ANY)
        lanes = len(weights)
        return pl.pallas_call(
            first_gathers,
            out_shape=(
                jax.ShapeDtypeStruct((micro, 4, count, width), rows.dtype),
                *(jax.ShapeDtypeStruct((8,) + w.shape, w.dtype) for w in weights),
            ),
            in_specs=[hbm] * (1 + lanes),
            out_specs=[hbm] * (1 + lanes),
            scratch_shapes=[
                pltpu.SemaphoreType.DMA((copies,)) for copies in (5, 6, 6, *(9, 8) * lanes)
            ],
            compiler_params=pltpu.CompilerParams(collective_id=0, has_side_effects=True),
        )(rows, *weights)

    def middle_call(self, body, operands, outputs, places, line, line_sems, scratch, identity):
        micro, count, width = self.rows
        vmem, hbm = pl.BlockSpec(memory_space=pltpu.VMEM), pl.BlockSpec(memory_space=pl.ANY)
        return pl.pallas_call(
            body,
            out_shape=outputs,
            in_specs=[vmem] * (len(operands) - 1) + [line],
            out_specs=[hbm if place else vmem for place in places],
            scratch_shapes=[
                pltpu.VMEM((micro, 2, count, width), BF16),
                *[pltpu.VMEM(self.rows, BF16)] * 3,
                *scratch,
                *[pltpu.SemaphoreType.DMA((copies,)) for copies in line_sems],
            ],
            compiler_params=pltpu.CompilerParams(collective_id=identity, has_side_effects=True),
        )(*operands)

    def middle_forward(self, part, x_own, gain, buf):
        self.rows = micro, count, width = x_own.shape
        return self.middle_call(
            middle_forward,
            (part, x_own, gain.reshape(1, -1), buf),
            (
                jax.ShapeDtypeStruct(self.rows, F32),
                jax.ShapeDtypeStruct((micro, 4, count, width), BF16),
                jax.ShapeDtypeStruct((8,) + buf.shape, BF16),
            ),
            (False, True, True),
            pl.BlockSpec(memory_space=pl.ANY),
            (2, 12, 12, 9, 8),
            (),
            2,
        )

    def middle_backward(self, part, g_own, resid, gain, line):
        self.rows = micro, count, width = g_own.shape
        block = (line.shape[0] // 4, line.shape[1])
        total, rows, sums, grads = self.middle_call(
            middle_backward,
            (part, g_own, resid, gain.reshape(1, -1), line),
            (
                jax.ShapeDtypeStruct(self.rows, F32),
                jax.ShapeDtypeStruct((micro, 4, count, width), BF16),
                jax.ShapeDtypeStruct((1, width), F32),
                jax.ShapeDtypeStruct(block, F32),
            ),
            (False, True, False, False),
            pl.BlockSpec(memory_space=pltpu.VMEM),
            (1, 17, 17),
            (pltpu.VMEM((3,) + block, BF16), pltpu.VMEM((5,) + block, BF16)),
            3,
        )
        return total, rows, sums.reshape(-1), grads

    def scatter_here(self, parts):
        summed, half = [], parts[0][0].shape[1] // 2
        for left, right in parts:
            away = lax.ppermute(dot_tn(left[:, half:], right).astype(BF16), "dp", CORE)
            summed.append((dot_tn(left[:, :half], right) + away.astype(F32)).astype(BF16))
        return jnp.concatenate(summed, axis=1)

    def scatter_grads(self, parts):
        return self.scatter_line(self.scatter_here(parts))

    def scatter_line(self, summed):
        own, pair, two, three = jnp.split(summed, 4, axis=0)
        (got,) = yield [(three, INWARD)]
        two_sum = add_rounded(two, got)
        got, got_inner = yield [(two, INWARD), (two_sum, INNER)]
        three, pair = add_rounded(three, got), add_rounded(pair, got_inner)
        got_inner, got_pair = yield [(three, INNER), (pair, PAIR)]
        return own.astype(F32) + got_inner.astype(F32) + got_pair.astype(F32)

    def gather_rows(self, rows):
        near_x, near_y = yield (
            lax.ppermute(rows, "tensor", XNEXT),
            lax.ppermute(rows, "tensor", YNEXT),
        )
        diag_first, diag_second = yield (
            lax.ppermute(near_x[0], "tensor", YNEXT),
            lax.ppermute(near_y[1], "tensor", XNEXT),
        )
        return jnp.concatenate([rows, near_x, near_y, jnp.stack([diag_first, diag_second])], axis=1)

    def scatter_rows(self, partial):
        first, second = (jnp.split(partial[i], 4, axis=0) for i in range(2))
        near_first, near_second = yield (
            lax.ppermute(jnp.stack([first[1], first[3]]), "tensor", XNEXT),
            lax.ppermute(jnp.stack([second[2], second[3]]), "tensor", YNEXT),
        )
        far_first, far_second = yield (
            lax.ppermute(add_rounded(first[2], near_first[1]), "tensor", YNEXT),
            lax.ppermute(add_rounded(second[1], near_second[1]), "tensor", XNEXT),
        )
        return jnp.stack(
            [
                first[0].astype(F32) + near_first[0].astype(F32) + far_first.astype(F32),
                second[0].astype(F32) + near_second[0].astype(F32) + far_second.astype(F32),
            ]
        )


def unit_of(rows):
    recip = lax.rsqrt(jnp.mean(rows * rows, axis=-1, keepdims=True) + EPS)
    return rows * recip, recip


def norm_back(upstream, unit, recip, gain):
    scaled = upstream * gain
    return recip * (scaled - unit * jnp.mean(scaled * unit, axis=-1, keepdims=True))


def rotary(offsets):
    freqs = jnp.exp(
        jnp.arange(0, HEAD_SIZE, 2).astype(F32) * (-math.log(THETA) / HEAD_SIZE)
    )
    angles = offsets.astype(F32)[..., None] * freqs
    cosine, sine = jnp.cos(angles), jnp.sin(angles)
    return jnp.concatenate([cosine, cosine], -1), jnp.concatenate([-sine, sine], -1)


def on_device(
    net,
    hidden_in,
    cotangent,
    segment_ids,
    positions,
    pad_mask,
    attn_gain,
    w_query,
    key_weight,
    value_weight,
    query_norm_gain,
    key_gain,
    w_out,
    ffn_gain,
    w_gate,
    w_up,
    w_down,
):
    net = net()
    micro, own_rows, width = hidden_in.shape
    seq_len = segment_ids.shape[1]
    rows = micro * seq_len
    share = attn_gain.shape[0]
    head_share = query_norm_gain.shape[0]
    q_cols, kv_cols = w_query.shape[1], key_weight.shape[1]
    heads_q, heads_kv = q_cols // HEAD_SIZE, kv_cols // HEAD_SIZE
    units = w_gate.shape[1] // CHUNKS

    rounds = net.rounds
    x_own = net.to_local(hidden_in)
    packed = jnp.concatenate([attn_gain, ffn_gain, query_norm_gain, key_gain], axis=0)
    pad = -packed.shape[0] % 2048
    packed = jnp.pad(packed, (0, pad)).reshape(-1, 128)
    x_all, w_qkv, w_out_t, gains = net.first_gathers(
        x_own, jnp.concatenate([w_query, key_weight, value_weight], axis=1), w_out.T, packed
    )
    w_qkv = w_qkv.reshape(width, -1)
    w_out_t = w_out_t.reshape(width, -1)
    gains = gains.reshape(gains.shape[0], -1).astype(F32)
    x_bf = x_all.reshape(rows, width)
    later = (segment_ids, positions, pad_mask, cotangent, w_gate, w_up, w_down)
    x_bf, *later = lax.optimization_barrier((x_bf, *later))
    segment_ids, positions, pad_mask, cotangent, *ffn_weights = later
    w_gate, w_up, w_down = ffn_weights
    ffn_bufs = []
    for chunk in range(CHUNKS):
        cut = slice(chunk * units, (chunk + 1) * units)
        ffn_bufs.append(jnp.concatenate([w_gate[:, cut], w_up[:, cut], w_down[cut, :].T], axis=1))
    job_first = rounds.add(net.gather_weights(ffn_bufs[0]), 4)
    (x_bf,) = rounds.pump(x_bf)
    g_own, x_bf = lax.optimization_barrier((net.to_local(cotangent), x_bf))
    g_steps = Steps(net.gather_rows(g_own))
    gain_one = net.gains_local(gains[:, :share])
    gain_two = net.gains_local(gains[:, share : 2 * share])
    gain_q = net.gains_plain(gains[:, 2 * share : 2 * share + head_share])
    gain_k = net.gains_plain(gains[:, 2 * share + head_share : 2 * (share + head_share)])

    segment = net.row_order(segment_ids)
    offsets = net.row_order(positions)
    valid = net.row_order(pad_mask)
    row_ids = net.row_order(jnp.arange(seq_len, dtype=jnp.int32))
    cosine, sine = rotary(offsets.reshape(rows))
    ids = jnp.stack([segment, jnp.broadcast_to(row_ids, segment.shape), valid], axis=1)
    ids_col = jnp.stack([ids[:, i].reshape(rows) for i in range(3)], axis=1)
    tables = (cosine, sine, ids_col, ids, gain_q.reshape(1, -1), gain_k.reshape(1, -1))
    unit_all, _ = unit_of(x_bf.astype(F32))
    a1 = (unit_all * gain_one).astype(BF16)
    (qkv,) = net.mix(g_steps, dot_nn(a1, w_qkv))
    mixed = []
    for sequence in range(micro):
        mixed.append(
            attention_call(
                attention_forward,
                1,
                heads_q,
                heads_kv,
                (qkv,),
                tables,
                jax.ShapeDtypeStruct((seq_len, q_cols), BF16),
                pl.BlockSpec((seq_len, q_cols), lambda i: (i, 0)),
                2,
                sequence,
            )
        )
        if sequence == 0:
            mixed[0], qkv = net.mix(g_steps, mixed[0], qkv)
    mixed_bf = jnp.concatenate(mixed, axis=0)
    attn_part = dot_nt(mixed_bf, w_out_t).astype(BF16).reshape(micro, seq_len, width)
    resid, a2, w_second = net.middle_forward(attn_part, x_own, gain_two, ffn_bufs[1])
    (a2,) = rounds.pump(a2.reshape(rows, width))
    w_chunks = [jnp.concatenate(job_first.value, axis=0), w_second.reshape(width, -1)]
    g_all = net.free(g_steps).reshape(rows, width)

    da2, inners, grad_jobs = None, [], []
    for chunk in range(CHUNKS):
        w_chunk = w_chunks[chunk]
        w_gu, w_down_t = w_chunk[:, : 2 * units], w_chunk[:, 2 * units :]
        gate_up = dot_nn(a2, w_gu)
        d_inner = dot_nn(g_all, w_down_t)
        (gate_up,) = rounds.pump(gate_up)
        gate, upper = gate_up[:, :units], gate_up[:, units:]
        sigma = jax.nn.sigmoid(gate)
        swish = gate * sigma
        inner = (swish * upper).astype(BF16)
        d_gate = (d_inner * upper * sigma * (1.0 + gate * (1.0 - sigma))).astype(BF16)
        d_upper = (d_inner * swish).astype(BF16)
        d_gu = jnp.concatenate([d_gate, d_upper], axis=1)
        inner, d_gu = rounds.pump(inner, d_gu)
        inners.append(inner)
        part_da2 = dot_nt(d_gu, w_gu)
        da2 = part_da2 if da2 is None else da2 + part_da2
        parts = [(a2, d_gu), (g_all, inner)]
        if chunk == 0:
            grad_jobs.append(rounds.add(net.scatter_grads(parts), 4))
    line = net.scatter_here(parts)
    mlp = sum(
        dot_nt(inner, w_chunk[:, 2 * units :]) for inner, w_chunk in zip(inners, w_chunks)
    )
    da2, mlp = rounds.pump(da2.astype(BF16), mlp.astype(BF16))
    d_resid, d_resid_all, acc_ffn_gain, grad_second = net.middle_backward(
        da2.reshape(micro, seq_len, width), g_own, resid, gain_two, line
    )
    (d_resid_all,) = rounds.pump(d_resid_all.reshape(rows, width))
    d_resid_all, mlp = lax.optimization_barrier((d_resid_all, mlp.astype(BF16)))
    mlp_steps = Steps(net.scatter_rows(mlp.reshape(micro, seq_len, width)))
    line_out = net.scatter_here([(d_resid_all, mixed_bf)])
    job_grad_out = rounds.add(net.scatter_line(line_out), 3)

    d_mixed = dot_nn(d_resid_all, w_out_t).astype(BF16)
    d_mixed, _ = lax.optimization_barrier((d_mixed, line_out))
    (d_mixed,) = net.mix(mlp_steps, d_mixed)
    d_qkv, head_sums = attention_call(
        attention_backward,
        micro,
        heads_q,
        heads_kv,
        (qkv, d_mixed),
        tables,
        (
            jax.ShapeDtypeStruct(qkv.shape, BF16),
            jax.ShapeDtypeStruct((micro, 2, HEAD_SIZE), F32),
        ),
        (
            pl.BlockSpec((seq_len, qkv.shape[1]), lambda i: (i, 0)),
            pl.BlockSpec((1, 2, HEAD_SIZE), lambda i: (i, 0, 0)),
        ),
        5,
    )
    acc_q_gain, acc_k_gain = jnp.sum(head_sums, axis=0)
    (d_qkv,) = net.mix(mlp_steps, d_qkv)
    layer_out = net.from_local((resid + net.free(mlp_steps)).astype(BF16))
    line_qkv = net.scatter_here([(a1, d_qkv)])
    job_grad_qkv = rounds.add(net.scatter_line(line_qkv), 3)
    da1, _ = lax.optimization_barrier((dot_nt(d_qkv, w_qkv), line_qkv))
    (da1,) = rounds.pump(da1)
    acc_attn_gain = jnp.sum(da1 * unit_all, axis=0)
    d_normed = net.run(net.scatter_rows(da1.astype(BF16).reshape(micro, seq_len, width)))
    unit_one, recip_one = unit_of(x_own.astype(F32))
    input_grad = net.from_local(
        (d_resid + norm_back(d_normed, unit_one, recip_one, gain_one)).astype(BF16)
    )

    sums = net.sum_all(
        jnp.concatenate(
            [
                net.plain_vector(acc_attn_gain),
                net.plain_vector(acc_ffn_gain),
                acc_q_gain,
                acc_k_gain,
            ]
        )
    )
    rounds.drain()
    grad_qkv = job_grad_qkv.value
    grads_ffn = [*(job.value for job in grad_jobs), grad_second]

    def own_part(start, size):
        return lax.dynamic_slice_in_dim(sums, start + net.me * size, size, 0)

    return (
        layer_out,
        input_grad,
        own_part(0, share),
        grad_qkv[:, :q_cols],
        grad_qkv[:, q_cols : q_cols + kv_cols],
        grad_qkv[:, q_cols + kv_cols :],
        own_part(2 * width, head_share),
        own_part(2 * width + HEAD_SIZE, head_share),
        job_grad_out.value.T,
        own_part(width, share),
        jnp.concatenate([g[:, :units] for g in grads_ffn], axis=1),
        jnp.concatenate([g[:, units : 2 * units] for g in grads_ffn], axis=1),
        jnp.concatenate([g[:, 2 * units :] for g in grads_ffn], axis=1).T,
    )


def solution(mesh):
    dp, tensor = mesh.shape["dp"], mesh.shape["tensor"]
    kind = Links if (dp, tensor) == (8, 4) else Direct
    weight, weight_t = P("dp", "tensor"), P("tensor", "dp")
    acts, ids = P(None, ("dp", "tensor"), None), P(None, "dp")
    gain = P("dp")

    def step(*args):
        return on_device(lambda: kind(dp, tensor), *args)

    return jax.shard_map(
        step,
        mesh=mesh,
        in_specs=(
            acts,
            acts,
            ids,
            ids,
            ids,
            gain,
            weight,
            weight,
            weight,
            gain,
            gain,
            weight_t,
            gain,
            weight,
            weight,
            weight_t,
        ),
        out_specs=(
            acts,
            acts,
            gain,
            weight,
            weight,
            weight,
            gain,
            gain,
            weight_t,
            gain,
            weight,
            weight,
            weight_t,
        ),
        check_vma=False,
    )
```

```python
import functools
import math

import jax
import jax.numpy as jnp
from jax import lax
from jax.experimental import pallas as pl
from jax.experimental.pallas import tpu as pltpu
from jax.sharding import PartitionSpec as P

HEAD_SIZE = 128
EPS = 1e-06
THETA = 1000000.0
CHUNKS = 2
F32 = jnp.float32
BF16 = jnp.bfloat16

ORDER = (0, 2, 4, 6, 1, 3, 5, 7)
PAIR = [(d, d ^ 2) for d in range(8)]
ACROSS = [(d, d ^ 4) for d in range(8)]
CORE = [(d, d ^ 1) for d in range(8)]
INNER = [(2, 4), (3, 5), (4, 2), (5, 3)]
OUTWARD = [(2, 0), (3, 1), (4, 6), (5, 7)]
INWARD = [(0, 2), (1, 3), (6, 4), (7, 5)]
XNEXT = [(t, t ^ 1) for t in range(4)]
YNEXT = [(t, t ^ 2) for t in range(4)]


def add_rounded(left, right):
    return (left.astype(F32) + right.astype(F32)).astype(BF16)


def dot_nn(left, right):
    return jnp.dot(left, right, preferred_element_type=F32)


def dot_nt(left, right):
    return lax.dot_general(left, right, (((1,), (1,)), ((), ())), preferred_element_type=F32)


def dot_tn(left, right):
    return lax.dot_general(left, right, (((0,), (0,)), ((), ())), preferred_element_type=F32)


def block_move(table, rows):
    micro, count, width = rows.shape
    blocks = table.shape[0]
    size = width // blocks

    def body(table_ref, in_ref, out_ref):
        for i in range(blocks):
            start = pl.multiple_of(table_ref[i] * size, size)
            out_ref[:, :, i * size : (i + 1) * size] = in_ref[:, :, pl.ds(start, size)]

    return pl.pallas_call(
        body,
        out_shape=jax.ShapeDtypeStruct(rows.shape, rows.dtype),
        grid_spec=pltpu.PrefetchScalarGridSpec(
            num_scalar_prefetch=1,
            grid=(micro,),
            in_specs=[pl.BlockSpec((1, count, width), lambda i, ref: (i, 0, 0))],
            out_specs=pl.BlockSpec((1, count, width), lambda i, ref: (i, 0, 0)),
        ),
        cost_estimate=pl.CostEstimate(
            flops=0, bytes_accessed=4 * micro * count * width, transcendentals=0
        ),
    )(table, rows)


def turn(rows, cosine, sine):
    return rows * cosine + pltpu.roll(rows, HEAD_SIZE // 2, 1) * sine


def allowed_bias(col_ref, row_ref):
    segment, row_id, valid = row_ref[0, 0:1, :], row_ref[0, 1:2, :], row_ref[0, 2:3, :]
    segment_col, row_id_col = col_ref[:, 0:1], col_ref[:, 1:2]
    allowed = (
        (segment_col == segment)
        & (row_id <= row_id_col)
        & ((valid > 0) | (row_id == row_id_col))
    )
    return jnp.where(allowed, 0.0, -1e30)


def head(index):
    return slice(index * HEAD_SIZE, (index + 1) * HEAD_SIZE)


def softmax_rows(query, key, bias):
    scores = dot_nt(query, key) * (1.0 / math.sqrt(HEAD_SIZE)) + bias
    shifted = jnp.exp(scores - jnp.max(scores, axis=-1, keepdims=True))
    return shifted * (1.0 / jnp.sum(shifted, axis=-1, keepdims=True))


def attention_forward(
    heads_q, heads_kv, qkv_ref, cos_ref, sin_ref, col_ref, row_ref, gain_q_ref, gain_k_ref, out_ref
):
    cosine, sine = cos_ref[...], sin_ref[...]
    bias = allowed_bias(col_ref, row_ref)
    valid = col_ref[:, 2:3].astype(F32)
    groups = heads_q // heads_kv
    for kv in range(heads_kv):
        k_unit, _ = unit_of(qkv_ref[:, head(heads_q + kv)])
        key = turn(k_unit * gain_k_ref[...], cosine, sine).astype(BF16)
        value = qkv_ref[:, head(heads_q + heads_kv + kv)].astype(BF16)
        for h in range(kv * groups, (kv + 1) * groups):
            q_unit, _ = unit_of(qkv_ref[:, head(h)])
            query = turn(q_unit * gain_q_ref[...], cosine, sine).astype(BF16)
            probs = softmax_rows(query, key, bias).astype(BF16)
            out_ref[:, head(h)] = (dot_nn(probs, value) * valid).astype(BF16)


def attention_backward(
    heads_q,
    heads_kv,
    qkv_ref,
    grad_ref,
    cos_ref,
    sin_ref,
    col_ref,
    row_ref,
    gain_q_ref,
    gain_k_ref,
    out_ref,
    sums_ref,
):
    cosine, sine = cos_ref[...], sin_ref[...]
    bias = allowed_bias(col_ref, row_ref)
    valid = col_ref[:, 2:3].astype(BF16)
    groups = heads_q // heads_kv
    scale = 1.0 / math.sqrt(HEAD_SIZE)
    gain_q, gain_k = gain_q_ref[...], gain_k_ref[...]
    sum_q = sum_k = jnp.zeros((1, HEAD_SIZE), F32)
    for kv in range(heads_kv):
        k_unit, k_recip = unit_of(qkv_ref[:, head(heads_q + kv)])
        key = turn(k_unit * gain_k, cosine, sine).astype(BF16)
        value = qkv_ref[:, head(heads_q + heads_kv + kv)].astype(BF16)
        d_key = d_value = None
        for h in range(kv * groups, (kv + 1) * groups):
            q_unit, q_recip = unit_of(qkv_ref[:, head(h)])
            query = turn(q_unit * gain_q, cosine, sine).astype(BF16)
            probs = softmax_rows(query, key, bias)
            d_mixed = grad_ref[:, head(h)] * valid
            d_probs = dot_nt(d_mixed, value)
            delta = jnp.sum(probs * d_probs, axis=-1, keepdims=True)
            d_scores = (probs * (d_probs - delta)).astype(BF16)
            d_query = turn(scale * dot_nn(d_scores, key), cosine, -sine)
            sum_q = sum_q + jnp.sum(d_query * q_unit, axis=0, keepdims=True)
            out_ref[:, head(h)] = norm_back(d_query, q_unit, q_recip, gain_q).astype(BF16)
            part_key, part_value = dot_tn(d_scores, query), dot_tn(probs.astype(BF16), d_mixed)
            d_key = part_key if d_key is None else d_key + part_key
            d_value = part_value if d_value is None else d_value + part_value
        d_key = turn(scale * d_key, cosine, -sine)
        sum_k = sum_k + jnp.sum(d_key * k_unit, axis=0, keepdims=True)
        out_ref[:, head(heads_q + kv)] = norm_back(d_key, k_unit, k_recip, gain_k).astype(BF16)
        out_ref[:, head(heads_q + heads_kv + kv)] = d_value.astype(BF16)
    sums_ref[0, 0:1, :] = sum_q
    sums_ref[0, 1:2, :] = sum_k


def attention_call(body, micro, heads_q, heads_kv, wide, tables, out_shape, out_specs, passes):
    seq_len = wide[0].shape[0] // micro

    def rows_of(array):
        return pl.BlockSpec((seq_len, array.shape[1]), lambda i: (i, 0))

    def whole(array):
        return pl.BlockSpec(array.shape, lambda i: (0, 0))

    cosine, sine, col, row, gain_q, gain_k = tables
    return pl.pallas_call(
        functools.partial(body, heads_q, heads_kv),
        out_shape=out_shape,
        grid=(micro,),
        in_specs=[rows_of(array) for array in (*wide, cosine, sine, col)]
        + [
            pl.BlockSpec((1,) + row.shape[1:], lambda i: (i, 0, 0)),
            whole(gain_q),
            whole(gain_k),
        ],
        out_specs=out_specs,
        cost_estimate=pl.CostEstimate(
            flops=2 * passes * micro * heads_q * seq_len * seq_len * HEAD_SIZE,
            bytes_accessed=sum(array.size * array.dtype.itemsize for array in wide) * 2,
            transcendentals=micro * heads_q * seq_len * seq_len,
        ),
    )(*wide, *tables)


class ZLane:
    def __init__(self, me, own, out, send_sems, recv_sems):
        self.me, self.own, self.out = me, own, out
        self.send_sems, self.recv_sems = send_sems, recv_sems

    def copy(self, index, source, slot, device):
        return pltpu.make_async_remote_copy(
            src_ref=source,
            dst_ref=self.out.at[slot],
            send_sem=self.send_sems.at[index],
            recv_sem=self.recv_sems.at[slot],
            device_id={"dp": device},
            device_id_type=pl.DeviceIdType.MESH,
        )

    def parts(self, slot):
        return self.own if slot == 0 else self.out.at[slot]

    def along(self, slot):
        index, to_slot, bits = {0: (1, 3, 6), 1: (2, 2, 6), 3: (3, 2, 2), 2: (4, 3, 2)}[slot]
        return self.copy(index, self.parts(slot), to_slot, self.me ^ bits)

    def across(self, slot):
        return self.copy(5 + slot, self.parts(slot), 4 + slot, self.me ^ 1)

    def pair(self):
        return self.copy(0, self.own, 1, self.me ^ 2)

    def arrived(self, slot):
        self.copy(0, self.own, slot, self.me ^ 2).wait_recv()

    def begin(self, inner):
        self.pair().start()

        @pl.when(inner)
        def _():
            self.along(0).start()

        self.across(0).start()

    def middle(self, inner):
        self.arrived(1)

        @pl.when(inner)
        def _():
            self.along(1).start()
            self.arrived(3)
            self.along(3).start()
            self.across(3).start()

        self.across(1).start()

    def last(self, inner):
        self.arrived(2)

        @pl.when(inner)
        def _():
            self.along(2).start()

        self.across(2).start()

        @pl.when(jnp.logical_not(inner))
        def _():
            self.arrived(3)
            self.across(3).start()

    def end(self, inner):
        self.pair().wait_send()
        for slot in range(4):
            self.across(slot).wait_send()
            self.arrived(4 + slot)

        @pl.when(inner)
        def _():
            for slot in range(4):
                self.along(slot).wait_send()


def first_gathers(
    x_ref, qkv_ref, out_ref, gain_ref, x_all, qkv_all, out_all, gain_all, local_sems, *sems
):
    me, own = lax.axis_index("dp"), lax.axis_index("tensor")
    z = me // 2
    inner = (z == 1) | (z == 2)
    barrier = pltpu.get_barrier_semaphore()
    peers = [{"dp": me ^ bits} for bits in (1, 2, 6)]
    peers += [{"tensor": own ^ bit} for bit in (1, 2)]
    for device in peers:
        pl.semaphore_signal(barrier, device_id=device, device_id_type=pl.DeviceIdType.MESH)
    pl.semaphore_wait(barrier, len(peers))

    x_send, x_recv, qkv_send, qkv_recv, out_send, out_recv, gain_send, gain_recv = sems
    local = [
        pltpu.make_async_copy(source, target, local_sems.at[i])
        for i, (source, target) in enumerate(
            (
                (x_ref.at[0], x_all.at[0, 0]),
                (x_ref.at[1], x_all.at[1, 0]),
                (qkv_ref, qkv_all.at[0]),
                (out_ref, out_all.at[0]),
                (gain_ref, gain_all.at[0]),
            )
        )
    ]

    def plane(index, source, part, slot, bit):
        return pltpu.make_async_remote_copy(
            src_ref=source,
            dst_ref=x_all.at[part, slot],
            send_sem=x_send.at[index],
            recv_sem=x_recv.at[index],
            device_id={"tensor": own ^ bit},
            device_id_type=pl.DeviceIdType.MESH,
        )

    qkv_lane = ZLane(me, qkv_ref, qkv_all, qkv_send, qkv_recv)
    out_lane = ZLane(me, out_ref, out_all, out_send, out_recv)
    gain_lane = ZLane(me, gain_ref, gain_all, gain_send, gain_recv)
    x_first = plane(0, x_ref.at[0], 0, 1, 1)
    y_second = plane(1, x_ref.at[1], 1, 2, 2)
    x_second = plane(2, x_ref.at[1], 1, 1, 1)
    y_first = plane(3, x_ref.at[0], 0, 2, 2)
    d_first = plane(4, x_all.at[0, 1], 0, 3, 2)
    d_second = plane(5, x_all.at[1, 2], 1, 3, 1)
    gain_lane.begin(inner)
    qkv_lane.begin(inner)
    for copy in (x_first, y_second, x_second, y_first):
        copy.start()
    for copy in local:
        copy.start()
    gain_lane.middle(inner)
    gain_lane.last(inner)
    x_first.wait_recv()
    d_first.start()
    y_second.wait_recv()
    d_second.start()
    qkv_lane.middle(inner)
    out_lane.begin(inner)
    qkv_lane.last(inner)
    out_lane.middle(inner)
    out_lane.last(inner)
    for copy in (x_second, y_first, d_first, d_second):
        copy.wait_recv()
    for copy in (x_first, y_second, x_second, y_first, d_first, d_second):
        copy.wait_send()
    for copy in local:
        copy.wait()
    gain_lane.end(inner)
    qkv_lane.end(inner)
    out_lane.end(inner)


class Copies:
    def __init__(self, send_sems, recv_sems):
        self.send_sems, self.recv_sems, self.count = send_sems, recv_sems, 0

    def make(self, source, target, device):
        index = self.count
        self.count += 1
        return pltpu.make_async_remote_copy(
            src_ref=source,
            dst_ref=target,
            send_sem=self.send_sems.at[index],
            recv_sem=self.recv_sems.at[index],
            device_id=device,
            device_id_type=pl.DeviceIdType.MESH,
        )


def greet(peers):
    barrier = pltpu.get_barrier_semaphore()
    for device in peers:
        pl.semaphore_signal(barrier, device_id=device, device_id_type=pl.DeviceIdType.MESH)
    pl.semaphore_wait(barrier, len(peers))


class PlaneSum:
    def __init__(self, copies, own, part_ref, near, far_send, far):
        x, y = {"tensor": own ^ 1}, {"tensor": own ^ 2}
        self.part, self.near, self.far_send, self.far_got = part_ref, near, far_send, far
        self.diag, self.direct, self.far = [], [], []
        for i, (device, other, block) in enumerate(((x, y, 1), (y, x, 2))):
            self.diag.append(copies.make(self.rows(i, 3), near.at[i, 1], device))
            self.direct.append(copies.make(self.rows(i, block), near.at[i, 0], device))
            self.far.append(copies.make(far_send.at[i], far.at[i], other))

    def rows(self, i, block):
        count = self.far_got.shape[1]
        return self.part.at[i, block * count : (block + 1) * count]

    def begin(self):
        for copy in (*self.diag, *self.direct):
            copy.start()

    def middle(self):
        for i in range(2):
            self.diag[i].wait_recv()
            self.far_send[i] = add_rounded(self.rows(i, 2 - i)[...], self.near[i, 1])
            self.far[i].start()

    def arrive(self, i):
        self.direct[i].wait_recv()
        self.far[i].wait_recv()
        return (
            self.rows(i, 0)[...].astype(F32)
            + self.near[i, 0].astype(F32)
            + self.far_got[i].astype(F32)
        )

    def end(self):
        for copy in (*self.diag, *self.direct, *self.far):
            copy.wait_send()


class LineSum:
    def __init__(self, copies, me, inner, in_ref, sent, got):
        self.inner, self.part, self.sent, self.got = inner, in_ref, sent, got
        pair, over = {"dp": me ^ 2}, {"dp": me ^ 6}
        self.inward = [
            copies.make(self.block(3), got.at[0], pair),
            copies.make(self.block(2), got.at[1], pair),
        ]
        self.over = [
            copies.make(sent.at[0], got.at[2], over),
            copies.make(sent.at[1], got.at[3], over),
        ]
        self.pair = copies.make(sent.at[2], got.at[4], pair)

    def block(self, index):
        count = self.got.shape[1]
        return self.part.at[index * count : (index + 1) * count]

    def begin(self):
        @pl.when(jnp.logical_not(self.inner))
        def _():
            for copy in self.inward:
                copy.start()
            self.sent[2] = self.block(1)[...]
            self.pair.start()

    def middle(self):
        @pl.when(self.inner)
        def _():
            self.inward[0].wait_recv()
            self.sent[0] = add_rounded(self.block(2)[...], self.got[0])
            self.over[0].start()

    def last(self):
        @pl.when(self.inner)
        def _():
            self.inward[1].wait_recv()
            self.sent[1] = add_rounded(self.block(3)[...], self.got[1])
            self.over[1].start()
            self.over[0].wait_recv()
            self.sent[2] = add_rounded(self.block(1)[...], self.got[2])
            self.pair.start()

    def end(self, out_ref):
        self.pair.wait_recv()
        out_ref[...] = self.block(0)[...].astype(F32) + self.got[4].astype(F32)

        @pl.when(self.inner)
        def _():
            self.over[1].wait_recv()
            out_ref[...] += self.got[3].astype(F32)
            for copy in self.over:
                copy.wait_send()

        @pl.when(jnp.logical_not(self.inner))
        def _():
            for copy in self.inward:
                copy.wait_send()

        self.pair.wait_send()


class PlaneShare:
    def __init__(self, copies, own, mine, out, local_sem):
        x, y = {"tensor": own ^ 1}, {"tensor": own ^ 2}
        self.local = pltpu.make_async_copy(mine, out.at[:, 0], local_sem)
        self.near = [
            copies.make(mine.at[0], out.at[0, 1], x),
            copies.make(mine.at[1], out.at[1, 2], y),
            copies.make(mine.at[1], out.at[1, 1], x),
            copies.make(mine.at[0], out.at[0, 2], y),
        ]
        self.diag = [
            copies.make(out.at[0, 1], out.at[0, 3], y),
            copies.make(out.at[1, 2], out.at[1, 3], x),
        ]

    def begin(self):
        for copy in self.near:
            copy.start()
        self.local.start()

    def middle(self):
        for i in range(2):
            self.near[i].wait_recv()
            self.diag[i].start()

    def end(self):
        for copy in (*self.near[2:], *self.diag):
            copy.wait_recv()
        for copy in (*self.near, *self.diag):
            copy.wait_send()
        self.local.wait()


def places():
    me, own = lax.axis_index("dp"), lax.axis_index("tensor")
    z = me // 2
    greet(
        (
            *({"tensor": own ^ 1}, {"tensor": own ^ 2}),
            *({"dp": me ^ 1}, {"dp": me ^ 2}, {"dp": me ^ 6}),
        )
    )
    return me, own, (z == 1) | (z == 2)


def middle_forward(
    part_ref,
    x_ref,
    gain_ref,
    buf_ref,
    resid_ref,
    rows_ref,
    bufs_ref,
    near,
    far_send,
    far,
    mine,
    local_sems,
    send_sems,
    recv_sems,
    line_send,
    line_recv,
):
    me, own, inner = places()
    copies = Copies(send_sems, recv_sems)
    line = ZLane(me, buf_ref, bufs_ref, line_send, line_recv)
    plane = PlaneSum(copies, own, part_ref, near, far_send, far)
    share = PlaneShare(copies, own, mine, rows_ref, local_sems.at[0])
    kept = pltpu.make_async_copy(buf_ref, bufs_ref.at[0], local_sems.at[1])
    plane.begin()
    line.begin(inner)
    kept.start()
    plane.middle()
    line.middle(inner)
    for i in range(2):
        resid = x_ref[i].astype(F32) + plane.arrive(i)
        resid_ref[i] = resid
        mine[i] = (unit_of(resid)[0] * gain_ref[...]).astype(BF16)
    share.begin()
    share.middle()
    line.last(inner)
    share.end()
    plane.end()
    kept.wait()
    line.end(inner)


def middle_backward(
    part_ref,
    g_ref,
    resid_ref,
    gain_ref,
    line_ref,
    out_ref,
    rows_ref,
    sum_ref,
    line_out,
    near,
    far_send,
    far,
    mine,
    line_sent,
    line_got,
    local_sems,
    send_sems,
    recv_sems,
):
    me, own, inner = places()
    copies = Copies(send_sems, recv_sems)
    line = LineSum(copies, me, inner, line_ref, line_sent, line_got)
    plane = PlaneSum(copies, own, part_ref, near, far_send, far)
    share = PlaneShare(copies, own, mine, rows_ref, local_sems.at[0])
    plane.begin()
    line.begin()
    plane.middle()
    line.middle()
    sum_ref[...] = jnp.zeros_like(sum_ref)
    for i in range(2):
        unit, recip = unit_of(resid_ref[i])
        upstream = plane.arrive(i)
        sum_ref[...] += jnp.sum(upstream * unit, axis=0, keepdims=True)
        total = g_ref[i].astype(F32) + norm_back(upstream, unit, recip, gain_ref[...])
        out_ref[i] = total
        mine[i] = total.astype(BF16)
    share.begin()
    line.last()
    share.middle()
    line.end(line_out)
    share.end()
    plane.end()


class Job:
    def __init__(self, gen, open_at):
        self.gen, self.open_at = gen, open_at
        self.rounds, self.flight, self.value, self.done = 0, (), None, False

    def step(self, results, anchor=()):
        try:
            sends = self.gen.send(results)
        except StopIteration as stop:
            self.value, self.done, self.flight = stop.value, True, ()
            return
        arrays = [array for array, _ in sends]
        if anchor:
            arrays = lax.optimization_barrier((*arrays, *anchor))[: len(arrays)]
        self.flight = tuple(
            lax.ppermute(array, "dp", perm) for array, (_, perm) in zip(arrays, sends)
        )
        self.rounds += 1

    @property
    def open(self):
        return self.done or self.rounds >= self.open_at


class Rounds:
    def __init__(self):
        self.live, self.queue = [], []

    def add(self, gen, open_at):
        job = Job(gen, open_at)
        self.queue.append(job)
        return job

    def pump(self, *values):
        flight = [array for job in self.live for array in job.flight]
        if flight:
            out = lax.optimization_barrier((*values, *flight))
            values, flight = out[: len(values)], list(out[len(values) :])
            for job in self.live:
                count = len(job.flight)
                results, flight = flight[:count], flight[count:]
                job.step(results)
            self.live = [job for job in self.live if not job.done]
        while self.queue and all(job.open for job in self.live):
            job = self.queue.pop(0)
            job.step(None, values[:1])
            if not job.done:
                self.live.append(job)
        return values

    def drain(self):
        while self.live or self.queue:
            self.pump()


class Steps:
    def __init__(self, gen):
        self.gen, self.pending, self.value = gen, (), None
        self.feed(None)

    def feed(self, results):
        try:
            self.pending = self.gen.send(results)
        except StopIteration as stop:
            self.value, self.pending = stop.value, ()


class Direct:
    def __init__(self, dp, tensor):
        self.dp, self.tensor = dp, tensor
        self.me = lax.axis_index("dp")
        self.own = lax.axis_index("tensor")
        self.rounds = Rounds()

    def mix(self, steps, *values):
        out = self.rounds.pump(*values, *steps.pending)
        if steps.pending:
            steps.feed(out[len(values) :])
        return out[: len(values)]

    def run(self, gen):
        steps = Steps(gen)
        while steps.pending:
            self.mix(steps)
        return steps.value

    def free(self, gen):
        steps = gen if isinstance(gen, Steps) else Steps(gen)
        while steps.pending:
            steps.feed(lax.optimization_barrier(steps.pending))
        return steps.value

    def to_local(self, rows):
        return rows

    def from_local(self, rows):
        return rows

    def row_order(self, value):
        return value

    def gains_local(self, blocks):
        return blocks.reshape(-1)

    def gains_plain(self, blocks):
        return blocks.reshape(-1)

    def plain_vector(self, vector):
        return vector

    def sum_all(self, vector):
        return lax.psum(vector, ("dp", "tensor"))

    def gather_weights(self, buf):
        return list(lax.all_gather(buf, "dp", axis=0))
        yield

    def first_gathers(self, rows, *weights):
        gathered = self.free(self.gather_rows(rows))
        return gathered, *(lax.all_gather(array, "dp", axis=0) for array in weights)

    def middle_forward(self, part, x_own, gain, buf):
        resid = x_own.astype(F32) + self.free(self.scatter_rows(part))
        rows = self.free(self.gather_rows((unit_of(resid)[0] * gain).astype(BF16)))
        return resid, rows, lax.all_gather(buf, "dp", axis=0)

    def middle_backward(self, part, g_own, resid, gain, line):
        unit, recip = unit_of(resid)
        upstream = self.free(self.scatter_rows(part))
        total = g_own.astype(F32) + norm_back(upstream, unit, recip, gain)
        rows = self.free(self.gather_rows(total.astype(BF16)))
        return total, rows, jnp.sum(upstream * unit, axis=(0, 1)), line

    def scatter_here(self, parts):
        job = Job(self.scatter_grads(parts), 0)
        job.step(None)
        return job.value

    def scatter_grads(self, parts):
        full = jnp.concatenate([dot_tn(l, r).astype(BF16) for l, r in parts], axis=1)
        return lax.psum_scatter(full, "dp", scatter_dimension=0, tiled=True).astype(F32)
        yield

    def gather_rows(self, rows):
        return lax.all_gather(rows, "tensor", axis=1, tiled=True)
        yield

    def scatter_rows(self, partial):
        return lax.psum_scatter(partial, "tensor", scatter_dimension=1, tiled=True).astype(F32)
        yield


class Links(Direct):
    def __init__(self, dp, tensor):
        super().__init__(dp, tensor)
        z = self.me // 2
        self.inner = (z == 1) | (z == 2)
        self.blocks = self.me ^ jnp.array(ORDER, jnp.int32)
        hit = (self.me ^ jnp.arange(8, dtype=jnp.int32))[:, None] == jnp.array(ORDER, jnp.int32)
        self.hit = hit
        self.places = jnp.sum(jnp.where(hit, jnp.arange(8, dtype=jnp.int32)[None, :], 0), axis=1)

    def to_local(self, rows):
        return block_move(self.blocks, rows)

    def from_local(self, rows):
        return block_move(self.places, rows)

    def row_order(self, value):
        parts = list(jnp.split(value, 4, axis=-1))
        for bit in (1, 2):
            swap = (self.own & bit) != 0
            parts = [jnp.where(swap, parts[j ^ bit], parts[j]) for j in range(4)]
        return jnp.concatenate(parts, axis=-1)

    def gains_plain(self, blocks):
        return jnp.sum(jnp.where(self.hit[:, :, None], blocks[None], 0), axis=1).reshape(-1)

    def plain_vector(self, vector):
        return self.gains_plain(vector.reshape(8, -1))

    def sum_all(self, vector):
        for axis, perm in (
            ("tensor", XNEXT),
            ("tensor", YNEXT),
            ("dp", CORE),
            ("dp", PAIR),
            ("dp", ACROSS),
        ):
            vector = vector + lax.ppermute(vector, axis, perm)
        return vector

    def gather_weights(self, buf):
        pair, over_own, other = yield [(buf, PAIR), (buf, INNER), (buf, CORE)]
        over_pair, out_own, other_pair = yield [(pair, INNER), (over_own, OUTWARD), (pair, CORE)]
        two = jnp.where(self.inner, over_pair, out_own)
        out_pair, other_two = yield [(over_pair, OUTWARD), (two, CORE)]
        three = jnp.where(self.inner, over_own, out_pair)
        other_three = lax.ppermute(three, "dp", CORE)
        return [buf, pair, two, three, other, other_pair, other_two, other_three]

    def first_gathers(self, rows, *weights):
        micro, count, width = rows.shape
        hbm = pl.BlockSpec(memory_space=pl.ANY)
        lanes = len(weights)
        return pl.pallas_call(
            first_gathers,
            out_shape=(
                jax.ShapeDtypeStruct((micro, 4, count, width), rows.dtype),
                *(jax.ShapeDtypeStruct((8,) + w.shape, w.dtype) for w in weights),
            ),
            in_specs=[hbm] * (1 + lanes),
            out_specs=[hbm] * (1 + lanes),
            scratch_shapes=[
                pltpu.SemaphoreType.DMA((copies,)) for copies in (5, 6, 6, *(9, 8) * lanes)
            ],
            compiler_params=pltpu.CompilerParams(collective_id=0, has_side_effects=True),
        )(rows, *weights)

    def middle_call(self, body, operands, outputs, places, line, line_sems, scratch, identity):
        micro, count, width = self.rows
        vmem, hbm = pl.BlockSpec(memory_space=pltpu.VMEM), pl.BlockSpec(memory_space=pl.ANY)
        return pl.pallas_call(
            body,
            out_shape=outputs,
            in_specs=[vmem] * (len(operands) - 1) + [line],
            out_specs=[hbm if place else vmem for place in places],
            scratch_shapes=[
                pltpu.VMEM((micro, 2, count, width), BF16),
                *[pltpu.VMEM(self.rows, BF16)] * 3,
                *scratch,
                *[pltpu.SemaphoreType.DMA((copies,)) for copies in line_sems],
            ],
            compiler_params=pltpu.CompilerParams(collective_id=identity, has_side_effects=True),
        )(*operands)

    def middle_forward(self, part, x_own, gain, buf):
        self.rows = micro, count, width = x_own.shape
        return self.middle_call(
            middle_forward,
            (part, x_own, gain.reshape(1, -1), buf),
            (
                jax.ShapeDtypeStruct(self.rows, F32),
                jax.ShapeDtypeStruct((micro, 4, count, width), BF16),
                jax.ShapeDtypeStruct((8,) + buf.shape, BF16),
            ),
            (False, True, True),
            pl.BlockSpec(memory_space=pl.ANY),
            (2, 12, 12, 9, 8),
            (),
            2,
        )

    def middle_backward(self, part, g_own, resid, gain, line):
        self.rows = micro, count, width = g_own.shape
        block = (line.shape[0] // 4, line.shape[1])
        total, rows, sums, grads = self.middle_call(
            middle_backward,
            (part, g_own, resid, gain.reshape(1, -1), line),
            (
                jax.ShapeDtypeStruct(self.rows, F32),
                jax.ShapeDtypeStruct((micro, 4, count, width), BF16),
                jax.ShapeDtypeStruct((1, width), F32),
                jax.ShapeDtypeStruct(block, F32),
            ),
            (False, True, False, False),
            pl.BlockSpec(memory_space=pltpu.VMEM),
            (1, 17, 17),
            (pltpu.VMEM((3,) + block, BF16), pltpu.VMEM((5,) + block, BF16)),
            3,
        )
        return total, rows, sums.reshape(-1), grads

    def scatter_here(self, parts):
        summed, half = [], parts[0][0].shape[1] // 2
        for left, right in parts:
            away = lax.ppermute(dot_tn(left[:, half:], right).astype(BF16), "dp", CORE)
            summed.append((dot_tn(left[:, :half], right) + away.astype(F32)).astype(BF16))
        return jnp.concatenate(summed, axis=1)

    def scatter_grads(self, parts):
        away, half = [], parts[0][0].shape[1] // 2
        for left, right in parts:
            away.append(dot_tn(left[:, half:], right).astype(BF16))
        summed = [
            (dot_tn(left[:, :half], right) + lax.ppermute(array, "dp", CORE).astype(F32)).astype(BF16)
            for (left, right), array in zip(parts, away)
        ]
        own, pair, two, three = jnp.split(jnp.concatenate(summed, axis=1), 4, axis=0)
        (got,) = yield [(three, INWARD)]
        two_sum = add_rounded(two, got)
        got, got_inner = yield [(two, INWARD), (two_sum, INNER)]
        three, pair = add_rounded(three, got), add_rounded(pair, got_inner)
        got_inner, got_pair = yield [(three, INNER), (pair, PAIR)]
        return own.astype(F32) + got_inner.astype(F32) + got_pair.astype(F32)

    def gather_rows(self, rows):
        near_x, near_y = yield (
            lax.ppermute(rows, "tensor", XNEXT),
            lax.ppermute(rows, "tensor", YNEXT),
        )
        diag_first, diag_second = yield (
            lax.ppermute(near_x[0], "tensor", YNEXT),
            lax.ppermute(near_y[1], "tensor", XNEXT),
        )
        return jnp.concatenate([rows, near_x, near_y, jnp.stack([diag_first, diag_second])], axis=1)

    def scatter_rows(self, partial):
        first, second = (jnp.split(partial[i], 4, axis=0) for i in range(2))
        near_first, near_second = yield (
            lax.ppermute(jnp.stack([first[1], first[3]]), "tensor", XNEXT),
            lax.ppermute(jnp.stack([second[2], second[3]]), "tensor", YNEXT),
        )
        far_first, far_second = yield (
            lax.ppermute(add_rounded(first[2], near_first[1]), "tensor", YNEXT),
            lax.ppermute(add_rounded(second[1], near_second[1]), "tensor", XNEXT),
        )
        return jnp.stack(
            [
                first[0].astype(F32) + near_first[0].astype(F32) + far_first.astype(F32),
                second[0].astype(F32) + near_second[0].astype(F32) + far_second.astype(F32),
            ]
        )


def unit_of(rows):
    recip = lax.rsqrt(jnp.mean(rows * rows, axis=-1, keepdims=True) + EPS)
    return rows * recip, recip


def norm_back(upstream, unit, recip, gain):
    scaled = upstream * gain
    return recip * (scaled - unit * jnp.mean(scaled * unit, axis=-1, keepdims=True))


def rotary(offsets):
    freqs = jnp.exp(
        jnp.arange(0, HEAD_SIZE, 2).astype(F32) * (-math.log(THETA) / HEAD_SIZE)
    )
    angles = offsets.astype(F32)[..., None] * freqs
    cosine, sine = jnp.cos(angles), jnp.sin(angles)
    return jnp.concatenate([cosine, cosine], -1), jnp.concatenate([-sine, sine], -1)


def on_device(
    net,
    hidden_in,
    cotangent,
    segment_ids,
    positions,
    pad_mask,
    attn_gain,
    w_query,
    key_weight,
    value_weight,
    query_norm_gain,
    key_gain,
    w_out,
    ffn_gain,
    w_gate,
    w_up,
    w_down,
):
    net = net()
    micro, own_rows, width = hidden_in.shape
    seq_len = segment_ids.shape[1]
    rows = micro * seq_len
    share = attn_gain.shape[0]
    head_share = query_norm_gain.shape[0]
    q_cols, kv_cols = w_query.shape[1], key_weight.shape[1]
    heads_q, heads_kv = q_cols // HEAD_SIZE, kv_cols // HEAD_SIZE
    units = w_gate.shape[1] // CHUNKS

    rounds = net.rounds
    x_own = net.to_local(hidden_in)
    packed = jnp.concatenate([attn_gain, ffn_gain, query_norm_gain, key_gain], axis=0)
    pad = -packed.shape[0] % 2048
    packed = jnp.pad(packed, (0, pad)).reshape(-1, 128)
    x_all, w_qkv, w_out_t, gains = net.first_gathers(
        x_own, jnp.concatenate([w_query, key_weight, value_weight], axis=1), w_out.T, packed
    )
    w_qkv = w_qkv.reshape(width, -1)
    w_out_t = w_out_t.reshape(width, -1)
    gains = gains.reshape(gains.shape[0], -1).astype(F32)
    x_bf = x_all.reshape(rows, width)
    later = (segment_ids, positions, pad_mask, cotangent, w_gate, w_up, w_down)
    x_bf, *later = lax.optimization_barrier((x_bf, *later))
    segment_ids, positions, pad_mask, cotangent, *ffn_weights = later
    w_gate, w_up, w_down = ffn_weights
    ffn_bufs = []
    for chunk in range(CHUNKS):
        cut = slice(chunk * units, (chunk + 1) * units)
        ffn_bufs.append(jnp.concatenate([w_gate[:, cut], w_up[:, cut], w_down[cut, :].T], axis=1))
    job_first = rounds.add(net.gather_weights(ffn_bufs[0]), 4)
    (x_bf,) = rounds.pump(x_bf)
    g_own, x_bf = lax.optimization_barrier((net.to_local(cotangent), x_bf))
    g_steps = Steps(net.gather_rows(g_own))
    gain_one = net.gains_local(gains[:, :share])
    gain_two = net.gains_local(gains[:, share : 2 * share])
    gain_q = net.gains_plain(gains[:, 2 * share : 2 * share + head_share])
    gain_k = net.gains_plain(gains[:, 2 * share + head_share : 2 * (share + head_share)])

    segment = net.row_order(segment_ids)
    offsets = net.row_order(positions)
    valid = net.row_order(pad_mask)
    row_ids = net.row_order(jnp.arange(seq_len, dtype=jnp.int32))
    cosine, sine = rotary(offsets.reshape(rows))
    ids = jnp.stack([segment, jnp.broadcast_to(row_ids, segment.shape), valid], axis=1)
    ids_col = jnp.stack([ids[:, i].reshape(rows) for i in range(3)], axis=1)
    tables = (cosine, sine, ids_col, ids, gain_q.reshape(1, -1), gain_k.reshape(1, -1))
    unit_all, _ = unit_of(x_bf.astype(F32))
    a1 = (unit_all * gain_one).astype(BF16)
    (qkv,) = net.mix(g_steps, dot_nn(a1, w_qkv))
    mixed_bf = attention_call(
        attention_forward,
        micro,
        heads_q,
        heads_kv,
        (qkv,),
        tables,
        jax.ShapeDtypeStruct((rows, q_cols), BF16),
        pl.BlockSpec((seq_len, q_cols), lambda i: (i, 0)),
        2,
    )
    (mixed_bf,) = net.mix(g_steps, mixed_bf)
    attn_part = dot_nt(mixed_bf, w_out_t).astype(BF16).reshape(micro, seq_len, width)
    resid, a2, w_second = net.middle_forward(attn_part, x_own, gain_two, ffn_bufs[1])
    (a2,) = rounds.pump(a2.reshape(rows, width))
    w_chunks = [jnp.concatenate(job_first.value, axis=0), w_second.reshape(width, -1)]
    g_all = net.free(g_steps).reshape(rows, width)

    da2, inners = None, []
    for chunk in range(CHUNKS):
        w_chunk = w_chunks[chunk]
        w_gu, w_down_t = w_chunk[:, : 2 * units], w_chunk[:, 2 * units :]
        gate_up = dot_nn(a2, w_gu)
        d_inner = dot_nn(g_all, w_down_t)
        (gate_up,) = rounds.pump(gate_up)
        gate, upper = gate_up[:, :units], gate_up[:, units:]
        sigma = jax.nn.sigmoid(gate)
        swish = gate * sigma
        inner = (swish * upper).astype(BF16)
        d_gate = (d_inner * upper * sigma * (1.0 + gate * (1.0 - sigma))).astype(BF16)
        d_upper = (d_inner * swish).astype(BF16)
        d_gu = jnp.concatenate([d_gate, d_upper], axis=1)
        inner, d_gu = rounds.pump(inner, d_gu)
        inners.append(inner)
        part_da2 = dot_nt(d_gu, w_gu)
        da2 = part_da2 if da2 is None else da2 + part_da2
        parts = [(a2, d_gu), (g_all, inner)]
        if chunk == 0:
            job_grad = rounds.add(net.scatter_grads(parts), 4)
    line = net.scatter_here(parts)
    mlp = sum(
        dot_nt(inner, w_chunk[:, 2 * units :]) for inner, w_chunk in zip(inners, w_chunks)
    )
    da2, mlp = rounds.pump(da2.astype(BF16), mlp.astype(BF16))
    d_resid, d_resid_all, acc_ffn_gain, grad_second = net.middle_backward(
        da2.reshape(micro, seq_len, width), g_own, resid, gain_two, line
    )
    (d_resid_all,) = rounds.pump(d_resid_all.reshape(rows, width))
    d_resid_all, mlp = lax.optimization_barrier((d_resid_all, mlp.astype(BF16)))
    mlp_steps = Steps(net.scatter_rows(mlp.reshape(micro, seq_len, width)))
    job_grad_out = rounds.add(net.scatter_grads([(d_resid_all, mixed_bf)]), 3)

    (d_mixed,) = net.mix(mlp_steps, dot_nn(d_resid_all, w_out_t).astype(BF16))
    d_qkv, head_sums = attention_call(
        attention_backward,
        micro,
        heads_q,
        heads_kv,
        (qkv, d_mixed),
        tables,
        (
            jax.ShapeDtypeStruct(qkv.shape, BF16),
            jax.ShapeDtypeStruct((micro, 2, HEAD_SIZE), F32),
        ),
        (
            pl.BlockSpec((seq_len, qkv.shape[1]), lambda i: (i, 0)),
            pl.BlockSpec((1, 2, HEAD_SIZE), lambda i: (i, 0, 0)),
        ),
        5,
    )
    acc_q_gain, acc_k_gain = jnp.sum(head_sums, axis=0)
    (d_qkv,) = net.mix(mlp_steps, d_qkv)
    layer_out = net.from_local((resid + net.free(mlp_steps)).astype(BF16))
    job_grad_qkv = rounds.add(net.scatter_grads([(a1, d_qkv)]), 4)
    (da1,) = rounds.pump(dot_nt(d_qkv, w_qkv))
    acc_attn_gain = jnp.sum(da1 * unit_all, axis=0)
    d_normed = net.run(net.scatter_rows(da1.astype(BF16).reshape(micro, seq_len, width)))
    unit_one, recip_one = unit_of(x_own.astype(F32))
    input_grad = net.from_local(
        (d_resid + norm_back(d_normed, unit_one, recip_one, gain_one)).astype(BF16)
    )

    sums = net.sum_all(
        jnp.concatenate(
            [
                net.plain_vector(acc_attn_gain),
                net.plain_vector(acc_ffn_gain),
                acc_q_gain,
                acc_k_gain,
            ]
        )
    )
    rounds.drain()
    grad_qkv = job_grad_qkv.value
    grads_ffn = [job_grad.value, grad_second]

    def own_part(start, size):
        return lax.dynamic_slice_in_dim(sums, start + net.me * size, size, 0)

    return (
        layer_out,
        input_grad,
        own_part(0, share),
        grad_qkv[:, :q_cols],
        grad_qkv[:, q_cols : q_cols + kv_cols],
        grad_qkv[:, q_cols + kv_cols :],
        own_part(2 * width, head_share),
        own_part(2 * width + HEAD_SIZE, head_share),
        job_grad_out.value.T,
        own_part(width, share),
        jnp.concatenate([g[:, :units] for g in grads_ffn], axis=1),
        jnp.concatenate([g[:, units : 2 * units] for g in grads_ffn], axis=1),
        jnp.concatenate([g[:, 2 * units :] for g in grads_ffn], axis=1).T,
    )


def solution(mesh):
    dp, tensor = mesh.shape["dp"], mesh.shape["tensor"]
    kind = Links if (dp, tensor) == (8, 4) else Direct
    weight, weight_t = P("dp", "tensor"), P("tensor", "dp")
    acts, ids = P(None, ("dp", "tensor"), None), P(None, "dp")
    gain = P("dp")

    def step(*args):
        return on_device(lambda: kind(dp, tensor), *args)

    return jax.shard_map(
        step,
        mesh=mesh,
        in_specs=(
            acts,
            acts,
            ids,
            ids,
            ids,
            gain,
            weight,
            weight,
            weight,
            gain,
            gain,
            weight_t,
            gain,
            weight,
            weight,
            weight_t,
        ),
        out_specs=(
            acts,
            acts,
            gain,
            weight,
            weight,
            weight,
            gain,
            gain,
            weight_t,
            gain,
            weight,
            weight,
            weight_t,
        ),
        check_vma=False,
    )
```
